128 devices in a mesh: dp: 4 (over y_hi, core), cells: 32 (over y_lo, x, z).
Axes of the slice: x: 4, y: 4 (y_hi: 2, y_lo: 2; y = y_hi * 2 + y_lo), z: 4, core: 2. Of those that a mesh axis runs over, the one named last changes fastest.
Arguments:
- sensitivity: float32 [8192, 49152], P('dp', 'cells'), may hold values from -0.02734375 to 0.02734375
- observed: float32 [8192, 256], P('dp'), may hold values from -6 to 6
- models: float32 [49152, 256], P('cells'), may hold values from -6 to 6
- neighbour_map: int32 [4, 768], replicated, may hold values from 0 to 767, as said below
- edge_mask: int32 [49152], P('cells'), may hold values 0 or 1
Outputs:
- updated: float32 [49152, 256], P('cells')
The draws below stay inside these ranges and needn't reach their ends.
Inputs may be any that keep to these rules, and one draw needn't show every extreme that they name: `neighbour_map`: each row k maps every cell of a periodic 32 by 24 plane grid, numbered in a drawn order, to its neighbour in one of the four grid directions; every row is a permutation.
All inputs are finite; a program needn't handle non-finite values. No bound on the sum of `edge_mask` on one device may be relied on, other than what follows from the above.
Results may differ from the reference program's by a relative error of at most 0.0001.
Values sent between devices are 32-bit elements; how exact they have to be, the bound alone decides.
No kernel may reach another device: no remote copies, remote signals or barrier semaphores. Data moves between devices by JAX's collectives and lax.ppermute only.
A program may use at most 128 MiB of HBM per device.

```python
import jax
import jax.numpy as jnp
from jax import lax

NDATA = 8192
PX = 32
PY = 24
SOLS = 256
ITERS = 2
PLANE = 768
NCELL = 49152


def draw_neighbour_map(key, part):
    total = PX * PY
    labels = jax.random.permutation(jax.random.fold_in(key, 11), total).astype(jnp.int32)
    index = jnp.arange(total, dtype=jnp.int32)
    first = index // PY
    second = index % PY
    targets = [(first + 1) % PX * PY + second, (first + PX - 1) % PX * PY + second, first * PY + (second + 1) % PY, first * PY + (second + PY - 1) % PY]
    rows = []
    for target in targets:
        row = jnp.zeros((total,), jnp.int32).at[labels].set(labels[target])
        rows.append(row)
    return jnp.stack(rows, axis=0)


def set_ends(entries, stream_key, low, largest):
    longest = entries.shape.index(max(entries.shape))
    spots = []
    for shift in (0, 1):
        where = [jax.random.randint(jax.random.fold_in(stream_key, axis), (), 0, length) for axis, length in enumerate(entries.shape)]
        where[longest] = (where[longest] + shift) % entries.shape[longest]
        spots.append(tuple(where))
    return entries.at[spots[0]].set(low).at[spots[1]].set(largest)


def level_of(own_key, shape, shards, least, high):
    def one(dim, parts):
        steps = jax.random.uniform(jax.random.fold_in(jax.random.fold_in(own_key, 6), dim), (parts,), jnp.float32, least / len(shards), high / len(shards))
        return jnp.repeat(jnp.exp(steps), shape[dim] // parts).reshape((-1,) + (1,) * (len(shape) - dim - 1))

    factor_of = one(*shards[0])
    for cut in shards[1:]:
        factor_of = factor_of * one(*cut)
    return factor_of


def centred(rng, shape, spread, most, shards=(), kind=jnp.bfloat16):
    values = jax.random.normal(rng, shape, jnp.float32) * spread
    if len(shards) > 0:
        values = level_of(rng, shape, shards, -0.22, 0.18) * values
    return jnp.clip(values, min=-most, max=most).astype(kind)


def setup_inputs(seed: int = 0) -> dict:
    key_of = jax.random.split(jax.random.key(seed), 6)
    return {
        "sensitivity": centred(key_of[0], (NDATA, NCELL), NCELL ** -0.5, 0.02734375, ((0, 4), (1, 32)), jnp.float32),
        "observed": centred(key_of[1], (NDATA, SOLS), 1.0, 6.0, ((0, 4),), jnp.float32),
        "models": centred(key_of[2], (NCELL, SOLS), 1.0, 6.0, ((0, 32),), jnp.float32),
        "neighbour_map": draw_neighbour_map(jax.random.fold_in(key_of[5], 71), 0),
        "edge_mask": set_ends((jax.random.randint(key_of[4], (NCELL,), 0, 4) < 1).astype(jnp.int32), jax.random.fold_in(key_of[4], 1), 0, 1),
    }


def smooth_all(current, neighbour_map, edge_mask):
    count = current.shape[0] // PLANE
    planes = current.reshape(count, PLANE, current.shape[1])
    zero_plane = jnp.zeros((1, PLANE, current.shape[1]), jnp.float32)
    above = jnp.concatenate([zero_plane, planes[:-1]], axis=0)
    below = jnp.concatenate([planes[1:], zero_plane], axis=0)
    total = jnp.zeros_like(planes)
    for other in (above, below):
        diff = other - planes
        total = total + diff / jnp.sqrt(1.0 + diff * diff)
    for k in range(4):
        other = jnp.take(planes, neighbour_map[k], axis=1)
        diff = other - planes
        total = total + diff / jnp.sqrt(1.0 + diff * diff)
    scale = 1.0 - 0.75 * edge_mask.astype(jnp.float32).reshape(count, PLANE, 1)
    return (total * scale).reshape(current.shape)

def reference(sensitivity, observed, models, neighbour_map, edge_mask):
    current = models
    for step in range(ITERS):
        predicted = jnp.dot(sensitivity, current, precision=lax.Precision.HIGHEST, preferred_element_type=jnp.float32)
        misfit = predicted - observed
        weighted = misfit / jnp.maximum(jnp.abs(misfit), 1.0)
        gradient = lax.dot_general(sensitivity, weighted, (((0,), (0,)), ((), ())), precision=lax.Precision.HIGHEST, preferred_element_type=jnp.float32)
        current = current - 1.0 * gradient + 0.05 * smooth_all(current, neighbour_map, edge_mask)
    return current
```

```python
import jax
import jax.numpy as jnp
from jax import lax
from jax.sharding import Mesh, PartitionSpec as P

ITERS = 2
DATA = ("yh", "core")
CELLS = ("yl", "x", "z")
ALL = DATA + CELLS


def reweight(misfit):
    return misfit / jnp.maximum(jnp.abs(misfit), 1.0)


def huber(diff):
    return diff / jnp.sqrt(1.0 + diff * diff)


def reduce_pieces(partial, ranks):
    pieces = partial.reshape(ranks, partial.shape[0] // ranks, partial.shape[1])
    return jnp.sum(lax.all_to_all(pieces, CELLS, 0, 0), axis=0)


def gather_pieces(piece, ranks):
    copies = jnp.broadcast_to(piece[None], (ranks,) + piece.shape)
    return lax.all_to_all(copies, CELLS, 0, 0).reshape(-1, piece.shape[1])


def swap(value, axis):
    return lax.ppermute(value, axis, [(0, 1), (1, 0)])


def halo_pairs(ranks):
    up = [(i, i + 1) for i in range(ranks - 1)]
    down = [(ranks + i + 1, ranks + i) for i in range(ranks - 1)]
    return up + down


def local(sensitivity, observed, models, neighbour_map, edge_mask):
    core = lax.axis_index("core")
    ranks = lax.axis_size(CELLS)
    rank = lax.axis_index(CELLS)
    plane_cells = neighbour_map.shape[1]
    sols = models.shape[1]
    rows = observed.shape[0] // ranks
    own_observed = lax.dynamic_slice_in_dim(observed, rank * rows, rows, axis=0)
    own_mask = lax.dynamic_slice_in_dim(edge_mask, core * plane_cells, plane_cells, axis=0)
    scale = 0.05 * (1.0 - 0.75 * own_mask.astype(jnp.float32))[:, None]
    current = models
    for step in range(ITERS):
        own = lax.dynamic_slice_in_dim(current, core * plane_cells, plane_cells, axis=0)
        twin = lax.dynamic_slice_in_dim(current, (1 - core) * plane_cells, plane_cells, axis=0)
        partial = jnp.dot(
            sensitivity,
            current,
            precision=lax.Precision.HIGH,
            preferred_element_type=jnp.float32,
        )
        weighted = reweight(reduce_pieces(partial, ranks) - own_observed)
        weighted = gather_pieces(weighted, ranks)
        partial_grad = lax.dot_general(
            sensitivity,
            weighted,
            (((0,), (0,)), ((), ())),
            precision=lax.Precision.HIGH,
            preferred_element_type=jnp.float32,
        )
        keep = lax.dynamic_slice_in_dim(partial_grad, core * plane_cells, plane_cells, axis=0)
        send = lax.dynamic_slice_in_dim(partial_grad, (1 - core) * plane_cells, plane_cells, axis=0)
        half = keep + swap(send, "core")
        gradient = half + swap(half, "yh")
        beyond = lax.ppermute(twin, ("core",) + CELLS, halo_pairs(ranks))
        total = huber(twin - own) + huber(beyond - own)
        for k in range(4):
            total = total + huber(jnp.take(own, neighbour_map[k], axis=0) - own)
        own = own - 1.0 * gradient + scale * total
        other = swap(own, "core")
        first = jnp.where(core == 0, own, other)
        second = jnp.where(core == 0, other, own)
        current = jnp.concatenate([first, second], axis=0)
    return current


def solution(mesh):
    fine = Mesh(mesh.devices.reshape(2, 2, 2, 4, 4), ALL)
    return jax.shard_map(
        local,
        mesh=fine,
        in_specs=(P(DATA, CELLS), P(DATA, None), P(CELLS, None), P(), P(CELLS)),
        out_specs=P(CELLS, None),
        check_vma=False,
    )
```

```python
import functools

import jax
import jax.numpy as jnp
from jax import lax
from jax.experimental import pallas as pl
from jax.experimental.pallas import tpu as pltpu
from jax.sharding import Mesh, PartitionSpec as P

ITERS = 2
DATA = ("yh", "core")
CELLS = ("yl", "x", "z")
ALL = DATA + CELLS
ROWS = 512
COLS = 256
VMEM_LIMIT = 40 * 1024 * 1024


def reweight(misfit):
    return misfit / jnp.maximum(jnp.abs(misfit), 1.0)


def huber(diff):
    return diff / jnp.sqrt(1.0 + diff * diff)


def split(value):
    high = value.astype(jnp.bfloat16)
    low = (value - high.astype(jnp.float32)).astype(jnp.bfloat16)
    return high, low


def dot(a, b):
    return jnp.dot(a, b, preferred_element_type=jnp.float32)


def forward_kernel(add, plane_ref, s_ref, x_ref, *refs):
    if add:
        p_ref, o_ref, high_ref, low_ref = refs
    else:
        o_ref, high_ref, low_ref = refs

    @pl.when(pl.program_id(0) == 0)
    def _():
        high_ref[...], low_ref[...] = split(x_ref[...])

    s_high, s_low = split(s_ref[...])
    total = dot(s_high, high_ref[...]) + (dot(s_high, low_ref[...]) + dot(s_low, high_ref[...]))
    if add:
        total = total + p_ref[...]
    o_ref[...] = total


def forward(plane, sensitivity, x, before=None):
    data, sols = sensitivity.shape[0], x.shape[1]
    cells = x.shape[0]
    in_specs = [
        pl.BlockSpec((ROWS, cells), lambda i, plane: (i, plane[0])),
        pl.BlockSpec((cells, sols), lambda i, plane: (0, 0)),
    ]
    args = [sensitivity, x]
    if before is not None:
        in_specs.append(pl.BlockSpec((ROWS, sols), lambda i, plane: (i, 0)))
        args.append(before)
    return pl.pallas_call(
        functools.partial(forward_kernel, before is not None),
        grid_spec=pltpu.PrefetchScalarGridSpec(
            num_scalar_prefetch=1,
            grid=(data // ROWS,),
            in_specs=in_specs,
            out_specs=pl.BlockSpec((ROWS, sols), lambda i, plane: (i, 0)),
            scratch_shapes=[
                pltpu.VMEM((cells, sols), jnp.bfloat16),
                pltpu.VMEM((cells, sols), jnp.bfloat16),
            ],
        ),
        out_shape=jax.ShapeDtypeStruct((data, sols), jnp.float32),
        compiler_params=pltpu.CompilerParams(vmem_limit_bytes=VMEM_LIMIT),
        cost_estimate=pl.CostEstimate(
            flops=6 * data * cells * sols,
            bytes_accessed=4 * (data * cells + cells * sols + data * sols),
            transcendentals=0,
        ),
    )(plane, *args)


def backward_kernel(plane_ref, s_ref, w_ref, o_ref, high_ref, low_ref):
    @pl.when(pl.program_id(0) == 0)
    def _():
        high_ref[...], low_ref[...] = split(w_ref[...].T)

    s_high, s_low = split(s_ref[...])
    total = dot(high_ref[...], s_high) + (dot(low_ref[...], s_high) + dot(high_ref[...], s_low))
    o_ref[...] = total.T


def backward(plane, sensitivity, w, cells):
    data, sols = w.shape
    blocks = cells // COLS
    return pl.pallas_call(
        backward_kernel,
        grid_spec=pltpu.PrefetchScalarGridSpec(
            num_scalar_prefetch=1,
            grid=(blocks,),
            in_specs=[
                pl.BlockSpec((data, COLS), lambda i, plane: (0, plane[0] * blocks + i)),
                pl.BlockSpec((data, sols), lambda i, plane: (0, 0)),
            ],
            out_specs=pl.BlockSpec((COLS, sols), lambda i, plane: (i, 0)),
            scratch_shapes=[
                pltpu.VMEM((sols, data), jnp.bfloat16),
                pltpu.VMEM((sols, data), jnp.bfloat16),
            ],
        ),
        out_shape=jax.ShapeDtypeStruct((cells, sols), jnp.float32),
        compiler_params=pltpu.CompilerParams(vmem_limit_bytes=VMEM_LIMIT),
        cost_estimate=pl.CostEstimate(
            flops=6 * data * cells * sols,
            bytes_accessed=4 * (data * cells + cells * sols + data * sols),
            transcendentals=0,
        ),
    )(plane, sensitivity, w)


def swap(value, axis):
    return lax.ppermute(value, axis, [(0, 1), (1, 0)])


def halo_pairs(ranks):
    up = [(i, i + 1) for i in range(ranks - 1)]
    down = [(ranks + i + 1, ranks + i) for i in range(ranks - 1)]
    return up + down


def local(sensitivity, observed, models, neighbour_map, edge_mask):
    core = lax.axis_index("core").astype(jnp.int32)
    mine, theirs = core.reshape(1), (1 - core).reshape(1)
    ranks = lax.axis_size(CELLS)
    rank = lax.axis_index(CELLS)
    cells = neighbour_map.shape[1]
    rows = observed.shape[0] // ranks
    own_observed = lax.dynamic_slice_in_dim(observed, rank * rows, rows, axis=0)
    own_mask = lax.dynamic_slice_in_dim(edge_mask, core * cells, cells, axis=0)
    scale = 0.05 * (1.0 - 0.75 * own_mask.astype(jnp.float32))[:, None]
    own = lax.dynamic_slice_in_dim(models, core * cells, cells, axis=0)
    twin = lax.dynamic_slice_in_dim(models, (1 - core) * cells, cells, axis=0)
    for step in range(ITERS):
        partial = forward(mine, sensitivity, own)
        partial = forward(theirs, sensitivity, twin, partial)
        partial, own, twin = lax.optimization_barrier((partial, own, twin))
        pieces = lax.all_to_all(partial.reshape(ranks, rows, -1), CELLS, 0, 0)
        total = huber(twin - own)
        for k in range(4):
            total = total + huber(jnp.take(own, neighbour_map[k], axis=0) - own)
        weighted = reweight(jnp.sum(pieces, axis=0) - own_observed)
        weighted, total = lax.optimization_barrier((weighted, total))
        copies = jnp.broadcast_to(weighted[None], (ranks,) + weighted.shape)
        weighted = lax.all_to_all(copies, CELLS, 0, 0).reshape(ranks * rows, -1)
        away = backward(theirs, sensitivity, weighted, cells)
        home = backward(mine, sensitivity, weighted, cells)
        half = home + swap(away, "core")
        half, twin = lax.optimization_barrier((half, twin))
        beyond = lax.ppermute(twin, ("core",) + CELLS, halo_pairs(ranks))
        gradient = half + swap(half, "yh")
        total = total + huber(beyond - own)
        own = own - 1.0 * gradient + scale * total
        twin = swap(own, "core")
    place = lax.broadcasted_iota(jnp.int32, (2, 1, 1), 0)
    both = jnp.where(place == core, own[None], twin[None])
    return both.reshape(models.shape)


def solution(mesh):
    fine = Mesh(mesh.devices.reshape(2, 2, 2, 4, 4), ALL)
    return jax.shard_map(
        local,
        mesh=fine,
        in_specs=(P(DATA, CELLS), P(DATA, None), P(CELLS, None), P(), P(CELLS)),
        out_specs=P(CELLS, None),
        check_vma=False,
    )
```

```python
import functools

import jax
import jax.numpy as jnp
from jax import lax
from jax.experimental import pallas as pl
from jax.experimental.pallas import tpu as pltpu
from jax.sharding import Mesh, PartitionSpec as P

ITERS = 2
DATA = ("yh", "core")
CELLS = ("yl", "x", "z")
ALL = DATA + CELLS
ROWS = 256
TALL = 1024
SLOTS = 4
PARAMS = pltpu.CompilerParams(vmem_limit_bytes=24 * 1024 * 1024)
VMEM = pl.BlockSpec(memory_space=pltpu.VMEM)
SMEM = pl.BlockSpec(memory_space=pltpu.SMEM)
ANY = pl.BlockSpec(memory_space=pl.ANY)
F32 = jnp.float32
BF16 = jnp.bfloat16


def huber(diff):
    return diff / jnp.sqrt(1.0 + diff * diff)


def split(value):
    high = value.astype(BF16)
    low = (value - high.astype(F32)).astype(BF16)
    return high, low


def dot(a, b):
    return jnp.dot(a, b, preferred_element_type=F32)


def product(a, b):
    return dot(a[0], b[0]) + (dot(a[0], b[1]) + dot(a[1], b[0]))


def block_of(index, size):
    return pl.ds(pl.multiple_of(index * size, size), size)


def cost(data, cells, sols, wide):
    return pl.CostEstimate(
        flops=6 * data * cells * sols,
        bytes_accessed=4 * (wide * data * cells + cells * sols + data * sols),
        transcendentals=0,
    )


def first_kernel(s_ref, x_ref, p_ref, high_ref, low_ref, xh_ref, xl_ref, in_ref, out_ref, in_sem, out_sem):
    blocks = s_ref.shape[0] // ROWS

    def fetch(i):
        slot = lax.rem(i, SLOTS)
        return pltpu.make_async_copy(s_ref.at[block_of(i, ROWS)], in_ref.at[slot], in_sem.at[slot])

    def flush(i):
        rows = block_of(i, ROWS)
        return pltpu.make_async_copy(out_ref.at[rows], p_ref.at[rows], out_sem.at[i])

    for i in range(SLOTS):
        fetch(i).start()
    xh_ref[...], xl_ref[...] = split(x_ref[...])

    @pl.loop(0, blocks)
    def _(i):
        fetch(i).wait()
        high, low = split(in_ref[lax.rem(i, SLOTS)])
        rows = block_of(i, ROWS)
        high_ref[rows, :] = high
        low_ref[rows, :] = low

        @pl.when(i + SLOTS < blocks)
        def _():
            fetch(i + SLOTS).start()

        out_ref[rows, :] = product((high, low), (xh_ref[...], xl_ref[...]))
        flush(i).start()

    @pl.loop(0, blocks)
    def _(i):
        flush(i).wait()


def first_forward(sensitivity, x):
    data, cells = sensitivity.shape
    sols = x.shape[1]
    return pl.pallas_call(
        first_kernel,
        in_specs=[pl.BlockSpec(memory_space=pltpu.HBM), VMEM],
        out_specs=[ANY, VMEM, VMEM],
        out_shape=[
            jax.ShapeDtypeStruct((data, sols), F32),
            pltpu.VMEM((data, cells), BF16),
            pltpu.VMEM((data, cells), BF16),
        ],
        scratch_shapes=[
            pltpu.VMEM((cells, sols), BF16),
            pltpu.VMEM((cells, sols), BF16),
            pltpu.VMEM((SLOTS, ROWS, cells), F32),
            pltpu.VMEM((data, sols), F32),
            pltpu.SemaphoreType.DMA((SLOTS,)),
            pltpu.SemaphoreType.DMA((data // ROWS,)),
        ],
        compiler_params=PARAMS,
        cost_estimate=cost(data, cells, sols, 1),
    )(pltpu.with_memory_space_constraint(sensitivity, pltpu.HBM), x)


def start_kernel(plane_ref, high_ref, low_ref, x_ref, p_ref, xh_ref, xl_ref):
    columns = block_of(plane_ref[0], x_ref.shape[0])
    xh_ref[...], xl_ref[...] = split(x_ref[...])

    @pl.loop(0, p_ref.shape[0] // TALL)
    def _(i):
        rows = block_of(i, TALL)
        sense = (high_ref[rows, columns], low_ref[rows, columns])
        p_ref[rows, :] = product(sense, (xh_ref[...], xl_ref[...]))


def finish_kernel(plane_ref, high_ref, low_ref, x_ref, before_ref, p_ref, xh_ref, xl_ref):
    columns = block_of(plane_ref[0], x_ref.shape[0])
    xh_ref[...], xl_ref[...] = split(x_ref[...])

    @pl.loop(0, p_ref.shape[0] // TALL)
    def _(i):
        rows = block_of(i, TALL)
        sense = (high_ref[rows, columns], low_ref[rows, columns])
        p_ref[rows, :] = before_ref[rows, :] + product(sense, (xh_ref[...], xl_ref[...]))


def pinned(sense):
    return [pltpu.with_memory_space_constraint(half, pltpu.VMEM) for half in sense]


def forward(plane, sense, x, before=None):
    data = sense[0].shape[0]
    cells, sols = x.shape
    args = [plane, *pinned(sense), x]
    if before is not None:
        args += pinned([before])
    return pl.pallas_call(
        start_kernel if before is None else finish_kernel,
        in_specs=[SMEM] + [VMEM] * (len(args) - 1),
        out_specs=VMEM,
        out_shape=pltpu.VMEM((data, sols), F32),
        scratch_shapes=[pltpu.VMEM((cells, sols), BF16), pltpu.VMEM((cells, sols), BF16)],
        compiler_params=PARAMS,
        cost_estimate=cost(data, cells, sols, 0),
    )(*args)


def away_kernel(plane_ref, high_ref, low_ref, w_ref, g_ref, wh_ref, wl_ref):
    wh_ref[...], wl_ref[...] = split(w_ref[...].T)
    home_kernel(plane_ref, high_ref, low_ref, wh_ref, wl_ref, g_ref)


def home_kernel(plane_ref, high_ref, low_ref, wh_ref, wl_ref, g_ref):
    blocks = g_ref.shape[0] // ROWS

    @pl.loop(0, blocks)
    def _(i):
        columns = block_of(plane_ref[0] * blocks + i, ROWS)
        part = product((wh_ref[...], wl_ref[...]), (high_ref[:, columns], low_ref[:, columns]))
        g_ref[block_of(i, ROWS), :] = part.T


def backward(away, home, sense, w, cells):
    data, sols = w.shape
    other, high, low = pl.pallas_call(
        away_kernel,
        in_specs=[SMEM, VMEM, VMEM, VMEM],
        out_specs=[VMEM, VMEM, VMEM],
        out_shape=[
            jax.ShapeDtypeStruct((cells, sols), F32),
            pltpu.VMEM((sols, data), BF16),
            pltpu.VMEM((sols, data), BF16),
        ],
        compiler_params=PARAMS,
        cost_estimate=cost(data, cells, sols, 0),
    )(away, *pinned(sense), w)
    own = pl.pallas_call(
        home_kernel,
        in_specs=[SMEM, VMEM, VMEM, VMEM, VMEM],
        out_specs=VMEM,
        out_shape=jax.ShapeDtypeStruct((cells, sols), F32),
        compiler_params=PARAMS,
        cost_estimate=cost(data, cells, sols, 0),
    )(home, *pinned(sense), *pinned((high, low)))
    return other, own


def weigh_kernel(rank_ref, pieces_ref, observed_ref, copies_ref):
    misfit = jnp.sum(pieces_ref[...], axis=0) - observed_ref[...]
    weighted = misfit / jnp.maximum(jnp.abs(misfit), 1.0)
    copies_ref[...] = jnp.broadcast_to(weighted[None], copies_ref.shape)


def weigh(rank, pieces, observed):
    ranks, rows, sols = pieces.shape
    return pl.pallas_call(
        weigh_kernel,
        grid_spec=pltpu.PrefetchScalarGridSpec(
            num_scalar_prefetch=1,
            grid=(1,),
            in_specs=[
                pl.BlockSpec((ranks, rows, sols), lambda i, rank: (0, 0, 0)),
                pl.BlockSpec((rows, sols), lambda i, rank: (rank[0], 0)),
            ],
            out_specs=pl.BlockSpec((ranks, rows, sols), lambda i, rank: (0, 0, 0)),
        ),
        out_shape=jax.ShapeDtypeStruct(pieces.shape, F32),
        compiler_params=PARAMS,
    )(rank, pieces, observed)


def smooth_kernel(table_ref, own_ref, twin_ref, beyond_ref, total_ref, parts_ref, turned_ref):
    cells, sols = own_ref.shape
    whole = own_ref[...]
    high = whole.astype(BF16)
    rest = whole - high.astype(F32)
    middle = rest.astype(BF16)
    low = (rest - middle.astype(F32)).astype(BF16)
    parts_ref[...] = jnp.concatenate([high, middle, low], axis=1)
    turned_ref[...] = table_ref[...].T
    lanes = lax.broadcasted_iota(jnp.int32, (ROWS, cells), 1).astype(F32)

    @pl.loop(0, cells // ROWS)
    def _(i):
        rows = block_of(i, ROWS)
        own = own_ref[rows, :]
        total = huber(twin_ref[rows, :] - own) + huber(beyond_ref[rows, :] - own)
        for k in range(4):
            chosen = (lanes == turned_ref[rows, k : k + 1]).astype(F32).astype(BF16)
            taken = dot(chosen, parts_ref[...])
            other = taken[:, :sols] + taken[:, sols : 2 * sols] + taken[:, 2 * sols :]
            total = total + huber(other - own)
        total_ref[rows, :] = turned_ref[rows, 4:5] * total


def smooth_of(table, own, twin, beyond):
    cells, sols = own.shape
    return pl.pallas_call(
        smooth_kernel,
        in_specs=[VMEM] * 4,
        out_specs=VMEM,
        out_shape=jax.ShapeDtypeStruct(own.shape, F32),
        scratch_shapes=[pltpu.VMEM((cells, 3 * sols), BF16), pltpu.VMEM((cells, table.shape[0]), F32)],
        compiler_params=PARAMS,
        cost_estimate=pl.CostEstimate(
            flops=24 * cells * cells * sols,
            bytes_accessed=16 * cells * sols,
            transcendentals=12 * cells * sols,
        ),
    )(table, own, twin, beyond)


def swap(value, axis):
    return lax.ppermute(value, axis, [(0, 1), (1, 0)])


def beyond_of(own, ranks):
    up = [(ranks + i, i + 1) for i in range(ranks - 1)]
    down = [(i + 1, ranks + i) for i in range(ranks - 1)]
    return lax.ppermute(own, ("core",) + CELLS, up + down)


def local(sensitivity, observed, models, neighbour_map, edge_mask):
    core = lax.axis_index("core").astype(jnp.int32)
    rank = lax.axis_index(CELLS).astype(jnp.int32).reshape(1)
    ranks = lax.axis_size(CELLS)
    cells = neighbour_map.shape[1]
    rows = observed.shape[0] // ranks
    own_mask = lax.dynamic_slice_in_dim(edge_mask, core * cells, cells, axis=0)
    scale = 0.05 * (1.0 - 0.75 * own_mask.astype(F32))
    table = jnp.concatenate(
        [neighbour_map.astype(F32), scale[None], jnp.zeros((3, cells), F32)], axis=0
    )
    own = lax.dynamic_slice_in_dim(models, core * cells, cells, axis=0)
    twin = lax.dynamic_slice_in_dim(models, (1 - core) * cells, cells, axis=0)
    mine, theirs = core.reshape(1), (1 - core).reshape(1)
    models, own, twin, table, rank, mine, theirs = lax.optimization_barrier(
        (models, own, twin, table, rank, mine, theirs)
    )
    sense = None
    for step in range(ITERS):
        if step == 0:
            beyond = beyond_of(own, ranks)
            partial, *sense = first_forward(sensitivity, models)
        else:
            partial = forward(mine, sense, own)
            twin = swap(own, "core")
            beyond = beyond_of(own, ranks)
            partial = forward(theirs, sense, twin, partial)
        partial, beyond = lax.optimization_barrier((partial, beyond))
        pieces = lax.all_to_all(partial.reshape(ranks, rows, -1), CELLS, 0, 0)
        copies = weigh(rank, pieces, observed)
        weighted = lax.all_to_all(copies, CELLS, 0, 0).reshape(ranks * rows, -1)
        away, home = backward(theirs, mine, sense, weighted, cells)
        half = home + swap(away, "core")
        half, own, twin, beyond = lax.optimization_barrier((half, own, twin, beyond))
        gradient = half + swap(half, "yh")
        own = own - 1.0 * gradient + smooth_of(table, own, twin, beyond)
    twin = swap(own, "core")
    place = lax.broadcasted_iota(jnp.int32, (2, 1, 1), 0)
    both = jnp.where(place == core, own[None], twin[None])
    return both.reshape(models.shape)


def solution(mesh):
    fine = Mesh(mesh.devices.reshape(2, 2, 2, 4, 4), ALL)
    return jax.shard_map(
        local,
        mesh=fine,
        in_specs=(P(DATA, CELLS), P(DATA, None), P(CELLS, None), P(), P(CELLS)),
        out_specs=P(CELLS, None),
        check_vma=False,
    )
```

```python
import functools

import jax
import jax.numpy as jnp
from jax import lax
from jax.experimental import pallas as pl
from jax.experimental.pallas import tpu as pltpu
from jax.sharding import Mesh, PartitionSpec as P

ITERS = 2
DATA = ("yh", "core")
CELLS = ("yl", "x", "z")
ALL = DATA + CELLS
ROWS = 256
PARAMS = pltpu.CompilerParams(vmem_limit_bytes=24 * 1024 * 1024)
VMEM = pl.BlockSpec(memory_space=pltpu.VMEM)
SMEM = pl.BlockSpec(memory_space=pltpu.SMEM)
ANY = pl.BlockSpec(memory_space=pl.ANY)
F32 = jnp.float32
BF16 = jnp.bfloat16


def huber(diff):
    return diff / jnp.sqrt(1.0 + diff * diff)


def split(value):
    high = value.astype(BF16)
    low = (value - high.astype(F32)).astype(BF16)
    return high, low


def dot(a, b):
    return jnp.dot(a, b, preferred_element_type=F32)


def product(a, b):
    return dot(a[0], b[0]) + (dot(a[0], b[1]) + dot(a[1], b[0]))


def block_of(index, size):
    return pl.ds(pl.multiple_of(index * size, size), size)


def cost(data, cells, sols, wide):
    return pl.CostEstimate(
        flops=6 * data * cells * sols,
        bytes_accessed=4 * (wide * data * cells + cells * sols + data * sols),
        transcendentals=0,
    )


def first_kernel(blocks_ref, s_ref, x_ref, *refs):
    chunks = blocks_ref.shape[0]
    outs, (xh_ref, xl_ref, in_ref, in_sem) = refs[: 3 * chunks], refs[3 * chunks :]
    steps = outs[0].shape[0] // ROWS

    def fetch(chunk, step):
        start = pl.multiple_of((blocks_ref[chunk] * steps + step) * ROWS, ROWS)
        slot = chunk * steps + step
        return pltpu.make_async_copy(s_ref.at[pl.ds(start, ROWS)], in_ref.at[slot], in_sem.at[slot])

    order = [(chunk, step) for chunk in range(chunks) for step in range(steps)]
    for chunk, step in order:
        fetch(chunk, step).start()
    xh_ref[...], xl_ref[...] = split(x_ref[...])
    for chunk, step in order:
        p_ref, high_ref, low_ref = outs[3 * chunk : 3 * chunk + 3]
        fetch(chunk, step).wait()
        high, low = split(in_ref[chunk * steps + step])
        rows = pl.ds(step * ROWS, ROWS)
        high_ref[rows, :] = high
        low_ref[rows, :] = low
        p_ref[rows, :] = product((high, low), (xh_ref[...], xl_ref[...]))


def first_forward(blocks, sensitivity, x, rows):
    cells, sols = x.shape
    chunks = blocks.shape[0]
    one = [
        pltpu.VMEM((rows, sols), F32),
        pltpu.VMEM((rows, cells), BF16),
        pltpu.VMEM((rows, cells), BF16),
    ]
    slots = chunks * rows // ROWS
    return pl.pallas_call(
        first_kernel,
        in_specs=[SMEM, pl.BlockSpec(memory_space=pltpu.HBM), VMEM],
        out_specs=[VMEM] * (3 * chunks),
        out_shape=one * chunks,
        scratch_shapes=[
            pltpu.VMEM((cells, sols), BF16),
            pltpu.VMEM((cells, sols), BF16),
            pltpu.VMEM((slots, ROWS, cells), F32),
            pltpu.SemaphoreType.DMA((slots,)),
        ],
        compiler_params=PARAMS,
        cost_estimate=cost(chunks * rows, cells, sols, 1),
    )(blocks, pltpu.with_memory_space_constraint(sensitivity, pltpu.HBM), x)


def forward_kernel(terms, chunks, before, planes_ref, *refs):
    x_refs, refs = refs[:terms], refs[terms:]
    sense, refs = refs[: 2 * chunks], refs[2 * chunks :]
    starts, outs = (refs[:chunks], refs[chunks:]) if before else ((), refs)
    cells = x_refs[0].shape[0]
    xs = [split(x_ref[...]) for x_ref in x_refs]
    columns = [block_of(planes_ref[t], cells) for t in range(terms)]
    for i in range(chunks):
        total = starts[i][...] if before else None
        for t in range(terms):
            part = product((sense[2 * i][:, columns[t]], sense[2 * i + 1][:, columns[t]]), xs[t])
            total = part if total is None else total + part
        outs[i][...] = total


def forward(planes, xs, sense, before=()):
    chunks = len(sense) // 2
    rows = sense[0].shape[0]
    cells, sols = xs[0].shape
    args = [planes, *xs, *pinned(sense), *pinned(before)]
    return pl.pallas_call(
        functools.partial(forward_kernel, len(xs), chunks, len(before) > 0),
        in_specs=[SMEM] + [VMEM] * (len(args) - 1),
        out_specs=[VMEM] * chunks,
        out_shape=[pltpu.VMEM((rows, sols), F32)] * chunks,
        compiler_params=PARAMS,
        cost_estimate=cost(chunks * rows, len(xs) * cells, sols, 0),
    )(*args)


def pinned(sense):
    return [pltpu.with_memory_space_constraint(half, pltpu.VMEM) for half in sense]


def gather_kernel(chunks, before, *refs):
    w_refs, refs = refs[:chunks], refs[chunks:]
    sense, refs = refs[: 2 * chunks], refs[2 * chunks :]
    start_ref, refs = (refs[0], refs[1:]) if before else (None, refs)
    sum_ref, wh_ref, wl_ref = refs
    for i in range(chunks):
        wh_ref[i], wl_ref[i] = split(w_refs[i][...].T)

    @pl.loop(0, sum_ref.shape[1] // ROWS)
    def _(j):
        columns = block_of(j, ROWS)
        total = start_ref[:, columns] if before else None
        for i in range(chunks):
            part = product((wh_ref[i], wl_ref[i]), (sense[2 * i][:, columns], sense[2 * i + 1][:, columns]))
            total = part if total is None else total + part
        sum_ref[:, columns] = total


def gather_up(ws, sense, before=()):
    chunks = len(ws)
    rows, sols = ws[0].shape
    cells = sense[0].shape[1]
    args = [*ws, *pinned(sense), *pinned(before)]
    return pl.pallas_call(
        functools.partial(gather_kernel, chunks, len(before) > 0),
        in_specs=[VMEM] * len(args),
        out_specs=VMEM,
        out_shape=pltpu.VMEM((sols, cells), F32),
        scratch_shapes=[pltpu.VMEM((chunks, sols, rows), BF16), pltpu.VMEM((chunks, sols, rows), BF16)],
        compiler_params=PARAMS,
        cost_estimate=cost(chunks * rows, cells, sols, 0),
    )(*args)


def close_kernel(plane_ref, w_ref, high_ref, low_ref, start_ref, g_ref, wh_ref, wl_ref):
    blocks = g_ref.shape[0] // ROWS
    wh_ref[...], wl_ref[...] = split(w_ref[...].T)

    @pl.loop(0, blocks)
    def _(j):
        columns = block_of(plane_ref[0] * blocks + j, ROWS)
        part = product((wh_ref[...], wl_ref[...]), (high_ref[:, columns], low_ref[:, columns]))
        g_ref[block_of(j, ROWS), :] = (start_ref[:, columns] + part).T


def close(plane, w, sense, before, cells):
    rows, sols = w.shape
    args = [plane, w, *pinned(sense), *pinned([before])]
    return pl.pallas_call(
        close_kernel,
        in_specs=[SMEM] + [VMEM] * (len(args) - 1),
        out_specs=VMEM,
        out_shape=jax.ShapeDtypeStruct((cells, sols), F32),
        scratch_shapes=[pltpu.VMEM((sols, rows), BF16), pltpu.VMEM((sols, rows), BF16)],
        compiler_params=PARAMS,
        cost_estimate=cost(rows, cells, sols, 0),
    )(*args)


def weigh_kernel(rank_ref, pieces_ref, observed_ref, copies_ref):
    misfit = jnp.sum(pieces_ref[...], axis=0) - observed_ref[...]
    weighted = misfit / jnp.maximum(jnp.abs(misfit), 1.0)
    copies_ref[...] = jnp.broadcast_to(weighted[None], copies_ref.shape)


def weigh(rank, pieces, observed):
    ranks, rows, sols = pieces.shape
    return pl.pallas_call(
        weigh_kernel,
        grid_spec=pltpu.PrefetchScalarGridSpec(
            num_scalar_prefetch=1,
            grid=(1,),
            in_specs=[
                pl.BlockSpec((ranks, rows, sols), lambda i, rank: (0, 0, 0)),
                pl.BlockSpec((rows, sols), lambda i, rank: (rank[0], 0)),
            ],
            out_specs=pl.BlockSpec((ranks, rows, sols), lambda i, rank: (0, 0, 0)),
        ),
        out_shape=jax.ShapeDtypeStruct(pieces.shape, F32),
        compiler_params=PARAMS,
    )(rank, pieces, observed)


def smooth_kernel(table_ref, own_ref, twin_ref, beyond_ref, total_ref, parts_ref, turned_ref):
    cells, sols = own_ref.shape
    whole = own_ref[...]
    high = whole.astype(BF16)
    rest = whole - high.astype(F32)
    middle = rest.astype(BF16)
    low = (rest - middle.astype(F32)).astype(BF16)
    parts_ref[...] = jnp.concatenate([high, middle, low], axis=1)
    turned_ref[...] = table_ref[...].T
    lanes = lax.broadcasted_iota(jnp.int32, (ROWS, cells), 1).astype(F32)

    @pl.loop(0, cells // ROWS)
    def _(i):
        rows = block_of(i, ROWS)
        own = own_ref[rows, :]
        total = huber(twin_ref[rows, :] - own) + huber(beyond_ref[rows, :] - own)
        for k in range(4):
            chosen = (lanes == turned_ref[rows, k : k + 1]).astype(F32).astype(BF16)
            taken = dot(chosen, parts_ref[...])
            other = taken[:, :sols] + taken[:, sols : 2 * sols] + taken[:, 2 * sols :]
            total = total + huber(other - own)
        total_ref[rows, :] = turned_ref[rows, 4:5] * total


def smooth_of(table, own, twin, beyond):
    cells, sols = own.shape
    return pl.pallas_call(
        smooth_kernel,
        in_specs=[VMEM] * 4,
        out_specs=VMEM,
        out_shape=jax.ShapeDtypeStruct(own.shape, F32),
        scratch_shapes=[pltpu.VMEM((cells, 3 * sols), BF16), pltpu.VMEM((cells, table.shape[0]), F32)],
        compiler_params=PARAMS,
        cost_estimate=pl.CostEstimate(
            flops=24 * cells * cells * sols,
            bytes_accessed=16 * cells * sols,
            transcendentals=12 * cells * sols,
        ),
    )(table, own, twin, beyond)


def swap(value, axis):
    return lax.ppermute(value, axis, [(0, 1), (1, 0)])


def beyond_of(own, ranks):
    up = [(ranks + i, i + 1) for i in range(ranks - 1)]
    down = [(i + 1, ranks + i) for i in range(ranks - 1)]
    return lax.ppermute(own, ("core",) + CELLS, up + down)


def ring_of(value, shift):
    yh, core, yl, x, z = (lax.axis_size(axis) for axis in ALL)
    pairs = []
    for h in range(yh):
        for l in range(yl):
            for i in range(x):
                for j in range(z):
                    at = lambda c, i, j: (((h * core + c) * yl + l) * x + i % x) * z + j % z
                    pairs.append((at(0, i, j), at(0, i + shift, j)))
                    pairs.append((at(1, i, j), at(1, i, j + shift)))
    return lax.ppermute(value, ALL, pairs)


def spread(value):
    yh, core, yl, x, z = (lax.axis_size(axis) for axis in ALL)
    at = lambda h, c, l, i, j: (((h * core + c) * yl + l) * x + i) * z + j
    groups = []
    for h in range(yh):
        groups += [[at(h, 0, l, i, j) for l in range(yl) for j in range(z)] for i in range(x)]
        groups += [[at(h, 1, l, i, j) for l in range(yl) for i in range(x)] for j in range(z)]
    return lax.all_to_all(value, ALL, 0, 0, axis_index_groups=groups, tiled=True)


def local(sensitivity, observed, models, neighbour_map, edge_mask):
    core = lax.axis_index("core").astype(jnp.int32)
    x, z = (lax.axis_index(axis).astype(jnp.int32) for axis in ("x", "z"))
    ring = jnp.where(core == 0, x, z)
    sub = lax.axis_index("yl").astype(jnp.int32) * lax.axis_size("z") + jnp.where(core == 0, z, x)
    rings = lax.axis_size("x")
    ranks = lax.axis_size(CELLS)
    subs = ranks // rings
    rank = (ring * subs + sub).reshape(1)
    block = [((ring + s) % rings).reshape(1) for s in range(rings)]
    sides = jnp.concatenate([block[1], block[3]])
    mine, theirs = core.reshape(1), (1 - core).reshape(1)
    both = jnp.concatenate([mine, theirs])
    cells = neighbour_map.shape[1]
    rows = observed.shape[0] // rings
    own_mask = lax.dynamic_slice_in_dim(edge_mask, core * cells, cells, axis=0)
    scale = 0.05 * (1.0 - 0.75 * own_mask.astype(F32))
    table = jnp.concatenate(
        [neighbour_map.astype(F32), scale[None], jnp.zeros((3, cells), F32)], axis=0
    )
    own = lax.dynamic_slice_in_dim(models, core * cells, cells, axis=0)
    twin = lax.dynamic_slice_in_dim(models, (1 - core) * cells, cells, axis=0)
    models, own, twin, table, rank, mine, theirs, both, block, sides = lax.optimization_barrier(
        (models, own, twin, table, rank, mine, theirs, both, block, sides)
    )
    for step in range(ITERS):
        if step == 0:
            p2, *s2 = first_forward(block[2], sensitivity, models, rows)
            r2 = ring_of(p2, 2)
            p1, h1, l1, p3, h3, l3 = first_forward(sides, sensitivity, models, rows)
            s1, s3 = [h1, l1], [h3, l3]
            r1, r3 = ring_of(p1, 1), ring_of(p3, 3)
            p0, *s0 = first_forward(block[0], sensitivity, models, rows)
        else:
            p2, p1, p3 = forward(mine, [own], s2 + s1 + s3)
            twin = swap(own, "core")
            (p2,) = forward(theirs, [twin], s2, [p2])
            r2 = ring_of(p2, 2)
            p1, p3 = forward(theirs, [twin], s1 + s3, [p1, p3])
            r1, r3 = ring_of(p1, 1), ring_of(p3, 3)
            (p0,) = forward(both, [own, twin], s0)
        pieces = spread(p0 + (r1 + r3) + r2)
        copies = weigh(rank, pieces.reshape(subs, rows // subs, -1), observed)
        w0 = spread(copies.reshape(rows, -1))
        w2, w3, w1 = ring_of(w0, 2), ring_of(w0, 1), ring_of(w0, 3)
        near = gather_up([w0], s0)
        near = gather_up([w1, w3], s1 + s3, [near])
        near, sent = lax.optimization_barrier((near, own))
        beyond = beyond_of(sent, ranks)
        away = close(theirs, w2, s2, near, cells)
        home = close(mine, w2, s2, near, cells)
        half = home + swap(away, "core")
        half, own, twin, beyond = lax.optimization_barrier((half, own, twin, beyond))
        gradient = half + swap(half, "yh")
        own = own - 1.0 * gradient + smooth_of(table, own, twin, beyond)
    twin = swap(own, "core")
    place = lax.broadcasted_iota(jnp.int32, (2, 1, 1), 0)
    planes = jnp.where(place == core, own[None], twin[None])
    return planes.reshape(models.shape)


def solution(mesh):
    fine = Mesh(mesh.devices.reshape(2, 2, 2, 4, 4), ALL)
    return jax.shard_map(
        local,
        mesh=fine,
        in_specs=(P(DATA, CELLS), P(DATA, None), P(CELLS, None), P(), P(CELLS)),
        out_specs=P(CELLS, None),
        check_vma=False,
    )
```

```python
import functools

import jax
import jax.numpy as jnp
from jax import lax
from jax.experimental import pallas as pl
from jax.experimental.pallas import tpu as pltpu
from jax.sharding import Mesh, PartitionSpec as P

ITERS = 2
DATA = ("yh", "core")
CELLS = ("yl", "x", "z")
ALL = DATA + CELLS
ROWS = 256
PARAMS = pltpu.CompilerParams(vmem_limit_bytes=24 * 1024 * 1024)
VMEM = pl.BlockSpec(memory_space=pltpu.VMEM)
SMEM = pl.BlockSpec(memory_space=pltpu.SMEM)
ANY = pl.BlockSpec(memory_space=pl.ANY)
F32 = jnp.float32
BF16 = jnp.bfloat16


def huber(diff):
    return diff / jnp.sqrt(1.0 + diff * diff)


def split(value):
    high = value.astype(BF16)
    low = (value - high.astype(F32)).astype(BF16)
    return high, low


def dot(a, b):
    return jnp.dot(a, b, preferred_element_type=F32)


def product(a, b):
    return dot(a[0], b[0]) + (dot(a[0], b[1]) + dot(a[1], b[0]))


def block_of(index, size):
    return pl.ds(pl.multiple_of(index * size, size), size)


def cost(data, cells, sols, wide):
    return pl.CostEstimate(
        flops=6 * data * cells * sols,
        bytes_accessed=4 * (wide * data * cells + cells * sols + data * sols),
        transcendentals=0,
    )


def first_kernel(blocks_ref, s_ref, x_ref, *refs):
    chunks = blocks_ref.shape[0]
    outs, (xh_ref, xl_ref, in_ref, in_sem) = refs[: 3 * chunks], refs[3 * chunks :]
    steps = outs[0].shape[0] // ROWS

    def fetch(chunk, step):
        start = pl.multiple_of((blocks_ref[chunk] * steps + step) * ROWS, ROWS)
        slot = chunk * steps + step
        return pltpu.make_async_copy(s_ref.at[pl.ds(start, ROWS)], in_ref.at[slot], in_sem.at[slot])

    order = [(chunk, step) for chunk in range(chunks) for step in range(steps)]
    for chunk, step in order:
        fetch(chunk, step).start()
    xh_ref[...], xl_ref[...] = split(x_ref[...])
    for chunk, step in order:
        p_ref, high_ref, low_ref = outs[3 * chunk : 3 * chunk + 3]
        fetch(chunk, step).wait()
        high, low = split(in_ref[chunk * steps + step])
        rows = pl.ds(step * ROWS, ROWS)
        high_ref[rows, :] = high
        low_ref[rows, :] = low
        p_ref[rows, :] = product((high, low), (xh_ref[...], xl_ref[...]))


def first_forward(blocks, sensitivity, x, rows):
    cells, sols = x.shape
    chunks = blocks.shape[0]
    one = [
        pltpu.VMEM((rows, sols), F32),
        pltpu.VMEM((rows, cells), BF16),
        pltpu.VMEM((rows, cells), BF16),
    ]
    slots = chunks * rows // ROWS
    return pl.pallas_call(
        first_kernel,
        in_specs=[SMEM, pl.BlockSpec(memory_space=pltpu.HBM), VMEM],
        out_specs=[VMEM] * (3 * chunks),
        out_shape=one * chunks,
        scratch_shapes=[
            pltpu.VMEM((cells, sols), BF16),
            pltpu.VMEM((cells, sols), BF16),
            pltpu.VMEM((slots, ROWS, cells), F32),
            pltpu.SemaphoreType.DMA((slots,)),
        ],
        compiler_params=PARAMS,
        cost_estimate=cost(chunks * rows, cells, sols, 1),
    )(blocks, pltpu.with_memory_space_constraint(sensitivity, pltpu.HBM), x)


def forward_kernel(terms, chunks, before, planes_ref, *refs):
    x_refs, refs = refs[:terms], refs[terms:]
    sense, refs = refs[: 2 * chunks], refs[2 * chunks :]
    starts, outs = (refs[:chunks], refs[chunks:]) if before else ((), refs)
    cells = x_refs[0].shape[0]
    xs = [split(x_ref[...]) for x_ref in x_refs]
    columns = [block_of(planes_ref[t], cells) for t in range(terms)]
    for i in range(chunks):
        total = starts[i][...] if before else None
        for t in range(terms):
            part = product((sense[2 * i][:, columns[t]], sense[2 * i + 1][:, columns[t]]), xs[t])
            total = part if total is None else total + part
        outs[i][...] = total


def forward(planes, xs, sense, before=()):
    chunks = len(sense) // 2
    rows = sense[0].shape[0]
    cells, sols = xs[0].shape
    args = [planes, *xs, *pinned(sense), *pinned(before)]
    return pl.pallas_call(
        functools.partial(forward_kernel, len(xs), chunks, len(before) > 0),
        in_specs=[SMEM] + [VMEM] * (len(args) - 1),
        out_specs=[VMEM] * chunks,
        out_shape=[pltpu.VMEM((rows, sols), F32)] * chunks,
        compiler_params=PARAMS,
        cost_estimate=cost(chunks * rows, len(xs) * cells, sols, 0),
    )(*args)


def pinned(sense):
    return [pltpu.with_memory_space_constraint(half, pltpu.VMEM) for half in sense]


def gather_kernel(chunks, before, *refs):
    w_refs, refs = refs[:chunks], refs[chunks:]
    sense, refs = refs[: 2 * chunks], refs[2 * chunks :]
    start_ref, refs = (refs[0], refs[1:]) if before else (None, refs)
    sum_ref, wh_ref, wl_ref = refs
    for i in range(chunks):
        wh_ref[i], wl_ref[i] = split(w_refs[i][...].T)

    @pl.loop(0, sum_ref.shape[1] // ROWS)
    def _(j):
        columns = block_of(j, ROWS)
        total = start_ref[:, columns] if before else None
        for i in range(chunks):
            part = product((wh_ref[i], wl_ref[i]), (sense[2 * i][:, columns], sense[2 * i + 1][:, columns]))
            total = part if total is None else total + part
        sum_ref[:, columns] = total


def gather_up(ws, sense, before=()):
    chunks = len(ws)
    rows, sols = ws[0].shape
    cells = sense[0].shape[1]
    args = [*ws, *pinned(sense), *pinned(before)]
    return pl.pallas_call(
        functools.partial(gather_kernel, chunks, len(before) > 0),
        in_specs=[VMEM] * len(args),
        out_specs=VMEM,
        out_shape=pltpu.VMEM((sols, cells), F32),
        scratch_shapes=[pltpu.VMEM((chunks, sols, rows), BF16), pltpu.VMEM((chunks, sols, rows), BF16)],
        compiler_params=PARAMS,
        cost_estimate=cost(chunks * rows, cells, sols, 0),
    )(*args)


def close_kernel(plane_ref, w_ref, high_ref, low_ref, start_ref, g_ref, wh_ref, wl_ref):
    blocks = g_ref.shape[0] // ROWS
    wh_ref[...], wl_ref[...] = split(w_ref[...].T)

    @pl.loop(0, blocks)
    def _(j):
        columns = block_of(plane_ref[0] * blocks + j, ROWS)
        part = product((wh_ref[...], wl_ref[...]), (high_ref[:, columns], low_ref[:, columns]))
        g_ref[block_of(j, ROWS), :] = (start_ref[:, columns] + part).T


def close(plane, w, sense, before, cells):
    rows, sols = w.shape
    args = [plane, w, *pinned(sense), *pinned([before])]
    return pl.pallas_call(
        close_kernel,
        in_specs=[SMEM] + [VMEM] * (len(args) - 1),
        out_specs=VMEM,
        out_shape=jax.ShapeDtypeStruct((cells, sols), F32),
        scratch_shapes=[pltpu.VMEM((sols, rows), BF16), pltpu.VMEM((sols, rows), BF16)],
        compiler_params=PARAMS,
        cost_estimate=cost(rows, cells, sols, 0),
    )(*args)


def weigh_kernel(rank_ref, pieces_ref, observed_ref, copies_ref):
    misfit = jnp.sum(pieces_ref[...], axis=0) - observed_ref[...]
    weighted = misfit / jnp.maximum(jnp.abs(misfit), 1.0)
    copies_ref[...] = jnp.broadcast_to(weighted[None], copies_ref.shape)


def weigh(rank, pieces, observed):
    ranks, rows, sols = pieces.shape
    return pl.pallas_call(
        weigh_kernel,
        grid_spec=pltpu.PrefetchScalarGridSpec(
            num_scalar_prefetch=1,
            grid=(1,),
            in_specs=[
                pl.BlockSpec((ranks, rows, sols), lambda i, rank: (0, 0, 0)),
                pl.BlockSpec((rows, sols), lambda i, rank: (rank[0], 0)),
            ],
            out_specs=pl.BlockSpec((ranks, rows, sols), lambda i, rank: (0, 0, 0)),
        ),
        out_shape=jax.ShapeDtypeStruct(pieces.shape, F32),
        compiler_params=PARAMS,
    )(rank, pieces, observed)


def smooth_kernel(table_ref, own_ref, twin_ref, total_ref, parts_ref, turned_ref):
    cells, sols = own_ref.shape
    whole = own_ref[...]
    high = whole.astype(BF16)
    rest = whole - high.astype(F32)
    middle = rest.astype(BF16)
    low = (rest - middle.astype(F32)).astype(BF16)
    parts_ref[...] = jnp.concatenate([high, middle, low], axis=1)
    turned_ref[...] = table_ref[...].T
    lanes = lax.broadcasted_iota(jnp.int32, (ROWS, cells), 1).astype(F32)

    @pl.loop(0, cells // ROWS)
    def _(i):
        rows = block_of(i, ROWS)
        own = own_ref[rows, :]
        total = huber(twin_ref[rows, :] - own)
        for k in range(4):
            chosen = (lanes == turned_ref[rows, k : k + 1]).astype(F32).astype(BF16)
            taken = dot(chosen, parts_ref[...])
            other = taken[:, :sols] + taken[:, sols : 2 * sols] + taken[:, 2 * sols :]
            total = total + huber(other - own)
        total_ref[rows, :] = total


def smooth_of(table, own, twin):
    cells, sols = own.shape
    return pl.pallas_call(
        smooth_kernel,
        in_specs=[VMEM] * 3,
        out_specs=VMEM,
        out_shape=jax.ShapeDtypeStruct(own.shape, F32),
        scratch_shapes=[pltpu.VMEM((cells, 3 * sols), BF16), pltpu.VMEM((cells, table.shape[0]), F32)],
        compiler_params=PARAMS,
        cost_estimate=pl.CostEstimate(
            flops=24 * cells * cells * sols,
            bytes_accessed=16 * cells * sols,
            transcendentals=12 * cells * sols,
        ),
    )(table, own, twin)


def edge_kernel(table_ref, own_ref, beyond_ref, start_ref, total_ref):
    weight = table_ref[...].T[:, 4:5]
    total_ref[...] = weight * (start_ref[...] + huber(beyond_ref[...] - own_ref[...]))


def edge_of(table, own, beyond, start):
    cells, sols = own.shape
    return pl.pallas_call(
        edge_kernel,
        in_specs=[VMEM] * 4,
        out_specs=VMEM,
        out_shape=jax.ShapeDtypeStruct(own.shape, F32),
        compiler_params=PARAMS,
        cost_estimate=pl.CostEstimate(
            flops=6 * cells * sols, bytes_accessed=16 * cells * sols, transcendentals=2 * cells * sols
        ),
    )(table, own, beyond, start)


def swap(value, axis):
    return lax.ppermute(value, axis, [(0, 1), (1, 0)])


def beyond_of(own, ranks):
    up = [(ranks + i, i + 1) for i in range(ranks - 1)]
    down = [(i + 1, ranks + i) for i in range(ranks - 1)]
    return lax.ppermute(own, ("core",) + CELLS, up + down)


def ring_of(value, shift):
    yh, core, yl, x, z = (lax.axis_size(axis) for axis in ALL)
    pairs = []
    for h in range(yh):
        for l in range(yl):
            for i in range(x):
                for j in range(z):
                    at = lambda c, i, j: (((h * core + c) * yl + l) * x + i % x) * z + j % z
                    pairs.append((at(0, i, j), at(0, i + shift, j)))
                    pairs.append((at(1, i, j), at(1, i, j + shift)))
    return lax.ppermute(value, ALL, pairs)


def spread(value):
    yh, core, yl, x, z = (lax.axis_size(axis) for axis in ALL)
    at = lambda h, c, l, i, j: (((h * core + c) * yl + l) * x + i) * z + j
    groups = []
    for h in range(yh):
        groups += [[at(h, 0, l, i, j) for l in range(yl) for j in range(z)] for i in range(x)]
        groups += [[at(h, 1, l, i, j) for l in range(yl) for i in range(x)] for j in range(z)]
    return lax.all_to_all(value, ALL, 0, 0, axis_index_groups=groups, tiled=True)


def local(sensitivity, observed, models, neighbour_map, edge_mask):
    core = lax.axis_index("core").astype(jnp.int32)
    x, z = (lax.axis_index(axis).astype(jnp.int32) for axis in ("x", "z"))
    ring = jnp.where(core == 0, x, z)
    sub = lax.axis_index("yl").astype(jnp.int32) * lax.axis_size("z") + jnp.where(core == 0, z, x)
    rings = lax.axis_size("x")
    ranks = lax.axis_size(CELLS)
    subs = ranks // rings
    rank = (ring * subs + sub).reshape(1)
    block = [((ring + s) % rings).reshape(1) for s in range(rings)]
    sides = jnp.concatenate([block[1], block[3]])
    mine, theirs = core.reshape(1), (1 - core).reshape(1)
    both = jnp.concatenate([mine, theirs])
    cells = neighbour_map.shape[1]
    rows = observed.shape[0] // rings
    low_core = core == 0
    rank, mine, theirs, both, block, sides, low_core = lax.optimization_barrier(
        (rank, mine, theirs, both, block, sides, low_core)
    )
    for step in range(ITERS):
        if step == 0:
            p2, *s2 = first_forward(block[2], sensitivity, models, rows)
            r2 = ring_of(p2, 2)
            p1, h1, l1, p3, h3, l3 = first_forward(sides, sensitivity, models, rows)
            s1, s3 = [h1, l1], [h3, l3]
            r1, r3 = ring_of(p1, 1), ring_of(p3, 3)
            p0, *s0 = first_forward(block[0], sensitivity, models, rows)
        else:
            p2, p1, p3 = forward(mine, [own], s2 + s1 + s3)
            twin = swap(own, "core")
            (p2,) = forward(theirs, [twin], s2, [p2])
            r2 = ring_of(p2, 2)
            p1, p3 = forward(theirs, [twin], s1 + s3, [p1, p3])
            r1, r3 = ring_of(p1, 1), ring_of(p3, 3)
            (p0,) = forward(both, [own, twin], s0)
        pieces = spread(p0 + (r1 + r3) + r2)
        copies = weigh(rank, pieces.reshape(subs, rows // subs, -1), observed)
        w0 = spread(copies.reshape(rows, -1))
        if step == 0:
            w0, start, numbers, mask = lax.optimization_barrier((w0, models, neighbour_map, edge_mask))
            own = jnp.where(low_core, start[:cells], start[cells:])
            twin = jnp.where(low_core, start[cells:], start[:cells])
            mask = jnp.where(low_core, mask[:cells], mask[cells:])
            weight = 0.05 * (1.0 - 0.75 * mask.astype(F32))
            table = jnp.concatenate(
                [numbers.astype(F32), weight[None], jnp.zeros((3, cells), F32)], axis=0
            )
        w2, w3, w1 = ring_of(w0, 2), ring_of(w0, 1), ring_of(w0, 3)
        near = gather_up([w0], s0)
        near = gather_up([w1, w3], s1 + s3, [near])
        near, sent = lax.optimization_barrier((near, own))
        beyond = beyond_of(sent, ranks)
        away = close(theirs, w2, s2, near, cells)
        home = close(mine, w2, s2, near, cells)
        half = home + swap(away, "core")
        half, own, twin = lax.optimization_barrier((half, own, twin))
        gradient = half + swap(half, "yh")
        inner = smooth_of(table, own, twin)
        own = own - 1.0 * gradient + edge_of(table, own, beyond, inner)
    twin = swap(own, "core")
    place = lax.broadcasted_iota(jnp.int32, (2, 1, 1), 0)
    planes = jnp.where((place == 0) == low_core, own[None], twin[None])
    return planes.reshape(models.shape)


def solution(mesh):
    fine = Mesh(mesh.devices.reshape(2, 2, 2, 4, 4), ALL)
    return jax.shard_map(
        local,
        mesh=fine,
        in_specs=(P(DATA, CELLS), P(DATA, None), P(CELLS, None), P(), P(CELLS)),
        out_specs=P(CELLS, None),
        check_vma=False,
    )
```

```python
import functools

import jax
import jax.numpy as jnp
from jax import lax
from jax.experimental import pallas as pl
from jax.experimental.pallas import tpu as pltpu
from jax.sharding import Mesh, PartitionSpec as P

ITERS = 2
DATA = ("yh", "core")
CELLS = ("yl", "x", "z")
ALL = DATA + CELLS
ROWS = 256
PARAMS = pltpu.CompilerParams(vmem_limit_bytes=24 * 1024 * 1024)
VMEM = pl.BlockSpec(memory_space=pltpu.VMEM)
SMEM = pl.BlockSpec(memory_space=pltpu.SMEM)
ANY = pl.BlockSpec(memory_space=pl.ANY)
F32 = jnp.float32
BF16 = jnp.bfloat16


def huber(diff):
    return diff / jnp.sqrt(1.0 + diff * diff)


def split(value):
    high = value.astype(BF16)
    low = (value - high.astype(F32)).astype(BF16)
    return high, low


def dot(a, b):
    return jnp.dot(a, b, preferred_element_type=F32)


def product(a, b):
    return dot(a[0], b[0]) + (dot(a[0], b[1]) + dot(a[1], b[0]))


def block_of(index, size):
    return pl.ds(pl.multiple_of(index * size, size), size)


def cost(data, cells, sols, wide):
    return pl.CostEstimate(
        flops=6 * data * cells * sols,
        bytes_accessed=4 * (wide * data * cells + cells * sols + data * sols),
        transcendentals=0,
    )


def first_kernel(blocks_ref, s_ref, x_ref, *refs):
    chunks = blocks_ref.shape[0]
    outs, refs = refs[: 3 * chunks], refs[3 * chunks :]
    xh_ref, xl_ref, in_ref, x_in_ref, in_sem, x_sem = refs
    steps = outs[0].shape[0] // ROWS

    def fetch(chunk, step):
        start = pl.multiple_of((blocks_ref[chunk] * steps + step) * ROWS, ROWS)
        slot = chunk * steps + step
        return pltpu.make_async_copy(s_ref.at[pl.ds(start, ROWS)], in_ref.at[slot], in_sem.at[slot])

    order = [(chunk, step) for chunk in range(chunks) for step in range(steps)]
    take = pltpu.make_async_copy(x_ref, x_in_ref, x_sem)
    take.start()
    for chunk, step in order:
        fetch(chunk, step).start()
    take.wait()
    xh_ref[...], xl_ref[...] = split(x_in_ref[...])
    for chunk, step in order:
        p_ref, high_ref, low_ref = outs[3 * chunk : 3 * chunk + 3]
        fetch(chunk, step).wait()
        high, low = split(in_ref[chunk * steps + step])
        rows = pl.ds(step * ROWS, ROWS)
        high_ref[rows, :] = high
        low_ref[rows, :] = low
        p_ref[rows, :] = product((high, low), (xh_ref[...], xl_ref[...]))


def first_forward(blocks, sensitivity, x, rows):
    cells, sols = x.shape
    chunks = blocks.shape[0]
    slots = chunks * rows // ROWS
    hbm = pl.BlockSpec(memory_space=pltpu.HBM)
    one = [
        pltpu.VMEM((rows, sols), F32),
        pltpu.VMEM((rows, cells), BF16),
        pltpu.VMEM((rows, cells), BF16),
    ]
    return pl.pallas_call(
        first_kernel,
        in_specs=[SMEM, hbm, hbm],
        out_specs=[VMEM] * (3 * chunks + 2),
        out_shape=one * chunks + [pltpu.VMEM((cells, sols), BF16)] * 2,
        scratch_shapes=[
            pltpu.VMEM((slots, ROWS, cells), F32),
            pltpu.VMEM((cells, sols), F32),
            pltpu.SemaphoreType.DMA((slots,)),
            pltpu.SemaphoreType.DMA,
        ],
        compiler_params=PARAMS,
        cost_estimate=cost(chunks * rows, cells, sols, 1),
    )(blocks, *[pltpu.with_memory_space_constraint(value, pltpu.HBM) for value in (sensitivity, x)])


def rest_kernel(blocks_ref, s_ref, xh_ref, xl_ref, *outs):
    tall = outs[0].shape[0]
    for chunk in range(blocks_ref.shape[0]):
        p_ref, high_ref, low_ref = outs[3 * chunk : 3 * chunk + 3]
        for step in range(tall // ROWS):
            start = pl.multiple_of(blocks_ref[chunk] * tall + step * ROWS, ROWS)
            high, low = split(s_ref[pl.ds(start, ROWS), :])
            rows = pl.ds(step * ROWS, ROWS)
            high_ref[rows, :] = high
            low_ref[rows, :] = low
            p_ref[rows, :] = product((high, low), (xh_ref[...], xl_ref[...]))


def rest_forward(blocks, sensitivity, halves, rows):
    cells, sols = halves[0].shape
    chunks = blocks.shape[0]
    one = [
        pltpu.VMEM((rows, sols), F32),
        pltpu.VMEM((rows, cells), BF16),
        pltpu.VMEM((rows, cells), BF16),
    ]
    return pl.pallas_call(
        rest_kernel,
        in_specs=[SMEM] + [VMEM] * 3,
        out_specs=[VMEM] * (3 * chunks),
        out_shape=one * chunks,
        compiler_params=PARAMS,
        cost_estimate=cost(chunks * rows, cells, sols, 0),
    )(blocks, *pinned([sensitivity]), *pinned(halves))


def forward_kernel(terms, chunks, before, planes_ref, *refs):
    x_refs, refs = refs[:terms], refs[terms:]
    sense, refs = refs[: 2 * chunks], refs[2 * chunks :]
    starts, outs = (refs[:chunks], refs[chunks:]) if before else ((), refs)
    cells = x_refs[0].shape[0]
    xs = [split(x_ref[...]) for x_ref in x_refs]
    columns = [block_of(planes_ref[t], cells) for t in range(terms)]
    for i in range(chunks):
        total = starts[i][...] if before else None
        for t in range(terms):
            part = product((sense[2 * i][:, columns[t]], sense[2 * i + 1][:, columns[t]]), xs[t])
            total = part if total is None else total + part
        outs[i][...] = total


def forward(planes, xs, sense, before=()):
    chunks = len(sense) // 2
    rows = sense[0].shape[0]
    cells, sols = xs[0].shape
    args = [planes, *xs, *pinned(sense), *pinned(before)]
    return pl.pallas_call(
        functools.partial(forward_kernel, len(xs), chunks, len(before) > 0),
        in_specs=[SMEM] + [VMEM] * (len(args) - 1),
        out_specs=[VMEM] * chunks,
        out_shape=[pltpu.VMEM((rows, sols), F32)] * chunks,
        compiler_params=PARAMS,
        cost_estimate=cost(chunks * rows, len(xs) * cells, sols, 0),
    )(*args)


def pinned(sense):
    return [pltpu.with_memory_space_constraint(half, pltpu.VMEM) for half in sense]


def gather_kernel(chunks, before, *refs):
    w_refs, refs = refs[:chunks], refs[chunks:]
    sense, refs = refs[: 2 * chunks], refs[2 * chunks :]
    start_ref, refs = (refs[0], refs[1:]) if before else (None, refs)
    sum_ref, wh_ref, wl_ref = refs
    for i in range(chunks):
        wh_ref[i], wl_ref[i] = split(w_refs[i][...].T)

    @pl.loop(0, sum_ref.shape[1] // ROWS)
    def _(j):
        columns = block_of(j, ROWS)
        total = start_ref[:, columns] if before else None
        for i in range(chunks):
            part = product((wh_ref[i], wl_ref[i]), (sense[2 * i][:, columns], sense[2 * i + 1][:, columns]))
            total = part if total is None else total + part
        sum_ref[:, columns] = total


def gather_up(ws, sense, before=()):
    chunks = len(ws)
    rows, sols = ws[0].shape
    cells = sense[0].shape[1]
    args = [*ws, *pinned(sense), *pinned(before)]
    return pl.pallas_call(
        functools.partial(gather_kernel, chunks, len(before) > 0),
        in_specs=[VMEM] * len(args),
        out_specs=VMEM,
        out_shape=pltpu.VMEM((sols, cells), F32),
        scratch_shapes=[pltpu.VMEM((chunks, sols, rows), BF16), pltpu.VMEM((chunks, sols, rows), BF16)],
        compiler_params=PARAMS,
        cost_estimate=cost(chunks * rows, cells, sols, 0),
    )(*args)


def close_kernel(plane_ref, w_ref, high_ref, low_ref, start_ref, g_ref, wh_ref, wl_ref):
    blocks = g_ref.shape[0] // ROWS
    wh_ref[...], wl_ref[...] = split(w_ref[...].T)

    @pl.loop(0, blocks)
    def _(j):
        columns = block_of(plane_ref[0] * blocks + j, ROWS)
        part = product((wh_ref[...], wl_ref[...]), (high_ref[:, columns], low_ref[:, columns]))
        g_ref[block_of(j, ROWS), :] = (start_ref[:, columns] + part).T


def close(plane, w, sense, before, cells):
    rows, sols = w.shape
    args = [plane, w, *pinned(sense), *pinned([before])]
    return pl.pallas_call(
        close_kernel,
        in_specs=[SMEM] + [VMEM] * (len(args) - 1),
        out_specs=VMEM,
        out_shape=jax.ShapeDtypeStruct((cells, sols), F32),
        scratch_shapes=[pltpu.VMEM((sols, rows), BF16), pltpu.VMEM((sols, rows), BF16)],
        compiler_params=PARAMS,
        cost_estimate=cost(rows, cells, sols, 0),
    )(*args)


def weigh_kernel(rank_ref, pieces_ref, observed_ref, copies_ref):
    misfit = jnp.sum(pieces_ref[...], axis=0) - observed_ref[...]
    weighted = misfit / jnp.maximum(jnp.abs(misfit), 1.0)
    copies_ref[...] = jnp.broadcast_to(weighted[None], copies_ref.shape)


def weigh(rank, pieces, observed):
    ranks, rows, sols = pieces.shape
    return pl.pallas_call(
        weigh_kernel,
        grid_spec=pltpu.PrefetchScalarGridSpec(
            num_scalar_prefetch=1,
            grid=(1,),
            in_specs=[
                pl.BlockSpec((ranks, rows, sols), lambda i, rank: (0, 0, 0)),
                pl.BlockSpec((rows, sols), lambda i, rank: (rank[0], 0)),
            ],
            out_specs=pl.BlockSpec((ranks, rows, sols), lambda i, rank: (0, 0, 0)),
        ),
        out_shape=jax.ShapeDtypeStruct(pieces.shape, F32),
        compiler_params=PARAMS,
    )(rank, pieces, observed)


def smooth_kernel(table_ref, own_ref, twin_ref, total_ref, parts_ref, turned_ref):
    cells, sols = own_ref.shape
    whole = own_ref[...]
    high = whole.astype(BF16)
    rest = whole - high.astype(F32)
    middle = rest.astype(BF16)
    low = (rest - middle.astype(F32)).astype(BF16)
    parts_ref[...] = jnp.concatenate([high, middle, low], axis=1)
    turned_ref[...] = table_ref[...].T
    lanes = lax.broadcasted_iota(jnp.int32, (ROWS, cells), 1).astype(F32)

    @pl.loop(0, cells // ROWS)
    def _(i):
        rows = block_of(i, ROWS)
        own = own_ref[rows, :]
        total = huber(twin_ref[rows, :] - own)
        for k in range(4):
            chosen = (lanes == turned_ref[rows, k : k + 1]).astype(F32).astype(BF16)
            taken = dot(chosen, parts_ref[...])
            other = taken[:, :sols] + taken[:, sols : 2 * sols] + taken[:, 2 * sols :]
            total = total + huber(other - own)
        total_ref[rows, :] = total


def smooth_of(table, own, twin):
    cells, sols = own.shape
    return pl.pallas_call(
        smooth_kernel,
        in_specs=[VMEM] * 3,
        out_specs=VMEM,
        out_shape=jax.ShapeDtypeStruct(own.shape, F32),
        scratch_shapes=[pltpu.VMEM((cells, 3 * sols), BF16), pltpu.VMEM((cells, table.shape[0]), F32)],
        compiler_params=PARAMS,
        cost_estimate=pl.CostEstimate(
            flops=24 * cells * cells * sols,
            bytes_accessed=16 * cells * sols,
            transcendentals=12 * cells * sols,
        ),
    )(table, own, twin)


def edge_kernel(table_ref, own_ref, beyond_ref, start_ref, total_ref):
    weight = table_ref[...].T[:, 4:5]
    total_ref[...] = weight * (start_ref[...] + huber(beyond_ref[...] - own_ref[...]))


def edge_of(table, own, beyond, start):
    cells, sols = own.shape
    return pl.pallas_call(
        edge_kernel,
        in_specs=[VMEM] * 4,
        out_specs=VMEM,
        out_shape=jax.ShapeDtypeStruct(own.shape, F32),
        compiler_params=PARAMS,
        cost_estimate=pl.CostEstimate(
            flops=6 * cells * sols, bytes_accessed=16 * cells * sols, transcendentals=2 * cells * sols
        ),
    )(table, own, beyond, start)


def swap(value, axis):
    return lax.ppermute(value, axis, [(0, 1), (1, 0)])


def beyond_of(own, ranks):
    up = [(ranks + i, i + 1) for i in range(ranks - 1)]
    down = [(i + 1, ranks + i) for i in range(ranks - 1)]
    return lax.ppermute(own, ("core",) + CELLS, up + down)


def ring_of(value, shift):
    yh, core, yl, x, z = (lax.axis_size(axis) for axis in ALL)
    pairs = []
    for h in range(yh):
        for l in range(yl):
            for i in range(x):
                for j in range(z):
                    at = lambda c, i, j: (((h * core + c) * yl + l) * x + i % x) * z + j % z
                    pairs.append((at(0, i, j), at(0, i + shift, j)))
                    pairs.append((at(1, i, j), at(1, i, j + shift)))
    return lax.ppermute(value, ALL, pairs)


def spread(value):
    yh, core, yl, x, z = (lax.axis_size(axis) for axis in ALL)
    at = lambda h, c, l, i, j: (((h * core + c) * yl + l) * x + i) * z + j
    groups = []
    for h in range(yh):
        groups += [[at(h, 0, l, i, j) for l in range(yl) for j in range(z)] for i in range(x)]
        groups += [[at(h, 1, l, i, j) for l in range(yl) for i in range(x)] for j in range(z)]
    return lax.all_to_all(value, ALL, 0, 0, axis_index_groups=groups, tiled=True)


def local(sensitivity, observed, models, neighbour_map, edge_mask):
    core = lax.axis_index("core").astype(jnp.int32)
    x, z = (lax.axis_index(axis).astype(jnp.int32) for axis in ("x", "z"))
    ring = jnp.where(core == 0, x, z)
    sub = lax.axis_index("yl").astype(jnp.int32) * lax.axis_size("z") + jnp.where(core == 0, z, x)
    rings = lax.axis_size("x")
    ranks = lax.axis_size(CELLS)
    subs = ranks // rings
    rank = (ring * subs + sub).reshape(1)
    block = [((ring + s) % rings).reshape(1) for s in range(rings)]
    sides = jnp.concatenate([block[1], block[3]])
    mine, theirs = core.reshape(1), (1 - core).reshape(1)
    both = jnp.concatenate([mine, theirs])
    cells = neighbour_map.shape[1]
    rows = observed.shape[0] // rings
    low_core = core == 0
    rank, mine, theirs, both, block, sides, low_core = lax.optimization_barrier(
        (rank, mine, theirs, both, block, sides, low_core)
    )
    for step in range(ITERS):
        if step == 0:
            p1, h1, l1, p3, h3, l3, *halves = first_forward(sides, sensitivity, models, rows)
            s1, s3 = [h1, l1], [h3, l3]
            r1, r3 = ring_of(p1, 1), ring_of(p3, 3)
            p2, *s2 = rest_forward(block[2], sensitivity, halves, rows)
            r2 = ring_of(p2, 2)
            p0, *s0 = rest_forward(block[0], sensitivity, halves, rows)
            p0, start, numbers, mask = lax.optimization_barrier((p0, models, neighbour_map, edge_mask))
            own = jnp.where(low_core, start[:cells], start[cells:])
            twin = jnp.where(low_core, start[cells:], start[:cells])
            mask = jnp.where(low_core, mask[:cells], mask[cells:])
            weight = 0.05 * (1.0 - 0.75 * mask.astype(F32))
            table = jnp.concatenate(
                [numbers.astype(F32), weight[None], jnp.zeros((3, cells), F32)], axis=0
            )
        else:
            p2, p1, p3 = forward(mine, [own], s2 + s1 + s3)
            twin = swap(own, "core")
            (p2,) = forward(theirs, [twin], s2, [p2])
            r2 = ring_of(p2, 2)
            p1, p3 = forward(theirs, [twin], s1 + s3, [p1, p3])
            r1, r3 = ring_of(p1, 1), ring_of(p3, 3)
            (p0,) = forward(both, [own, twin], s0)
        p0, own, twin, table = lax.optimization_barrier((p0 + (r1 + r3) + r2, own, twin, table))
        pieces = spread(p0)
        copies = weigh(rank, pieces.reshape(subs, rows // subs, -1), observed)
        w0 = spread(copies.reshape(rows, -1))
        w0, sent = lax.optimization_barrier((w0, own))
        beyond = beyond_of(sent, ranks)
        w2, w3, w1 = ring_of(w0, 2), ring_of(w0, 1), ring_of(w0, 3)
        near = gather_up([w0], s0)
        near = gather_up([w1, w3], s1 + s3, [near])
        w2, beyond = lax.optimization_barrier((w2, beyond))
        away = close(theirs, w2, s2, near, cells)
        home = close(mine, w2, s2, near, cells)
        half = home + swap(away, "core")
        half, own, twin = lax.optimization_barrier((half, own, twin))
        gradient = half + swap(half, "yh")
        inner = smooth_of(table, own, twin)
        own = own - 1.0 * gradient + edge_of(table, own, beyond, inner)
    twin = swap(own, "core")
    place = lax.broadcasted_iota(jnp.int32, (2, 1, 1), 0)
    planes = jnp.where((place == 0) == low_core, own[None], twin[None])
    return planes.reshape(models.shape)


def solution(mesh):
    fine = Mesh(mesh.devices.reshape(2, 2, 2, 4, 4), ALL)
    return jax.shard_map(
        local,
        mesh=fine,
        in_specs=(P(DATA, CELLS), P(DATA, None), P(CELLS, None), P(), P(CELLS)),
        out_specs=P(CELLS, None),
        check_vma=False,
    )
```

```python
import functools

import jax
import jax.numpy as jnp
from jax import lax
from jax.experimental import pallas as pl
from jax.experimental.pallas import tpu as pltpu
from jax.sharding import Mesh, PartitionSpec as P

ITERS = 2
DATA = ("yh", "core")
CELLS = ("yl", "x", "z")
ALL = DATA + CELLS
ROWS = 256
PARAMS = pltpu.CompilerParams(vmem_limit_bytes=24 * 1024 * 1024)
VMEM = pl.BlockSpec(memory_space=pltpu.VMEM)
SMEM = pl.BlockSpec(memory_space=pltpu.SMEM)
ANY = pl.BlockSpec(memory_space=pl.ANY)
F32 = jnp.float32
BF16 = jnp.bfloat16


def huber(diff):
    return diff / jnp.sqrt(1.0 + diff * diff)


def split(value):
    high = value.astype(BF16)
    low = (value - high.astype(F32)).astype(BF16)
    return high, low


def dot(a, b):
    return jnp.dot(a, b, preferred_element_type=F32)


def product(a, b):
    return dot(a[0], b[0]) + (dot(a[0], b[1]) + dot(a[1], b[0]))


def block_of(index, size):
    return pl.ds(pl.multiple_of(index * size, size), size)


def cost(data, cells, sols, wide):
    return pl.CostEstimate(
        flops=6 * data * cells * sols,
        bytes_accessed=4 * (wide * data * cells + cells * sols + data * sols),
        transcendentals=0,
    )


def first_kernel(blocks_ref, s_ref, x_ref, *refs):
    chunks = blocks_ref.shape[0]
    outs, refs = refs[: 3 * chunks], refs[3 * chunks :]
    xh_ref, xl_ref, in_ref, x_in_ref, in_sem, x_sem = refs
    steps = outs[0].shape[0] // ROWS

    def fetch(chunk, step):
        start = pl.multiple_of((blocks_ref[chunk] * steps + step) * ROWS, ROWS)
        slot = chunk * steps + step
        return pltpu.make_async_copy(s_ref.at[pl.ds(start, ROWS)], in_ref.at[slot], in_sem.at[slot])

    order = [(chunk, step) for chunk in range(chunks) for step in range(steps)]
    take = pltpu.make_async_copy(x_ref, x_in_ref, x_sem)
    take.start()
    for chunk, step in order:
        fetch(chunk, step).start()
    take.wait()
    xh_ref[...], xl_ref[...] = split(x_in_ref[...])
    for chunk, step in order:
        p_ref, high_ref, low_ref = outs[3 * chunk : 3 * chunk + 3]
        fetch(chunk, step).wait()
        high, low = split(in_ref[chunk * steps + step])
        rows = pl.ds(step * ROWS, ROWS)
        high_ref[rows, :] = high
        low_ref[rows, :] = low
        p_ref[rows, :] = product((high, low), (xh_ref[...], xl_ref[...]))


def first_forward(blocks, sensitivity, x, rows):
    cells, sols = x.shape
    chunks = blocks.shape[0]
    slots = chunks * rows // ROWS
    hbm = pl.BlockSpec(memory_space=pltpu.HBM)
    one = [
        pltpu.VMEM((rows, sols), F32),
        pltpu.VMEM((rows, cells), BF16),
        pltpu.VMEM((rows, cells), BF16),
    ]
    return pl.pallas_call(
        first_kernel,
        in_specs=[SMEM, hbm, hbm],
        out_specs=[VMEM] * (3 * chunks + 2),
        out_shape=one * chunks + [pltpu.VMEM((cells, sols), BF16)] * 2,
        scratch_shapes=[
            pltpu.VMEM((slots, ROWS, cells), F32),
            pltpu.VMEM((cells, sols), F32),
            pltpu.SemaphoreType.DMA((slots,)),
            pltpu.SemaphoreType.DMA,
        ],
        compiler_params=PARAMS,
        cost_estimate=cost(chunks * rows, cells, sols, 1),
    )(blocks, *[pltpu.with_memory_space_constraint(value, pltpu.HBM) for value in (sensitivity, x)])


def rest_kernel(blocks_ref, s_ref, xh_ref, xl_ref, *outs):
    tall = outs[0].shape[0]
    for chunk in range(blocks_ref.shape[0]):
        p_ref, high_ref, low_ref = outs[3 * chunk : 3 * chunk + 3]
        for step in range(tall // ROWS):
            start = pl.multiple_of(blocks_ref[chunk] * tall + step * ROWS, ROWS)
            high, low = split(s_ref[pl.ds(start, ROWS), :])
            rows = pl.ds(step * ROWS, ROWS)
            high_ref[rows, :] = high
            low_ref[rows, :] = low
            p_ref[rows, :] = product((high, low), (xh_ref[...], xl_ref[...]))


def rest_forward(blocks, sensitivity, halves, rows):
    cells, sols = halves[0].shape
    chunks = blocks.shape[0]
    one = [
        pltpu.VMEM((rows, sols), F32),
        pltpu.VMEM((rows, cells), BF16),
        pltpu.VMEM((rows, cells), BF16),
    ]
    return pl.pallas_call(
        rest_kernel,
        in_specs=[SMEM] + [VMEM] * 3,
        out_specs=[VMEM] * (3 * chunks),
        out_shape=one * chunks,
        compiler_params=PARAMS,
        cost_estimate=cost(chunks * rows, cells, sols, 0),
    )(blocks, *pinned([sensitivity]), *pinned(halves))


def forward_kernel(terms, chunks, before, planes_ref, *refs):
    x_refs, refs = refs[:terms], refs[terms:]
    sense, refs = refs[: 2 * chunks], refs[2 * chunks :]
    starts, outs = (refs[:chunks], refs[chunks:]) if before else ((), refs)
    cells = x_refs[0].shape[0]
    xs = [split(x_ref[...]) for x_ref in x_refs]
    columns = [block_of(planes_ref[t], cells) for t in range(terms)]
    for i in range(chunks):
        total = starts[i][...] if before else None
        for t in range(terms):
            part = product((sense[2 * i][:, columns[t]], sense[2 * i + 1][:, columns[t]]), xs[t])
            total = part if total is None else total + part
        outs[i][...] = total


def forward(planes, xs, sense, before=()):
    chunks = len(sense) // 2
    rows = sense[0].shape[0]
    cells, sols = xs[0].shape
    args = [planes, *xs, *pinned(sense), *pinned(before)]
    return pl.pallas_call(
        functools.partial(forward_kernel, len(xs), chunks, len(before) > 0),
        in_specs=[SMEM] + [VMEM] * (len(args) - 1),
        out_specs=[VMEM] * chunks,
        out_shape=[pltpu.VMEM((rows, sols), F32)] * chunks,
        compiler_params=PARAMS,
        cost_estimate=cost(chunks * rows, len(xs) * cells, sols, 0),
    )(*args)


def pinned(sense):
    return [pltpu.with_memory_space_constraint(half, pltpu.VMEM) for half in sense]


def gather_kernel(chunks, before, *refs):
    w_refs, refs = refs[:chunks], refs[chunks:]
    sense, refs = refs[: 2 * chunks], refs[2 * chunks :]
    start_ref, refs = (refs[0], refs[1:]) if before else (None, refs)
    sum_ref, wh_ref, wl_ref = refs
    for i in range(chunks):
        wh_ref[i], wl_ref[i] = split(w_refs[i][...].T)

    @pl.loop(0, sum_ref.shape[1] // ROWS)
    def _(j):
        columns = block_of(j, ROWS)
        total = start_ref[:, columns] if before else None
        for i in range(chunks):
            part = product((wh_ref[i], wl_ref[i]), (sense[2 * i][:, columns], sense[2 * i + 1][:, columns]))
            total = part if total is None else total + part
        sum_ref[:, columns] = total


def gather_up(ws, sense, before=()):
    chunks = len(ws)
    rows, sols = ws[0].shape
    cells = sense[0].shape[1]
    args = [*ws, *pinned(sense), *pinned(before)]
    return pl.pallas_call(
        functools.partial(gather_kernel, chunks, len(before) > 0),
        in_specs=[VMEM] * len(args),
        out_specs=VMEM,
        out_shape=pltpu.VMEM((sols, cells), F32),
        scratch_shapes=[pltpu.VMEM((chunks, sols, rows), BF16), pltpu.VMEM((chunks, sols, rows), BF16)],
        compiler_params=PARAMS,
        cost_estimate=cost(chunks * rows, cells, sols, 0),
    )(*args)


def close_kernel(plane_ref, w_ref, high_ref, low_ref, start_ref, g_ref, wh_ref, wl_ref):
    blocks = g_ref.shape[0] // ROWS
    wh_ref[...], wl_ref[...] = split(w_ref[...].T)

    @pl.loop(0, blocks)
    def _(j):
        columns = block_of(plane_ref[0] * blocks + j, ROWS)
        part = product((wh_ref[...], wl_ref[...]), (high_ref[:, columns], low_ref[:, columns]))
        g_ref[block_of(j, ROWS), :] = (start_ref[:, columns] + part).T


def close(plane, w, sense, before, cells):
    rows, sols = w.shape
    args = [plane, w, *pinned(sense), *pinned([before])]
    return pl.pallas_call(
        close_kernel,
        in_specs=[SMEM] + [VMEM] * (len(args) - 1),
        out_specs=VMEM,
        out_shape=jax.ShapeDtypeStruct((cells, sols), F32),
        scratch_shapes=[pltpu.VMEM((sols, rows), BF16), pltpu.VMEM((sols, rows), BF16)],
        compiler_params=PARAMS,
        cost_estimate=cost(rows, cells, sols, 0),
    )(*args)


def weigh_kernel(rank_ref, pieces_ref, observed_ref, copies_ref):
    misfit = jnp.sum(pieces_ref[...], axis=0) - observed_ref[...]
    weighted = misfit / jnp.maximum(jnp.abs(misfit), 1.0)
    copies_ref[...] = jnp.broadcast_to(weighted[None], copies_ref.shape)


def weigh(rank, pieces, observed):
    ranks, rows, sols = pieces.shape
    return pl.pallas_call(
        weigh_kernel,
        grid_spec=pltpu.PrefetchScalarGridSpec(
            num_scalar_prefetch=1,
            grid=(1,),
            in_specs=[
                pl.BlockSpec((ranks, rows, sols), lambda i, rank: (0, 0, 0)),
                pl.BlockSpec((rows, sols), lambda i, rank: (rank[0], 0)),
            ],
            out_specs=pl.BlockSpec((ranks, rows, sols), lambda i, rank: (0, 0, 0)),
        ),
        out_shape=jax.ShapeDtypeStruct(pieces.shape, F32),
        compiler_params=PARAMS,
    )(rank, pieces, observed)


def smooth_kernel(table_ref, own_ref, twin_ref, total_ref, parts_ref, turned_ref):
    cells, sols = own_ref.shape
    whole = own_ref[...]
    high = whole.astype(BF16)
    rest = whole - high.astype(F32)
    middle = rest.astype(BF16)
    low = (rest - middle.astype(F32)).astype(BF16)
    parts_ref[...] = jnp.concatenate([high, middle, low], axis=1)
    turned_ref[...] = table_ref[...].T
    lanes = lax.broadcasted_iota(jnp.int32, (ROWS, cells), 1).astype(F32)

    @pl.loop(0, cells // ROWS)
    def _(i):
        rows = block_of(i, ROWS)
        own = own_ref[rows, :]
        total = huber(twin_ref[rows, :] - own)
        for k in range(4):
            chosen = (lanes == turned_ref[rows, k : k + 1]).astype(F32).astype(BF16)
            taken = dot(chosen, parts_ref[...])
            other = taken[:, :sols] + taken[:, sols : 2 * sols] + taken[:, 2 * sols :]
            total = total + huber(other - own)
        total_ref[rows, :] = total


def smooth_of(table, own, twin):
    cells, sols = own.shape
    return pl.pallas_call(
        smooth_kernel,
        in_specs=[VMEM] * 3,
        out_specs=VMEM,
        out_shape=jax.ShapeDtypeStruct(own.shape, F32),
        scratch_shapes=[pltpu.VMEM((cells, 3 * sols), BF16), pltpu.VMEM((cells, table.shape[0]), F32)],
        compiler_params=PARAMS,
        cost_estimate=pl.CostEstimate(
            flops=24 * cells * cells * sols,
            bytes_accessed=16 * cells * sols,
            transcendentals=12 * cells * sols,
        ),
    )(table, own, twin)


def edge_kernel(table_ref, own_ref, beyond_ref, start_ref, total_ref):
    weight = table_ref[...].T[:, 4:5]
    total_ref[...] = weight * (start_ref[...] + huber(beyond_ref[...] - own_ref[...]))


def edge_of(table, own, beyond, start):
    cells, sols = own.shape
    return pl.pallas_call(
        edge_kernel,
        in_specs=[VMEM] * 4,
        out_specs=VMEM,
        out_shape=jax.ShapeDtypeStruct(own.shape, F32),
        compiler_params=PARAMS,
        cost_estimate=pl.CostEstimate(
            flops=6 * cells * sols, bytes_accessed=16 * cells * sols, transcendentals=2 * cells * sols
        ),
    )(table, own, beyond, start)


def swap(value, axis):
    return lax.ppermute(value, axis, [(0, 1), (1, 0)])


def relay_of(own, ranks):
    half = ranks // 2
    pairs = [(ranks + half - 1, 2 * ranks - 1), (half, 0)]
    return lax.ppermute(own, ("core",) + CELLS, pairs)


def beyond_of(sent, ranks):
    half = ranks // 2
    up = [(ranks + i, i + 1) for i in range(ranks - 1) if i != half - 1]
    down = [(i + 1, ranks + i) for i in range(ranks - 1) if i != half - 1]
    cut = [(2 * ranks - 1, half), (0, ranks + half - 1)]
    return lax.ppermute(sent, ("core",) + CELLS, up + down + cut)


def ring_of(value, shift):
    yh, core, yl, x, z = (lax.axis_size(axis) for axis in ALL)
    pairs = []
    for h in range(yh):
        for l in range(yl):
            for i in range(x):
                for j in range(z):
                    at = lambda c, i, j: (((h * core + c) * yl + l) * x + i % x) * z + j % z
                    pairs.append((at(0, i, j), at(0, i + shift, j)))
                    pairs.append((at(1, i, j), at(1, i, j + shift)))
    return lax.ppermute(value, ALL, pairs)


def spread(value):
    yh, core, yl, x, z = (lax.axis_size(axis) for axis in ALL)
    at = lambda h, c, l, i, j: (((h * core + c) * yl + l) * x + i) * z + j
    groups = []
    for h in range(yh):
        groups += [[at(h, 0, l, i, j) for l in range(yl) for j in range(z)] for i in range(x)]
        groups += [[at(h, 1, l, i, j) for l in range(yl) for i in range(x)] for j in range(z)]
    return lax.all_to_all(value, ALL, 0, 0, axis_index_groups=groups, tiled=True)


def local(sensitivity, observed, models, neighbour_map, edge_mask):
    core = lax.axis_index("core").astype(jnp.int32)
    x, z = (lax.axis_index(axis).astype(jnp.int32) for axis in ("x", "z"))
    ring = jnp.where(core == 0, x, z)
    sub = lax.axis_index("yl").astype(jnp.int32) * lax.axis_size("z") + jnp.where(core == 0, z, x)
    rings = lax.axis_size("x")
    ranks = lax.axis_size(CELLS)
    subs = ranks // rings
    rank = (ring * subs + sub).reshape(1)
    block = [((ring + s) % rings).reshape(1) for s in range(rings)]
    sides = jnp.concatenate([block[1], block[3]])
    mine, theirs = core.reshape(1), (1 - core).reshape(1)
    both = jnp.concatenate([mine, theirs])
    cells = neighbour_map.shape[1]
    rows = observed.shape[0] // rings
    low_core = core == 0
    cells_rank = lax.axis_index(CELLS).astype(jnp.int32)
    carrier = cells_rank == core * (ranks - 1)
    rank, mine, theirs, both, block, sides, low_core, carrier = lax.optimization_barrier(
        (rank, mine, theirs, both, block, sides, low_core, carrier)
    )
    for step in range(ITERS):
        if step == 0:
            p2, h2, l2, *halves = first_forward(block[2], sensitivity, models, rows)
            s2 = [h2, l2]
            r2 = ring_of(p2, 2)
            p1, h1, l1, p3, h3, l3 = rest_forward(sides, sensitivity, halves, rows)
            s1, s3 = [h1, l1], [h3, l3]
            r1, r3 = ring_of(p1, 1), ring_of(p3, 3)
            p1, halves = lax.optimization_barrier((p1, halves))
            p0, *s0 = rest_forward(block[0], sensitivity, halves, rows)
            p0, start, numbers, mask = lax.optimization_barrier((p0, models, neighbour_map, edge_mask))
            own = jnp.where(low_core, start[:cells], start[cells:])
            twin = jnp.where(low_core, start[cells:], start[:cells])
            mask = jnp.where(low_core, mask[:cells], mask[cells:])
            weight = 0.05 * (1.0 - 0.75 * mask.astype(F32))
            table = jnp.concatenate(
                [numbers.astype(F32), weight[None], jnp.zeros((3, cells), F32)], axis=0
            )
        else:
            p2, p1, p3 = forward(mine, [own], s2 + s1 + s3)
            twin = swap(own, "core")
            (p2,) = forward(theirs, [twin], s2, [p2])
            r2 = ring_of(p2, 2)
            p1, p3 = forward(theirs, [twin], s1 + s3, [p1, p3])
            r1, r3 = ring_of(p1, 1), ring_of(p3, 3)
            (p0,) = forward(both, [own, twin], s0)
        p0, own, twin, table = lax.optimization_barrier((p0 + (r1 + r3) + r2, own, twin, table))
        pieces = spread(p0)
        copies = weigh(rank, pieces.reshape(subs, rows // subs, -1), observed)
        w0 = spread(copies.reshape(rows, -1))
        w0, sent = lax.optimization_barrier((w0, own))
        relay = relay_of(sent, ranks)
        w2, w3, w1 = ring_of(w0, 2), ring_of(w0, 1), ring_of(w0, 3)
        near = gather_up([w0], s0)
        near = gather_up([w1, w3], s1 + s3, [near])
        near, relay = lax.optimization_barrier((near, relay))
        beyond = beyond_of(jnp.where(carrier, relay, own), ranks)
        away = close(theirs, w2, s2, near, cells)
        home = close(mine, w2, s2, near, cells)
        half = home + swap(away, "core")
        half, own, twin = lax.optimization_barrier((half, own, twin))
        gradient = half + swap(half, "yh")
        inner = smooth_of(table, own, twin)
        own = own - 1.0 * gradient + edge_of(table, own, beyond, inner)
    twin = swap(own, "core")
    place = lax.broadcasted_iota(jnp.int32, (2, 1, 1), 0)
    planes = jnp.where((place == 0) == low_core, own[None], twin[None])
    return planes.reshape(models.shape)


def solution(mesh):
    fine = Mesh(mesh.devices.reshape(2, 2, 2, 4, 4), ALL)
    return jax.shard_map(
        local,
        mesh=fine,
        in_specs=(P(DATA, CELLS), P(DATA, None), P(CELLS, None), P(), P(CELLS)),
        out_specs=P(CELLS, None),
        check_vma=False,
    )
```

```python
import functools

import jax
import jax.numpy as jnp
from jax import lax
from jax.experimental import pallas as pl
from jax.experimental.pallas import tpu as pltpu
from jax.sharding import Mesh, PartitionSpec as P

ITERS = 2
DATA = ("yh", "core")
CELLS = ("yl", "x", "z")
ALL = DATA + CELLS
ROWS = 256
PARAMS = pltpu.CompilerParams(vmem_limit_bytes=24 * 1024 * 1024)
VMEM = pl.BlockSpec(memory_space=pltpu.VMEM)
SMEM = pl.BlockSpec(memory_space=pltpu.SMEM)
ANY = pl.BlockSpec(memory_space=pl.ANY)
F32 = jnp.float32
BF16 = jnp.bfloat16


def huber(diff):
    return diff / jnp.sqrt(1.0 + diff * diff)


def split(value):
    high = value.astype(BF16)
    low = (value - high.astype(F32)).astype(BF16)
    return high, low


def dot(a, b):
    return jnp.dot(a, b, preferred_element_type=F32)


def product(a, b):
    return dot(a[0], b[0]) + (dot(a[0], b[1]) + dot(a[1], b[0]))


def block_of(index, size):
    return pl.ds(pl.multiple_of(index * size, size), size)


def cost(data, cells, sols, wide):
    return pl.CostEstimate(
        flops=6 * data * cells * sols,
        bytes_accessed=4 * (wide * data * cells + cells * sols + data * sols),
        transcendentals=0,
    )


def first_kernel(blocks_ref, s_ref, x_ref, *refs):
    chunks = blocks_ref.shape[0]
    outs, refs = refs[: 3 * chunks], refs[3 * chunks :]
    xh_ref, xl_ref, in_ref, x_in_ref, in_sem, x_sem = refs
    steps = outs[0].shape[0] // ROWS

    def fetch(chunk, step):
        start = pl.multiple_of((blocks_ref[chunk] * steps + step) * ROWS, ROWS)
        slot = chunk * steps + step
        return pltpu.make_async_copy(s_ref.at[pl.ds(start, ROWS)], in_ref.at[slot], in_sem.at[slot])

    order = [(chunk, step) for chunk in range(chunks) for step in range(steps)]
    take = pltpu.make_async_copy(x_ref, x_in_ref, x_sem)
    take.start()
    for chunk, step in order:
        fetch(chunk, step).start()
    take.wait()
    xh_ref[...], xl_ref[...] = split(x_in_ref[...])
    for chunk, step in order:
        p_ref, high_ref, low_ref = outs[3 * chunk : 3 * chunk + 3]
        fetch(chunk, step).wait()
        high, low = split(in_ref[chunk * steps + step])
        rows = pl.ds(step * ROWS, ROWS)
        high_ref[rows, :] = high
        low_ref[rows, :] = low
        p_ref[rows, :] = product((high, low), (xh_ref[...], xl_ref[...]))


def first_forward(blocks, sensitivity, x, rows):
    cells, sols = x.shape
    chunks = blocks.shape[0]
    slots = chunks * rows // ROWS
    hbm = pl.BlockSpec(memory_space=pltpu.HBM)
    one = [
        pltpu.VMEM((rows, sols), F32),
        pltpu.VMEM((rows, cells), BF16),
        pltpu.VMEM((rows, cells), BF16),
    ]
    return pl.pallas_call(
        first_kernel,
        in_specs=[SMEM, hbm, hbm],
        out_specs=[VMEM] * (3 * chunks + 2),
        out_shape=one * chunks + [pltpu.VMEM((cells, sols), BF16)] * 2,
        scratch_shapes=[
            pltpu.VMEM((slots, ROWS, cells), F32),
            pltpu.VMEM((cells, sols), F32),
            pltpu.SemaphoreType.DMA((slots,)),
            pltpu.SemaphoreType.DMA,
        ],
        compiler_params=PARAMS,
        cost_estimate=cost(chunks * rows, cells, sols, 1),
    )(blocks, *[pltpu.with_memory_space_constraint(value, pltpu.HBM) for value in (sensitivity, x)])


def rest_kernel(blocks_ref, s_ref, xh_ref, xl_ref, *outs):
    tall = outs[0].shape[0]
    for chunk in range(blocks_ref.shape[0]):
        p_ref, high_ref, low_ref = outs[3 * chunk : 3 * chunk + 3]
        for step in range(tall // ROWS):
            start = pl.multiple_of(blocks_ref[chunk] * tall + step * ROWS, ROWS)
            high, low = split(s_ref[pl.ds(start, ROWS), :])
            rows = pl.ds(step * ROWS, ROWS)
            high_ref[rows, :] = high
            low_ref[rows, :] = low
            p_ref[rows, :] = product((high, low), (xh_ref[...], xl_ref[...]))


def rest_forward(blocks, sensitivity, halves, rows):
    cells, sols = halves[0].shape
    chunks = blocks.shape[0]
    one = [
        pltpu.VMEM((rows, sols), F32),
        pltpu.VMEM((rows, cells), BF16),
        pltpu.VMEM((rows, cells), BF16),
    ]
    return pl.pallas_call(
        rest_kernel,
        in_specs=[SMEM] + [VMEM] * 3,
        out_specs=[VMEM] * (3 * chunks),
        out_shape=one * chunks,
        compiler_params=PARAMS,
        cost_estimate=cost(chunks * rows, cells, sols, 0),
    )(blocks, *pinned([sensitivity]), *pinned(halves))


def forward_kernel(terms, chunks, before, planes_ref, *refs):
    x_refs, refs = refs[:terms], refs[terms:]
    sense, refs = refs[: 2 * chunks], refs[2 * chunks :]
    starts, outs = (refs[:chunks], refs[chunks:]) if before else ((), refs)
    cells = x_refs[0].shape[0]
    xs = [split(x_ref[...]) for x_ref in x_refs]
    columns = [block_of(planes_ref[t], cells) for t in range(terms)]
    for i in range(chunks):
        total = starts[i][...] if before else None
        for t in range(terms):
            part = product((sense[2 * i][:, columns[t]], sense[2 * i + 1][:, columns[t]]), xs[t])
            total = part if total is None else total + part
        outs[i][...] = total


def forward(planes, xs, sense, before=()):
    chunks = len(sense) // 2
    rows = sense[0].shape[0]
    cells, sols = xs[0].shape
    args = [planes, *xs, *pinned(sense), *pinned(before)]
    return pl.pallas_call(
        functools.partial(forward_kernel, len(xs), chunks, len(before) > 0),
        in_specs=[SMEM] + [VMEM] * (len(args) - 1),
        out_specs=[VMEM] * chunks,
        out_shape=[pltpu.VMEM((rows, sols), F32)] * chunks,
        compiler_params=PARAMS,
        cost_estimate=cost(chunks * rows, len(xs) * cells, sols, 0),
    )(*args)


def pinned(sense):
    return [pltpu.with_memory_space_constraint(half, pltpu.VMEM) for half in sense]


def gather_kernel(chunks, before, *refs):
    w_refs, refs = refs[:chunks], refs[chunks:]
    sense, refs = refs[: 2 * chunks], refs[2 * chunks :]
    start_ref, refs = (refs[0], refs[1:]) if before else (None, refs)
    sum_ref, wh_ref, wl_ref = refs
    for i in range(chunks):
        wh_ref[i], wl_ref[i] = split(w_refs[i][...].T)

    @pl.loop(0, sum_ref.shape[1] // ROWS)
    def _(j):
        columns = block_of(j, ROWS)
        total = start_ref[:, columns] if before else None
        for i in range(chunks):
            part = product((wh_ref[i], wl_ref[i]), (sense[2 * i][:, columns], sense[2 * i + 1][:, columns]))
            total = part if total is None else total + part
        sum_ref[:, columns] = total


def gather_up(ws, sense, before=()):
    chunks = len(ws)
    rows, sols = ws[0].shape
    cells = sense[0].shape[1]
    args = [*ws, *pinned(sense), *pinned(before)]
    return pl.pallas_call(
        functools.partial(gather_kernel, chunks, len(before) > 0),
        in_specs=[VMEM] * len(args),
        out_specs=VMEM,
        out_shape=pltpu.VMEM((sols, cells), F32),
        scratch_shapes=[pltpu.VMEM((chunks, sols, rows), BF16), pltpu.VMEM((chunks, sols, rows), BF16)],
        compiler_params=PARAMS,
        cost_estimate=cost(chunks * rows, cells, sols, 0),
    )(*args)


def close_kernel(plane_ref, w_ref, high_ref, low_ref, start_ref, g_ref, wh_ref, wl_ref):
    blocks = g_ref.shape[0] // ROWS
    wh_ref[...], wl_ref[...] = split(w_ref[...].T)

    @pl.loop(0, blocks)
    def _(j):
        columns = block_of(plane_ref[0] * blocks + j, ROWS)
        part = product((wh_ref[...], wl_ref[...]), (high_ref[:, columns], low_ref[:, columns]))
        g_ref[block_of(j, ROWS), :] = (start_ref[:, columns] + part).T


def close(plane, w, sense, before, cells):
    rows, sols = w.shape
    args = [plane, w, *pinned(sense), *pinned([before])]
    return pl.pallas_call(
        close_kernel,
        in_specs=[SMEM] + [VMEM] * (len(args) - 1),
        out_specs=VMEM,
        out_shape=jax.ShapeDtypeStruct((cells, sols), F32),
        scratch_shapes=[pltpu.VMEM((sols, rows), BF16), pltpu.VMEM((sols, rows), BF16)],
        compiler_params=PARAMS,
        cost_estimate=cost(rows, cells, sols, 0),
    )(*args)


def weigh_kernel(rank_ref, pieces_ref, observed_ref, copies_ref):
    misfit = jnp.sum(pieces_ref[...], axis=0) - observed_ref[...]
    weighted = misfit / jnp.maximum(jnp.abs(misfit), 1.0)
    copies_ref[...] = jnp.broadcast_to(weighted[None], copies_ref.shape)


def weigh(rank, pieces, observed):
    ranks, rows, sols = pieces.shape
    return pl.pallas_call(
        weigh_kernel,
        grid_spec=pltpu.PrefetchScalarGridSpec(
            num_scalar_prefetch=1,
            grid=(1,),
            in_specs=[
                pl.BlockSpec((ranks, rows, sols), lambda i, rank: (0, 0, 0)),
                pl.BlockSpec((rows, sols), lambda i, rank: (rank[0], 0)),
            ],
            out_specs=pl.BlockSpec((ranks, rows, sols), lambda i, rank: (0, 0, 0)),
        ),
        out_shape=jax.ShapeDtypeStruct(pieces.shape, F32),
        compiler_params=PARAMS,
    )(rank, pieces, observed)


def smooth_kernel(table_ref, own_ref, twin_ref, total_ref, parts_ref, turned_ref):
    cells, sols = own_ref.shape
    whole = own_ref[...]
    high = whole.astype(BF16)
    rest = whole - high.astype(F32)
    middle = rest.astype(BF16)
    low = (rest - middle.astype(F32)).astype(BF16)
    parts_ref[...] = jnp.concatenate([high, middle, low], axis=1)
    turned_ref[...] = table_ref[...].T
    lanes = lax.broadcasted_iota(jnp.int32, (ROWS, cells), 1).astype(F32)

    @pl.loop(0, cells // ROWS)
    def _(i):
        rows = block_of(i, ROWS)
        own = own_ref[rows, :]
        total = huber(twin_ref[rows, :] - own)
        for k in range(4):
            chosen = (lanes == turned_ref[rows, k : k + 1]).astype(F32).astype(BF16)
            taken = dot(chosen, parts_ref[...])
            other = taken[:, :sols] + taken[:, sols : 2 * sols] + taken[:, 2 * sols :]
            total = total + huber(other - own)
        total_ref[rows, :] = total


def smooth_of(table, own, twin):
    cells, sols = own.shape
    return pl.pallas_call(
        smooth_kernel,
        in_specs=[VMEM] * 3,
        out_specs=VMEM,
        out_shape=jax.ShapeDtypeStruct(own.shape, F32),
        scratch_shapes=[pltpu.VMEM((cells, 3 * sols), BF16), pltpu.VMEM((cells, table.shape[0]), F32)],
        compiler_params=PARAMS,
        cost_estimate=pl.CostEstimate(
            flops=24 * cells * cells * sols,
            bytes_accessed=16 * cells * sols,
            transcendentals=12 * cells * sols,
        ),
    )(table, own, twin)


def edge_kernel(table_ref, own_ref, beyond_ref, inner_ref, start_ref, new_ref):
    weight = table_ref[...].T[:, 4:5]
    total = inner_ref[...] + huber(beyond_ref[...] - own_ref[...])
    new_ref[...] = start_ref[...] + weight * total


def edge_of(table, own, beyond, inner, start):
    cells, sols = own.shape
    return pl.pallas_call(
        edge_kernel,
        in_specs=[VMEM] * 5,
        out_specs=VMEM,
        out_shape=jax.ShapeDtypeStruct(own.shape, F32),
        compiler_params=PARAMS,
        cost_estimate=pl.CostEstimate(
            flops=6 * cells * sols, bytes_accessed=16 * cells * sols, transcendentals=2 * cells * sols
        ),
    )(table, own, beyond, inner, start)


def swap(value, axis):
    return lax.ppermute(value, axis, [(0, 1), (1, 0)])


def relay_of(own, ranks):
    half = ranks // 2
    pairs = [(ranks + half - 1, 2 * ranks - 1), (half, 0)]
    return lax.ppermute(own, ("core",) + CELLS, pairs)


def beyond_of(sent, ranks):
    half = ranks // 2
    up = [(ranks + i, i + 1) for i in range(ranks - 1) if i != half - 1]
    down = [(i + 1, ranks + i) for i in range(ranks - 1) if i != half - 1]
    cut = [(2 * ranks - 1, half), (0, ranks + half - 1)]
    return lax.ppermute(sent, ("core",) + CELLS, up + down + cut)


def ring_of(value, shift):
    yh, core, yl, x, z = (lax.axis_size(axis) for axis in ALL)
    pairs = []
    for h in range(yh):
        for l in range(yl):
            for i in range(x):
                for j in range(z):
                    at = lambda c, i, j: (((h * core + c) * yl + l) * x + i % x) * z + j % z
                    pairs.append((at(0, i, j), at(0, i + shift, j)))
                    pairs.append((at(1, i, j), at(1, i, j + shift)))
    return lax.ppermute(value, ALL, pairs)


def spread(value):
    yh, core, yl, x, z = (lax.axis_size(axis) for axis in ALL)
    at = lambda h, c, l, i, j: (((h * core + c) * yl + l) * x + i) * z + j
    groups = []
    for h in range(yh):
        groups += [[at(h, 0, l, i, j) for l in range(yl) for j in range(z)] for i in range(x)]
        groups += [[at(h, 1, l, i, j) for l in range(yl) for i in range(x)] for j in range(z)]
    return lax.all_to_all(value, ALL, 0, 0, axis_index_groups=groups, tiled=True)


def local(sensitivity, observed, models, neighbour_map, edge_mask):
    core = lax.axis_index("core").astype(jnp.int32)
    x, z = (lax.axis_index(axis).astype(jnp.int32) for axis in ("x", "z"))
    ring = jnp.where(core == 0, x, z)
    sub = lax.axis_index("yl").astype(jnp.int32) * lax.axis_size("z") + jnp.where(core == 0, z, x)
    rings = lax.axis_size("x")
    ranks = lax.axis_size(CELLS)
    subs = ranks // rings
    rank = (ring * subs + sub).reshape(1)
    block = [((ring + s) % rings).reshape(1) for s in range(rings)]
    sides = jnp.concatenate([block[1], block[3]])
    mine, theirs = core.reshape(1), (1 - core).reshape(1)
    both = jnp.concatenate([mine, theirs])
    cells = neighbour_map.shape[1]
    rows = observed.shape[0] // rings
    low_core = core == 0
    cells_rank = lax.axis_index(CELLS).astype(jnp.int32)
    carrier = cells_rank == core * (ranks - 1)
    rank, mine, theirs, both, block, sides, low_core, carrier = lax.optimization_barrier(
        (rank, mine, theirs, both, block, sides, low_core, carrier)
    )
    for step in range(ITERS):
        if step == 0:
            p2, h2, l2, *halves = first_forward(block[2], sensitivity, models, rows)
            s2 = [h2, l2]
            r2 = ring_of(p2, 2)
            p1, h1, l1, p3, h3, l3 = rest_forward(sides, sensitivity, halves, rows)
            s1, s3 = [h1, l1], [h3, l3]
            r1, r3 = ring_of(p1, 1), ring_of(p3, 3)
            p1, halves = lax.optimization_barrier((p1, halves))
            p0, *s0 = rest_forward(block[0], sensitivity, halves, rows)
            p0, start, numbers, mask = lax.optimization_barrier((p0, models, neighbour_map, edge_mask))
            own = jnp.where(low_core, start[:cells], start[cells:])
            twin = jnp.where(low_core, start[cells:], start[:cells])
            mask = jnp.where(low_core, mask[:cells], mask[cells:])
            weight = 0.05 * (1.0 - 0.75 * mask.astype(F32))
            table = jnp.concatenate(
                [numbers.astype(F32), weight[None], jnp.zeros((3, cells), F32)], axis=0
            )
        else:
            p2, p1, p3 = forward(mine, [own], s2 + s1 + s3)
            twin = swap(own, "core")
            (p2,) = forward(theirs, [twin], s2, [p2])
            r2 = ring_of(p2, 2)
            p1, p3 = forward(theirs, [twin], s1 + s3, [p1, p3])
            r1, r3 = ring_of(p1, 1), ring_of(p3, 3)
            (p0,) = forward(both, [own, twin], s0)
        p0, own, twin, table = lax.optimization_barrier((p0 + (r1 + r3) + r2, own, twin, table))
        pieces = spread(p0)
        copies = weigh(rank, pieces.reshape(subs, rows // subs, -1), observed)
        w0 = spread(copies.reshape(rows, -1))
        w0, sent = lax.optimization_barrier((w0, own))
        relay = relay_of(sent, ranks)
        w2, w3, w1 = ring_of(w0, 2), ring_of(w0, 1), ring_of(w0, 3)
        near = gather_up([w0], s0)
        near = gather_up([w3], s3, [near])
        near = gather_up([w1], s1, [near])
        near, relay = lax.optimization_barrier((near, relay))
        sent = jnp.where(carrier, relay, own)
        away = close(theirs, w2, s2, near, cells)
        home = close(mine, w2, s2, near, cells)
        half = home + swap(away, "core")
        half, own, twin, sent = lax.optimization_barrier((half, own, twin, sent))
        beyond = beyond_of(sent, ranks)
        gradient = half + swap(half, "yh")
        inner = smooth_of(table, own, twin)
        own = edge_of(table, own, beyond, inner, own - 1.0 * gradient)
    twin = swap(own, "core")
    place = lax.broadcasted_iota(jnp.int32, (2, 1, 1), 0)
    planes = jnp.where((place == 0) == low_core, own[None], twin[None])
    return planes.reshape(models.shape)


def solution(mesh):
    fine = Mesh(mesh.devices.reshape(2, 2, 2, 4, 4), ALL)
    return jax.shard_map(
        local,
        mesh=fine,
        in_specs=(P(DATA, CELLS), P(DATA, None), P(CELLS, None), P(), P(CELLS)),
        out_specs=P(CELLS, None),
        check_vma=False,
    )
```

```python
import functools

import jax
import jax.numpy as jnp
from jax import lax
from jax.experimental import pallas as pl
from jax.experimental.pallas import tpu as pltpu
from jax.sharding import Mesh, PartitionSpec as P

ITERS = 2
DATA = ("yh", "core")
CELLS = ("yl", "x", "z")
ALL = DATA + CELLS
ROWS = 256
PARAMS = pltpu.CompilerParams(vmem_limit_bytes=24 * 1024 * 1024)
VMEM = pl.BlockSpec(memory_space=pltpu.VMEM)
SMEM = pl.BlockSpec(memory_space=pltpu.SMEM)
ANY = pl.BlockSpec(memory_space=pl.ANY)
F32 = jnp.float32
BF16 = jnp.bfloat16


def huber(diff):
    return diff / jnp.sqrt(1.0 + diff * diff)


def split(value):
    high = value.astype(BF16)
    low = (value - high.astype(F32)).astype(BF16)
    return high, low


def dot(a, b):
    return jnp.dot(a, b, preferred_element_type=F32)


def product(a, b):
    return dot(a[0], b[0]) + (dot(a[0], b[1]) + dot(a[1], b[0]))


def block_of(index, size):
    return pl.ds(pl.multiple_of(index * size, size), size)


def cost(data, cells, sols, wide):
    return pl.CostEstimate(
        flops=6 * data * cells * sols,
        bytes_accessed=4 * (wide * data * cells + cells * sols + data * sols),
        transcendentals=0,
    )


def first_kernel(blocks_ref, s_ref, x_ref, *refs):
    chunks = blocks_ref.shape[0]
    outs, refs = refs[: 3 * chunks], refs[3 * chunks :]
    xh_ref, xl_ref, in_ref, x_in_ref, in_sem, x_sem = refs
    steps = outs[0].shape[0] // ROWS

    def fetch(chunk, step):
        start = pl.multiple_of((blocks_ref[chunk] * steps + step) * ROWS, ROWS)
        slot = chunk * steps + step
        return pltpu.make_async_copy(s_ref.at[pl.ds(start, ROWS)], in_ref.at[slot], in_sem.at[slot])

    order = [(chunk, step) for chunk in range(chunks) for step in range(steps)]
    take = pltpu.make_async_copy(x_ref, x_in_ref, x_sem)
    take.start()
    for chunk, step in order:
        fetch(chunk, step).start()
    take.wait()
    xh_ref[...], xl_ref[...] = split(x_in_ref[...])
    for chunk, step in order:
        p_ref, high_ref, low_ref = outs[3 * chunk : 3 * chunk + 3]
        fetch(chunk, step).wait()
        high, low = split(in_ref[chunk * steps + step])
        rows = pl.ds(step * ROWS, ROWS)
        high_ref[rows, :] = high
        low_ref[rows, :] = low
        p_ref[rows, :] = product((high, low), (xh_ref[...], xl_ref[...]))


def first_forward(blocks, sensitivity, x, rows):
    cells, sols = x.shape
    chunks = blocks.shape[0]
    slots = chunks * rows // ROWS
    hbm = pl.BlockSpec(memory_space=pltpu.HBM)
    one = [
        pltpu.VMEM((rows, sols), F32),
        pltpu.VMEM((rows, cells), BF16),
        pltpu.VMEM((rows, cells), BF16),
    ]
    return pl.pallas_call(
        first_kernel,
        in_specs=[SMEM, hbm, hbm],
        out_specs=[VMEM] * (3 * chunks + 2),
        out_shape=one * chunks + [pltpu.VMEM((cells, sols), BF16)] * 2,
        scratch_shapes=[
            pltpu.VMEM((slots, ROWS, cells), F32),
            pltpu.VMEM((cells, sols), F32),
            pltpu.SemaphoreType.DMA((slots,)),
            pltpu.SemaphoreType.DMA,
        ],
        compiler_params=PARAMS,
        cost_estimate=cost(chunks * rows, cells, sols, 1),
    )(blocks, *[pltpu.with_memory_space_constraint(value, pltpu.HBM) for value in (sensitivity, x)])


def rest_kernel(blocks_ref, s_ref, xh_ref, xl_ref, *outs):
    tall = outs[0].shape[0]
    for chunk in range(blocks_ref.shape[0]):
        p_ref, high_ref, low_ref = outs[3 * chunk : 3 * chunk + 3]
        for step in range(tall // ROWS):
            start = pl.multiple_of(blocks_ref[chunk] * tall + step * ROWS, ROWS)
            high, low = split(s_ref[pl.ds(start, ROWS), :])
            rows = pl.ds(step * ROWS, ROWS)
            high_ref[rows, :] = high
            low_ref[rows, :] = low
            p_ref[rows, :] = product((high, low), (xh_ref[...], xl_ref[...]))


def rest_forward(blocks, sensitivity, halves, rows):
    cells, sols = halves[0].shape
    chunks = blocks.shape[0]
    one = [
        pltpu.VMEM((rows, sols), F32),
        pltpu.VMEM((rows, cells), BF16),
        pltpu.VMEM((rows, cells), BF16),
    ]
    return pl.pallas_call(
        rest_kernel,
        in_specs=[SMEM] + [VMEM] * 3,
        out_specs=[VMEM] * (3 * chunks),
        out_shape=one * chunks,
        compiler_params=PARAMS,
        cost_estimate=cost(chunks * rows, cells, sols, 0),
    )(blocks, *pinned([sensitivity]), *pinned(halves))


def forward_kernel(terms, chunks, before, planes_ref, *refs):
    x_refs, refs = refs[:terms], refs[terms:]
    sense, refs = refs[: 2 * chunks], refs[2 * chunks :]
    starts, outs = (refs[:chunks], refs[chunks:]) if before else ((), refs)
    cells = x_refs[0].shape[0]
    xs = [split(x_ref[...]) for x_ref in x_refs]
    columns = [block_of(planes_ref[t], cells) for t in range(terms)]
    for i in range(chunks):
        total = starts[i][...] if before else None
        for t in range(terms):
            part = product((sense[2 * i][:, columns[t]], sense[2 * i + 1][:, columns[t]]), xs[t])
            total = part if total is None else total + part
        outs[i][...] = total


def forward(planes, xs, sense, before=()):
    chunks = len(sense) // 2
    rows = sense[0].shape[0]
    cells, sols = xs[0].shape
    args = [planes, *xs, *pinned(sense), *pinned(before)]
    return pl.pallas_call(
        functools.partial(forward_kernel, len(xs), chunks, len(before) > 0),
        in_specs=[SMEM] + [VMEM] * (len(args) - 1),
        out_specs=[VMEM] * chunks,
        out_shape=[pltpu.VMEM((rows, sols), F32)] * chunks,
        compiler_params=PARAMS,
        cost_estimate=cost(chunks * rows, len(xs) * cells, sols, 0),
    )(*args)


def pinned(sense):
    return [pltpu.with_memory_space_constraint(half, pltpu.VMEM) for half in sense]


def gather_kernel(chunks, before, *refs):
    w_refs, refs = refs[:chunks], refs[chunks:]
    sense, refs = refs[: 2 * chunks], refs[2 * chunks :]
    start_ref, refs = (refs[0], refs[1:]) if before else (None, refs)
    sum_ref, wh_ref, wl_ref = refs
    for i in range(chunks):
        wh_ref[i], wl_ref[i] = split(w_refs[i][...].T)

    @pl.loop(0, sum_ref.shape[1] // ROWS)
    def _(j):
        columns = block_of(j, ROWS)
        total = start_ref[:, columns] if before else None
        for i in range(chunks):
            part = product((wh_ref[i], wl_ref[i]), (sense[2 * i][:, columns], sense[2 * i + 1][:, columns]))
            total = part if total is None else total + part
        sum_ref[:, columns] = total


def gather_up(ws, sense, before=()):
    chunks = len(ws)
    rows, sols = ws[0].shape
    cells = sense[0].shape[1]
    args = [*ws, *pinned(sense), *pinned(before)]
    return pl.pallas_call(
        functools.partial(gather_kernel, chunks, len(before) > 0),
        in_specs=[VMEM] * len(args),
        out_specs=VMEM,
        out_shape=pltpu.VMEM((sols, cells), F32),
        scratch_shapes=[pltpu.VMEM((chunks, sols, rows), BF16), pltpu.VMEM((chunks, sols, rows), BF16)],
        compiler_params=PARAMS,
        cost_estimate=cost(chunks * rows, cells, sols, 0),
    )(*args)


def close_kernel(plane_ref, w_ref, high_ref, low_ref, start_ref, g_ref, wh_ref, wl_ref):
    blocks = g_ref.shape[0] // ROWS
    wh_ref[...], wl_ref[...] = split(w_ref[...].T)

    @pl.loop(0, blocks)
    def _(j):
        columns = block_of(plane_ref[0] * blocks + j, ROWS)
        part = product((wh_ref[...], wl_ref[...]), (high_ref[:, columns], low_ref[:, columns]))
        g_ref[block_of(j, ROWS), :] = (start_ref[:, columns] + part).T


def close(plane, w, sense, before, cells):
    rows, sols = w.shape
    args = [plane, w, *pinned(sense), *pinned([before])]
    return pl.pallas_call(
        close_kernel,
        in_specs=[SMEM] + [VMEM] * (len(args) - 1),
        out_specs=VMEM,
        out_shape=jax.ShapeDtypeStruct((cells, sols), F32),
        scratch_shapes=[pltpu.VMEM((sols, rows), BF16), pltpu.VMEM((sols, rows), BF16)],
        compiler_params=PARAMS,
        cost_estimate=cost(rows, cells, sols, 0),
    )(*args)


def weigh_kernel(rank_ref, pieces_ref, observed_ref, copies_ref):
    misfit = jnp.sum(pieces_ref[...], axis=0) - observed_ref[...]
    weighted = misfit / jnp.maximum(jnp.abs(misfit), 1.0)
    copies_ref[...] = jnp.broadcast_to(weighted[None], copies_ref.shape)


def weigh(rank, pieces, observed):
    ranks, rows, sols = pieces.shape
    return pl.pallas_call(
        weigh_kernel,
        grid_spec=pltpu.PrefetchScalarGridSpec(
            num_scalar_prefetch=1,
            grid=(1,),
            in_specs=[
                pl.BlockSpec((ranks, rows, sols), lambda i, rank: (0, 0, 0)),
                pl.BlockSpec((rows, sols), lambda i, rank: (rank[0], 0)),
            ],
            out_specs=pl.BlockSpec((ranks, rows, sols), lambda i, rank: (0, 0, 0)),
        ),
        out_shape=jax.ShapeDtypeStruct(pieces.shape, F32),
        compiler_params=PARAMS,
    )(rank, pieces, observed)


def smooth_kernel(table_ref, own_ref, twin_ref, total_ref, parts_ref, turned_ref):
    cells, sols = own_ref.shape
    whole = own_ref[...]
    high = whole.astype(BF16)
    rest = whole - high.astype(F32)
    middle = rest.astype(BF16)
    low = (rest - middle.astype(F32)).astype(BF16)
    parts_ref[...] = jnp.concatenate([high, middle, low], axis=1)
    turned_ref[...] = table_ref[...].T
    lanes = lax.broadcasted_iota(jnp.int32, (ROWS, cells), 1).astype(F32)

    @pl.loop(0, cells // ROWS)
    def _(i):
        rows = block_of(i, ROWS)
        own = own_ref[rows, :]
        total = huber(twin_ref[rows, :] - own)
        for k in range(4):
            chosen = (lanes == turned_ref[rows, k : k + 1]).astype(F32).astype(BF16)
            taken = dot(chosen, parts_ref[...])
            other = taken[:, :sols] + taken[:, sols : 2 * sols] + taken[:, 2 * sols :]
            total = total + huber(other - own)
        total_ref[rows, :] = total


def smooth_of(table, own, twin):
    cells, sols = own.shape
    return pl.pallas_call(
        smooth_kernel,
        in_specs=[VMEM] * 3,
        out_specs=VMEM,
        out_shape=jax.ShapeDtypeStruct(own.shape, F32),
        scratch_shapes=[pltpu.VMEM((cells, 3 * sols), BF16), pltpu.VMEM((cells, table.shape[0]), F32)],
        compiler_params=PARAMS,
        cost_estimate=pl.CostEstimate(
            flops=24 * cells * cells * sols,
            bytes_accessed=16 * cells * sols,
            transcendentals=12 * cells * sols,
        ),
    )(table, own, twin)


def edge_kernel(table_ref, own_ref, beyond_ref, inner_ref, start_ref, new_ref):
    weight = table_ref[...].T[:, 4:5]
    total = inner_ref[...] + huber(beyond_ref[...] - own_ref[...])
    new_ref[...] = start_ref[...] + weight * total


def edge_of(table, own, beyond, inner, start):
    cells, sols = own.shape
    return pl.pallas_call(
        edge_kernel,
        in_specs=[VMEM] * 5,
        out_specs=VMEM,
        out_shape=jax.ShapeDtypeStruct(own.shape, F32),
        compiler_params=PARAMS,
        cost_estimate=pl.CostEstimate(
            flops=6 * cells * sols, bytes_accessed=16 * cells * sols, transcendentals=2 * cells * sols
        ),
    )(table, own, beyond, inner, start)


def swap(value, axis):
    return lax.ppermute(value, axis, [(0, 1), (1, 0)])


def relay_of(own, ranks):
    half = ranks // 2
    pairs = [(ranks + half - 1, 2 * ranks - 1), (half, 0)]
    return lax.ppermute(own, ("core",) + CELLS, pairs)


def beyond_of(sent, ranks):
    half = ranks // 2
    up = [(ranks + i, i + 1) for i in range(ranks - 1) if i != half - 1]
    down = [(i + 1, ranks + i) for i in range(ranks - 1) if i != half - 1]
    cut = [(2 * ranks - 1, half), (0, ranks + half - 1)]
    return lax.ppermute(sent, ("core",) + CELLS, up + down + cut)


def ring_of(value, shift):
    yh, core, yl, x, z = (lax.axis_size(axis) for axis in ALL)
    pairs = []
    for h in range(yh):
        for l in range(yl):
            for i in range(x):
                for j in range(z):
                    at = lambda c, i, j: (((h * core + c) * yl + l) * x + i % x) * z + j % z
                    pairs.append((at(0, i, j), at(0, i + shift, j)))
                    pairs.append((at(1, i, j), at(1, i, j + shift)))
    return lax.ppermute(value, ALL, pairs)


def spread(value):
    yh, core, yl, x, z = (lax.axis_size(axis) for axis in ALL)
    at = lambda h, c, l, i, j: (((h * core + c) * yl + l) * x + i) * z + j
    groups = []
    for h in range(yh):
        groups += [[at(h, 0, l, i, j) for l in range(yl) for j in range(z)] for i in range(x)]
        groups += [[at(h, 1, l, i, j) for l in range(yl) for i in range(x)] for j in range(z)]
    return lax.all_to_all(value, ALL, 0, 0, axis_index_groups=groups, tiled=True)


def local(sensitivity, observed, models, neighbour_map, edge_mask):
    core = lax.axis_index("core").astype(jnp.int32)
    x, z = (lax.axis_index(axis).astype(jnp.int32) for axis in ("x", "z"))
    ring = jnp.where(core == 0, x, z)
    sub = lax.axis_index("yl").astype(jnp.int32) * lax.axis_size("z") + jnp.where(core == 0, z, x)
    rings = lax.axis_size("x")
    ranks = lax.axis_size(CELLS)
    subs = ranks // rings
    rank = (ring * subs + sub).reshape(1)
    block = [((ring + s) % rings).reshape(1) for s in range(rings)]
    sides = jnp.concatenate([block[1], block[3]])
    mine, theirs = core.reshape(1), (1 - core).reshape(1)
    both = jnp.concatenate([mine, theirs])
    cells = neighbour_map.shape[1]
    rows = observed.shape[0] // rings
    low_core = core == 0
    cells_rank = lax.axis_index(CELLS).astype(jnp.int32)
    carrier = cells_rank == core * (ranks - 1)
    rank, mine, theirs, both, block, sides, low_core, carrier = lax.optimization_barrier(
        (rank, mine, theirs, both, block, sides, low_core, carrier)
    )
    for step in range(ITERS):
        if step == 0:
            p2, h2, l2, *halves = first_forward(block[2], sensitivity, models, rows)
            s2 = [h2, l2]
            r2 = ring_of(p2, 2)
            p1, h1, l1, p3, h3, l3 = rest_forward(sides, sensitivity, halves, rows)
            s1, s3 = [h1, l1], [h3, l3]
            r1, r3 = ring_of(p1, 1), ring_of(p3, 3)
            p1, halves = lax.optimization_barrier((p1, halves))
            p0, *s0 = rest_forward(block[0], sensitivity, halves, rows)
            p0, start, numbers, mask = lax.optimization_barrier((p0, models, neighbour_map, edge_mask))
            own = jnp.where(low_core, start[:cells], start[cells:])
            twin = jnp.where(low_core, start[cells:], start[:cells])
            mask = jnp.where(low_core, mask[:cells], mask[cells:])
            weight = 0.05 * (1.0 - 0.75 * mask.astype(F32))
            table = jnp.concatenate(
                [numbers.astype(F32), weight[None], jnp.zeros((3, cells), F32)], axis=0
            )
        else:
            p2, p1, p3 = forward(mine, [own], s2 + s1 + s3)
            twin = swap(own, "core")
            (p2,) = forward(theirs, [twin], s2, [p2])
            r2 = ring_of(p2, 2)
            p1, p3 = forward(theirs, [twin], s1 + s3, [p1, p3])
            r1, r3 = ring_of(p1, 1), ring_of(p3, 3)
            (p0,) = forward(both, [own, twin], s0)
        p0, r1, r3 = lax.optimization_barrier((p0 + r2, r1, r3))
        p0, own, twin, table = lax.optimization_barrier((p0 + (r1 + r3), own, twin, table))
        pieces = spread(p0)
        copies = weigh(rank, pieces.reshape(subs, rows // subs, -1), observed)
        w0 = spread(copies.reshape(rows, -1))
        w0, sent = lax.optimization_barrier((w0, own))
        relay = relay_of(sent, ranks)
        w2, w3, w1 = ring_of(w0, 2), ring_of(w0, 1), ring_of(w0, 3)
        near = gather_up([w0], s0)
        near = gather_up([w3], s3, [near])
        near = gather_up([w1], s1, [near])
        near, relay = lax.optimization_barrier((near, relay))
        sent = jnp.where(carrier, relay, own)
        away = close(theirs, w2, s2, near, cells)
        home = close(mine, w2, s2, near, cells)
        half = home + swap(away, "core")
        half, own, twin, sent = lax.optimization_barrier((half, own, twin, sent))
        beyond = beyond_of(sent, ranks)
        gradient = half + swap(half, "yh")
        inner = smooth_of(table, own, twin)
        own = edge_of(table, own, beyond, inner, own - 1.0 * gradient)
    twin = swap(own, "core")
    place = lax.broadcasted_iota(jnp.int32, (2, 1, 1), 0)
    planes = jnp.where((place == 0) == low_core, own[None], twin[None])
    return planes.reshape(models.shape)


def solution(mesh):
    fine = Mesh(mesh.devices.reshape(2, 2, 2, 4, 4), ALL)
    return jax.shard_map(
        local,
        mesh=fine,
        in_specs=(P(DATA, CELLS), P(DATA, None), P(CELLS, None), P(), P(CELLS)),
        out_specs=P(CELLS, None),
        check_vma=False,
    )
```

```python
import functools

import jax
import jax.numpy as jnp
from jax import lax
from jax.experimental import pallas as pl
from jax.experimental.pallas import tpu as pltpu
from jax.sharding import Mesh, PartitionSpec as P

ITERS = 2
DATA = ("yh", "core")
CELLS = ("yl", "x", "z")
ALL = DATA + CELLS
ROWS = 256
PARAMS = pltpu.CompilerParams(vmem_limit_bytes=24 * 1024 * 1024)
VMEM = pl.BlockSpec(memory_space=pltpu.VMEM)
SMEM = pl.BlockSpec(memory_space=pltpu.SMEM)
ANY = pl.BlockSpec(memory_space=pl.ANY)
F32 = jnp.float32
BF16 = jnp.bfloat16


def huber(diff):
    return diff / jnp.sqrt(1.0 + diff * diff)


def split(value):
    high = value.astype(BF16)
    low = (value - high.astype(F32)).astype(BF16)
    return high, low


def dot(a, b):
    return jnp.dot(a, b, preferred_element_type=F32)


def product(a, b):
    return dot(a[0], b[0]) + (dot(a[0], b[1]) + dot(a[1], b[0]))


def block_of(index, size):
    return pl.ds(pl.multiple_of(index * size, size), size)


def cost(data, cells, sols, wide):
    return pl.CostEstimate(
        flops=6 * data * cells * sols,
        bytes_accessed=4 * (wide * data * cells + cells * sols + data * sols),
        transcendentals=0,
    )


def first_kernel(blocks_ref, s_ref, x_ref, *refs):
    chunks = blocks_ref.shape[0]
    outs, refs = refs[: 3 * chunks], refs[3 * chunks :]
    xh_ref, xl_ref, in_ref, x_in_ref, in_sem, x_sem = refs
    steps = outs[0].shape[0] // ROWS

    def fetch(chunk, step):
        start = pl.multiple_of((blocks_ref[chunk] * steps + step) * ROWS, ROWS)
        slot = chunk * steps + step
        return pltpu.make_async_copy(s_ref.at[pl.ds(start, ROWS)], in_ref.at[slot], in_sem.at[slot])

    order = [(chunk, step) for chunk in range(chunks) for step in range(steps)]
    take = pltpu.make_async_copy(x_ref, x_in_ref, x_sem)
    take.start()
    for chunk, step in order:
        fetch(chunk, step).start()
    take.wait()
    xh_ref[...], xl_ref[...] = split(x_in_ref[...])
    for chunk, step in order:
        p_ref, high_ref, low_ref = outs[3 * chunk : 3 * chunk + 3]
        fetch(chunk, step).wait()
        high, low = split(in_ref[chunk * steps + step])
        rows = pl.ds(step * ROWS, ROWS)
        high_ref[rows, :] = high
        low_ref[rows, :] = low
        p_ref[rows, :] = product((high, low), (xh_ref[...], xl_ref[...]))


def first_forward(blocks, sensitivity, x, rows):
    cells, sols = x.shape
    chunks = blocks.shape[0]
    slots = chunks * rows // ROWS
    hbm = pl.BlockSpec(memory_space=pltpu.HBM)
    one = [
        pltpu.VMEM((rows, sols), F32),
        pltpu.VMEM((rows, cells), BF16),
        pltpu.VMEM((rows, cells), BF16),
    ]
    return pl.pallas_call(
        first_kernel,
        in_specs=[SMEM, hbm, hbm],
        out_specs=[VMEM] * (3 * chunks + 2),
        out_shape=one * chunks + [pltpu.VMEM((cells, sols), BF16)] * 2,
        scratch_shapes=[
            pltpu.VMEM((slots, ROWS, cells), F32),
            pltpu.VMEM((cells, sols), F32),
            pltpu.SemaphoreType.DMA((slots,)),
            pltpu.SemaphoreType.DMA,
        ],
        compiler_params=PARAMS,
        cost_estimate=cost(chunks * rows, cells, sols, 1),
    )(blocks, *[pltpu.with_memory_space_constraint(value, pltpu.HBM) for value in (sensitivity, x)])


def rest_kernel(blocks_ref, s_ref, xh_ref, xl_ref, *outs):
    tall = outs[0].shape[0]
    for chunk in range(blocks_ref.shape[0]):
        p_ref, high_ref, low_ref = outs[3 * chunk : 3 * chunk + 3]
        for step in range(tall // ROWS):
            start = pl.multiple_of(blocks_ref[chunk] * tall + step * ROWS, ROWS)
            high, low = split(s_ref[pl.ds(start, ROWS), :])
            rows = pl.ds(step * ROWS, ROWS)
            high_ref[rows, :] = high
            low_ref[rows, :] = low
            p_ref[rows, :] = product((high, low), (xh_ref[...], xl_ref[...]))


def rest_forward(blocks, sensitivity, halves, rows):
    cells, sols = halves[0].shape
    chunks = blocks.shape[0]
    one = [
        pltpu.VMEM((rows, sols), F32),
        pltpu.VMEM((rows, cells), BF16),
        pltpu.VMEM((rows, cells), BF16),
    ]
    return pl.pallas_call(
        rest_kernel,
        in_specs=[SMEM] + [VMEM] * 3,
        out_specs=[VMEM] * (3 * chunks),
        out_shape=one * chunks,
        compiler_params=PARAMS,
        cost_estimate=cost(chunks * rows, cells, sols, 0),
    )(blocks, *pinned([sensitivity]), *pinned(halves))


def forward_kernel(terms, chunks, before, planes_ref, *refs):
    x_refs, refs = refs[:terms], refs[terms:]
    sense, refs = refs[: 2 * chunks], refs[2 * chunks :]
    starts, outs = (refs[:chunks], refs[chunks:]) if before else ((), refs)
    cells = x_refs[0].shape[0]
    xs = [split(x_ref[...]) for x_ref in x_refs]
    columns = [block_of(planes_ref[t], cells) for t in range(terms)]
    for i in range(chunks):
        total = starts[i][...] if before else None
        for t in range(terms):
            part = product((sense[2 * i][:, columns[t]], sense[2 * i + 1][:, columns[t]]), xs[t])
            total = part if total is None else total + part
        outs[i][...] = total


def forward(planes, xs, sense, before=()):
    chunks = len(sense) // 2
    rows = sense[0].shape[0]
    cells, sols = xs[0].shape
    args = [planes, *xs, *pinned(sense), *pinned(before)]
    return pl.pallas_call(
        functools.partial(forward_kernel, len(xs), chunks, len(before) > 0),
        in_specs=[SMEM] + [VMEM] * (len(args) - 1),
        out_specs=[VMEM] * chunks,
        out_shape=[pltpu.VMEM((rows, sols), F32)] * chunks,
        compiler_params=PARAMS,
        cost_estimate=cost(chunks * rows, len(xs) * cells, sols, 0),
    )(*args)


def pinned(sense):
    return [pltpu.with_memory_space_constraint(half, pltpu.VMEM) for half in sense]


def gather_kernel(chunks, before, *refs):
    w_refs, refs = refs[:chunks], refs[chunks:]
    sense, refs = refs[: 2 * chunks], refs[2 * chunks :]
    start_ref, refs = (refs[0], refs[1:]) if before else (None, refs)
    sum_ref, wh_ref, wl_ref = refs
    for i in range(chunks):
        wh_ref[i], wl_ref[i] = split(w_refs[i][...].T)

    @pl.loop(0, sum_ref.shape[1] // ROWS)
    def _(j):
        columns = block_of(j, ROWS)
        total = start_ref[:, columns] if before else None
        for i in range(chunks):
            part = product((wh_ref[i], wl_ref[i]), (sense[2 * i][:, columns], sense[2 * i + 1][:, columns]))
            total = part if total is None else total + part
        sum_ref[:, columns] = total


def gather_up(ws, sense, before=()):
    chunks = len(ws)
    rows, sols = ws[0].shape
    cells = sense[0].shape[1]
    args = [*ws, *pinned(sense), *pinned(before)]
    return pl.pallas_call(
        functools.partial(gather_kernel, chunks, len(before) > 0),
        in_specs=[VMEM] * len(args),
        out_specs=VMEM,
        out_shape=pltpu.VMEM((sols, cells), F32),
        scratch_shapes=[pltpu.VMEM((chunks, sols, rows), BF16), pltpu.VMEM((chunks, sols, rows), BF16)],
        compiler_params=PARAMS,
        cost_estimate=cost(chunks * rows, cells, sols, 0),
    )(*args)


def close_kernel(plane_ref, w_ref, high_ref, low_ref, start_ref, g_ref, wh_ref, wl_ref):
    blocks = g_ref.shape[0] // ROWS
    wh_ref[...], wl_ref[...] = split(w_ref[...].T)

    @pl.loop(0, blocks)
    def _(j):
        columns = block_of(plane_ref[0] * blocks + j, ROWS)
        part = product((wh_ref[...], wl_ref[...]), (high_ref[:, columns], low_ref[:, columns]))
        g_ref[block_of(j, ROWS), :] = (start_ref[:, columns] + part).T


def close(plane, w, sense, before, cells):
    rows, sols = w.shape
    args = [plane, w, *pinned(sense), *pinned([before])]
    return pl.pallas_call(
        close_kernel,
        in_specs=[SMEM] + [VMEM] * (len(args) - 1),
        out_specs=VMEM,
        out_shape=jax.ShapeDtypeStruct((cells, sols), F32),
        scratch_shapes=[pltpu.VMEM((sols, rows), BF16), pltpu.VMEM((sols, rows), BF16)],
        compiler_params=PARAMS,
        cost_estimate=cost(rows, cells, sols, 0),
    )(*args)


def weigh_kernel(rank_ref, pieces_ref, observed_ref, copies_ref):
    misfit = jnp.sum(pieces_ref[...], axis=0) - observed_ref[...]
    weighted = misfit / jnp.maximum(jnp.abs(misfit), 1.0)
    copies_ref[...] = jnp.broadcast_to(weighted[None], copies_ref.shape)


def weigh(rank, pieces, observed):
    ranks, rows, sols = pieces.shape
    return pl.pallas_call(
        weigh_kernel,
        grid_spec=pltpu.PrefetchScalarGridSpec(
            num_scalar_prefetch=1,
            grid=(1,),
            in_specs=[
                pl.BlockSpec((ranks, rows, sols), lambda i, rank: (0, 0, 0)),
                pl.BlockSpec((rows, sols), lambda i, rank: (rank[0], 0)),
            ],
            out_specs=pl.BlockSpec((ranks, rows, sols), lambda i, rank: (0, 0, 0)),
        ),
        out_shape=jax.ShapeDtypeStruct(pieces.shape, F32),
        compiler_params=PARAMS,
    )(rank, pieces, observed)


def smooth_kernel(table_ref, own_ref, twin_ref, total_ref, parts_ref, turned_ref):
    cells, sols = own_ref.shape
    whole = own_ref[...]
    high = whole.astype(BF16)
    rest = whole - high.astype(F32)
    middle = rest.astype(BF16)
    low = (rest - middle.astype(F32)).astype(BF16)
    parts_ref[...] = jnp.concatenate([high, middle, low], axis=1)
    turned_ref[...] = table_ref[...].T
    lanes = lax.broadcasted_iota(jnp.int32, (ROWS, cells), 1).astype(F32)

    @pl.loop(0, cells // ROWS)
    def _(i):
        rows = block_of(i, ROWS)
        own = own_ref[rows, :]
        total = huber(twin_ref[rows, :] - own)
        for k in range(4):
            chosen = (lanes == turned_ref[rows, k : k + 1]).astype(F32).astype(BF16)
            taken = dot(chosen, parts_ref[...])
            other = taken[:, :sols] + taken[:, sols : 2 * sols] + taken[:, 2 * sols :]
            total = total + huber(other - own)
        total_ref[rows, :] = total


def smooth_of(table, own, twin):
    cells, sols = own.shape
    return pl.pallas_call(
        smooth_kernel,
        in_specs=[VMEM] * 3,
        out_specs=VMEM,
        out_shape=jax.ShapeDtypeStruct(own.shape, F32),
        scratch_shapes=[pltpu.VMEM((cells, 3 * sols), BF16), pltpu.VMEM((cells, table.shape[0]), F32)],
        compiler_params=PARAMS,
        cost_estimate=pl.CostEstimate(
            flops=24 * cells * cells * sols,
            bytes_accessed=16 * cells * sols,
            transcendentals=12 * cells * sols,
        ),
    )(table, own, twin)


def edge_kernel(table_ref, own_ref, beyond_ref, inner_ref, start_ref, new_ref):
    weight = table_ref[...].T[:, 4:5]
    total = inner_ref[...] + huber(beyond_ref[...] - own_ref[...])
    new_ref[...] = start_ref[...] + weight * total


def edge_of(table, own, beyond, inner, start):
    cells, sols = own.shape
    return pl.pallas_call(
        edge_kernel,
        in_specs=[VMEM] * 5,
        out_specs=VMEM,
        out_shape=jax.ShapeDtypeStruct(own.shape, F32),
        compiler_params=PARAMS,
        cost_estimate=pl.CostEstimate(
            flops=6 * cells * sols, bytes_accessed=16 * cells * sols, transcendentals=2 * cells * sols
        ),
    )(table, own, beyond, inner, start)


def place_kernel(plane_ref, value_ref, *refs):
    out_ref, sem = refs[-2:]
    rows = block_of(plane_ref[0], value_ref.shape[0])
    copy = pltpu.make_async_copy(value_ref, out_ref.at[rows], sem)
    copy.start()
    copy.wait()


def place(plane, value, before=()):
    cells, sols = value.shape
    return pl.pallas_call(
        place_kernel,
        in_specs=[SMEM, VMEM] + [ANY] * len(before),
        out_specs=ANY,
        out_shape=jax.ShapeDtypeStruct((2 * cells, sols), F32),
        scratch_shapes=[pltpu.SemaphoreType.DMA],
        input_output_aliases={2: 0} if before else {},
        compiler_params=PARAMS,
        cost_estimate=pl.CostEstimate(flops=0, bytes_accessed=8 * cells * sols, transcendentals=0),
    )(plane, value, *before)


def swap(value, axis):
    return lax.ppermute(value, axis, [(0, 1), (1, 0)])


def relay_of(own, ranks):
    half = ranks // 2
    pairs = [(ranks + half - 1, 2 * ranks - 1), (half, 0)]
    return lax.ppermute(own, ("core",) + CELLS, pairs)


def beyond_of(sent, ranks):
    half = ranks // 2
    up = [(ranks + i, i + 1) for i in range(ranks - 1) if i != half - 1]
    down = [(i + 1, ranks + i) for i in range(ranks - 1) if i != half - 1]
    cut = [(2 * ranks - 1, half), (0, ranks + half - 1)]
    return lax.ppermute(sent, ("core",) + CELLS, up + down + cut)


def ring_of(value, shift):
    yh, core, yl, x, z = (lax.axis_size(axis) for axis in ALL)
    pairs = []
    for h in range(yh):
        for l in range(yl):
            for i in range(x):
                for j in range(z):
                    at = lambda c, i, j: (((h * core + c) * yl + l) * x + i % x) * z + j % z
                    pairs.append((at(0, i, j), at(0, i, j + shift)))
                    pairs.append((at(1, i, j), at(1, i + shift, j)))
    return lax.ppermute(value, ALL, pairs)


def spread(value):
    yh, core, yl, x, z = (lax.axis_size(axis) for axis in ALL)
    at = lambda h, c, l, i, j: (((h * core + c) * yl + l) * x + i) * z + j
    groups = []
    for h in range(yh):
        groups += [[at(h, 0, l, i, j) for l in range(yl) for i in range(x)] for j in range(z)]
        groups += [[at(h, 1, l, i, j) for l in range(yl) for j in range(z)] for i in range(x)]
    return lax.all_to_all(value, ALL, 0, 0, axis_index_groups=groups, tiled=True)


def local(sensitivity, observed, models, neighbour_map, edge_mask):
    core = lax.axis_index("core").astype(jnp.int32)
    x, z = (lax.axis_index(axis).astype(jnp.int32) for axis in ("x", "z"))
    ring = jnp.where(core == 0, z, x)
    sub = lax.axis_index("yl").astype(jnp.int32) * lax.axis_size("x") + jnp.where(core == 0, x, z)
    rings = lax.axis_size("x")
    ranks = lax.axis_size(CELLS)
    subs = ranks // rings
    rank = (ring * subs + sub).reshape(1)
    block = [((ring + s) % rings).reshape(1) for s in range(rings)]
    sides = jnp.concatenate([block[1], block[3]])
    mine, theirs = core.reshape(1), (1 - core).reshape(1)
    both = jnp.concatenate([mine, theirs])
    cells = neighbour_map.shape[1]
    rows = observed.shape[0] // rings
    low_core = core == 0
    cells_rank = lax.axis_index(CELLS).astype(jnp.int32)
    carrier = cells_rank == core * (ranks - 1)
    rank, mine, theirs, both, block, sides, low_core, carrier = lax.optimization_barrier(
        (rank, mine, theirs, both, block, sides, low_core, carrier)
    )
    for step in range(ITERS):
        if step == 0:
            p2, h2, l2, *halves = first_forward(block[2], sensitivity, models, rows)
            s2 = [h2, l2]
            r2 = ring_of(p2, 2)
            p1, h1, l1, p3, h3, l3 = rest_forward(sides, sensitivity, halves, rows)
            s1, s3 = [h1, l1], [h3, l3]
            r1, r3 = ring_of(p1, 1), ring_of(p3, 3)
            p1, halves = lax.optimization_barrier((p1, halves))
            p0, *s0 = rest_forward(block[0], sensitivity, halves, rows)
            p0, start, numbers, mask = lax.optimization_barrier((p0, models, neighbour_map, edge_mask))
            own = jnp.where(low_core, start[:cells], start[cells:])
            twin = jnp.where(low_core, start[cells:], start[:cells])
            mask = jnp.where(low_core, mask[:cells], mask[cells:])
            weight = 0.05 * (1.0 - 0.75 * mask.astype(F32))
            table = jnp.concatenate(
                [numbers.astype(F32), weight[None], jnp.zeros((3, cells), F32)], axis=0
            )
        else:
            p2, p1, p3 = forward(mine, [own], s2 + s1 + s3)
            twin = swap(own, "core")
            (p2,) = forward(theirs, [twin], s2, [p2])
            r2 = ring_of(p2, 2)
            p1, p3 = forward(theirs, [twin], s1 + s3, [p1, p3])
            r1, r3 = ring_of(p1, 1), ring_of(p3, 3)
            (p0,) = forward(both, [own, twin], s0)
        p0, r1, r3 = lax.optimization_barrier((p0 + r2, r1, r3))
        p0, own, twin, table = lax.optimization_barrier((p0 + (r1 + r3), own, twin, table))
        pieces = spread(p0)
        copies = weigh(rank, pieces.reshape(subs, rows // subs, -1), observed)
        w0 = spread(copies.reshape(rows, -1))
        w0, sent = lax.optimization_barrier((w0, own))
        relay = relay_of(sent, ranks)
        w2, w3, w1 = ring_of(w0, 2), ring_of(w0, 1), ring_of(w0, 3)
        near = gather_up([w0], s0)
        near = gather_up([w3], s3, [near])
        near = gather_up([w1], s1, [near])
        near, relay = lax.optimization_barrier((near, relay))
        sent = jnp.where(carrier, relay, own)
        away = close(theirs, w2, s2, near, cells)
        home = close(mine, w2, s2, near, cells)
        half = home + swap(away, "core")
        half, own, twin, sent = lax.optimization_barrier((half, own, twin, sent))
        beyond = beyond_of(sent, ranks)
        gradient = half + swap(half, "yh")
        inner = smooth_of(table, own, twin)
        own = edge_of(table, own, beyond, inner, own - 1.0 * gradient)
    twin = swap(own, "core")
    return place(theirs, twin, [place(mine, own)])


def solution(mesh):
    fine = Mesh(mesh.devices.reshape(2, 2, 2, 4, 4), ALL)
    return jax.shard_map(
        local,
        mesh=fine,
        in_specs=(P(DATA, CELLS), P(DATA, None), P(CELLS, None), P(), P(CELLS)),
        out_specs=P(CELLS, None),
        check_vma=False,
    )
```

```python
import functools

import jax
import jax.numpy as jnp
from jax import lax
from jax.experimental import pallas as pl
from jax.experimental.pallas import tpu as pltpu
from jax.sharding import Mesh, PartitionSpec as P

ITERS = 2
DATA = ("yh", "core")
CELLS = ("yl", "x", "z")
ALL = DATA + CELLS
ROWS = 256
PARAMS = pltpu.CompilerParams(vmem_limit_bytes=24 * 1024 * 1024)
VMEM = pl.BlockSpec(memory_space=pltpu.VMEM)
SMEM = pl.BlockSpec(memory_space=pltpu.SMEM)
ANY = pl.BlockSpec(memory_space=pl.ANY)
F32 = jnp.float32
BF16 = jnp.bfloat16


def huber(diff):
    return diff / jnp.sqrt(1.0 + diff * diff)


def split(value):
    high = value.astype(BF16)
    low = (value - high.astype(F32)).astype(BF16)
    return high, low


def dot(a, b):
    return jnp.dot(a, b, preferred_element_type=F32)


def product(a, b):
    return dot(a[0], b[0]) + (dot(a[0], b[1]) + dot(a[1], b[0]))


def block_of(index, size):
    return pl.ds(pl.multiple_of(index * size, size), size)


def cost(data, cells, sols, wide):
    return pl.CostEstimate(
        flops=6 * data * cells * sols,
        bytes_accessed=4 * (wide * data * cells + cells * sols + data * sols),
        transcendentals=0,
    )


def first_kernel(blocks_ref, s_ref, x_ref, *refs):
    chunks = blocks_ref.shape[0]
    outs, refs = refs[: 3 * chunks], refs[3 * chunks :]
    xh_ref, xl_ref, in_ref, x_in_ref, in_sem, x_sem = refs
    steps = outs[0].shape[0] // ROWS

    def fetch(chunk, step):
        start = pl.multiple_of((blocks_ref[chunk] * steps + step) * ROWS, ROWS)
        slot = chunk * steps + step
        return pltpu.make_async_copy(s_ref.at[pl.ds(start, ROWS)], in_ref.at[slot], in_sem.at[slot])

    order = [(chunk, step) for chunk in range(chunks) for step in range(steps)]
    take = pltpu.make_async_copy(x_ref, x_in_ref, x_sem)
    take.start()
    for chunk, step in order:
        fetch(chunk, step).start()
    take.wait()
    xh_ref[...], xl_ref[...] = split(x_in_ref[...])
    for chunk, step in order:
        p_ref, high_ref, low_ref = outs[3 * chunk : 3 * chunk + 3]
        fetch(chunk, step).wait()
        high, low = split(in_ref[chunk * steps + step])
        rows = pl.ds(step * ROWS, ROWS)
        high_ref[rows, :] = high
        low_ref[rows, :] = low
        p_ref[rows, :] = product((high, low), (xh_ref[...], xl_ref[...]))


def first_forward(blocks, sensitivity, x, rows):
    cells, sols = x.shape
    chunks = blocks.shape[0]
    slots = chunks * rows // ROWS
    hbm = pl.BlockSpec(memory_space=pltpu.HBM)
    one = [
        pltpu.VMEM((rows, sols), F32),
        pltpu.VMEM((rows, cells), BF16),
        pltpu.VMEM((rows, cells), BF16),
    ]
    return pl.pallas_call(
        first_kernel,
        in_specs=[SMEM, hbm, hbm],
        out_specs=[VMEM] * (3 * chunks + 2),
        out_shape=one * chunks + [pltpu.VMEM((cells, sols), BF16)] * 2,
        scratch_shapes=[
            pltpu.VMEM((slots, ROWS, cells), F32),
            pltpu.VMEM((cells, sols), F32),
            pltpu.SemaphoreType.DMA((slots,)),
            pltpu.SemaphoreType.DMA,
        ],
        compiler_params=PARAMS,
        cost_estimate=cost(chunks * rows, cells, sols, 1),
    )(blocks, *[pltpu.with_memory_space_constraint(value, pltpu.HBM) for value in (sensitivity, x)])


def rest_kernel(blocks_ref, s_ref, xh_ref, xl_ref, *outs):
    tall = outs[0].shape[0]
    for chunk in range(blocks_ref.shape[0]):
        p_ref, high_ref, low_ref = outs[3 * chunk : 3 * chunk + 3]
        for step in range(tall // ROWS):
            start = pl.multiple_of(blocks_ref[chunk] * tall + step * ROWS, ROWS)
            high, low = split(s_ref[pl.ds(start, ROWS), :])
            rows = pl.ds(step * ROWS, ROWS)
            high_ref[rows, :] = high
            low_ref[rows, :] = low
            p_ref[rows, :] = product((high, low), (xh_ref[...], xl_ref[...]))


def rest_forward(blocks, sensitivity, halves, rows):
    cells, sols = halves[0].shape
    chunks = blocks.shape[0]
    one = [
        pltpu.VMEM((rows, sols), F32),
        pltpu.VMEM((rows, cells), BF16),
        pltpu.VMEM((rows, cells), BF16),
    ]
    return pl.pallas_call(
        rest_kernel,
        in_specs=[SMEM] + [VMEM] * 3,
        out_specs=[VMEM] * (3 * chunks),
        out_shape=one * chunks,
        compiler_params=PARAMS,
        cost_estimate=cost(chunks * rows, cells, sols, 0),
    )(blocks, *pinned([sensitivity]), *pinned(halves))


def forward_kernel(terms, chunks, before, planes_ref, *refs):
    x_refs, refs = refs[:terms], refs[terms:]
    sense, refs = refs[: 2 * chunks], refs[2 * chunks :]
    starts, outs = (refs[:chunks], refs[chunks:]) if before else ((), refs)
    cells = x_refs[0].shape[0]
    xs = [split(x_ref[...]) for x_ref in x_refs]
    columns = [block_of(planes_ref[t], cells) for t in range(terms)]
    for i in range(chunks):
        total = starts[i][...] if before else None
        for t in range(terms):
            part = product((sense[2 * i][:, columns[t]], sense[2 * i + 1][:, columns[t]]), xs[t])
            total = part if total is None else total + part
        outs[i][...] = total


def forward(planes, xs, sense, before=()):
    chunks = len(sense) // 2
    rows = sense[0].shape[0]
    cells, sols = xs[0].shape
    args = [planes, *xs, *pinned(sense), *pinned(before)]
    return pl.pallas_call(
        functools.partial(forward_kernel, len(xs), chunks, len(before) > 0),
        in_specs=[SMEM] + [VMEM] * (len(args) - 1),
        out_specs=[VMEM] * chunks,
        out_shape=[pltpu.VMEM((rows, sols), F32)] * chunks,
        compiler_params=PARAMS,
        cost_estimate=cost(chunks * rows, len(xs) * cells, sols, 0),
    )(*args)


def pinned(sense):
    return [pltpu.with_memory_space_constraint(half, pltpu.VMEM) for half in sense]


def gather_kernel(chunks, before, *refs):
    w_refs, refs = refs[:chunks], refs[chunks:]
    sense, refs = refs[: 2 * chunks], refs[2 * chunks :]
    start_ref, refs = (refs[0], refs[1:]) if before else (None, refs)
    sum_ref, wh_ref, wl_ref = refs
    for i in range(chunks):
        wh_ref[i], wl_ref[i] = split(w_refs[i][...].T)

    @pl.loop(0, sum_ref.shape[1] // ROWS)
    def _(j):
        columns = block_of(j, ROWS)
        total = start_ref[:, columns] if before else None
        for i in range(chunks):
            part = product((wh_ref[i], wl_ref[i]), (sense[2 * i][:, columns], sense[2 * i + 1][:, columns]))
            total = part if total is None else total + part
        sum_ref[:, columns] = total


def gather_up(ws, sense, before=()):
    chunks = len(ws)
    rows, sols = ws[0].shape
    cells = sense[0].shape[1]
    args = [*ws, *pinned(sense), *pinned(before)]
    return pl.pallas_call(
        functools.partial(gather_kernel, chunks, len(before) > 0),
        in_specs=[VMEM] * len(args),
        out_specs=VMEM,
        out_shape=pltpu.VMEM((sols, cells), F32),
        scratch_shapes=[pltpu.VMEM((chunks, sols, rows), BF16), pltpu.VMEM((chunks, sols, rows), BF16)],
        compiler_params=PARAMS,
        cost_estimate=cost(chunks * rows, cells, sols, 0),
    )(*args)


def close_kernel(chunks, plane_ref, *refs):
    w_refs, sense, refs = refs[:chunks], refs[chunks : 3 * chunks], refs[3 * chunks :]
    start_ref, g_ref, wh_ref, wl_ref = refs
    blocks = g_ref.shape[0] // ROWS
    for i in range(chunks):
        wh_ref[i], wl_ref[i] = split(w_refs[i][...].T)

    @pl.loop(0, blocks)
    def _(j):
        columns = block_of(plane_ref[0] * blocks + j, ROWS)
        total = start_ref[:, columns]
        for i in range(chunks):
            parts = (sense[2 * i][:, columns], sense[2 * i + 1][:, columns])
            total = total + product((wh_ref[i], wl_ref[i]), parts)
        g_ref[block_of(j, ROWS), :] = total.T


def close(plane, ws, sense, before, cells):
    chunks = len(ws)
    rows, sols = ws[0].shape
    args = [plane, *ws, *pinned(sense), *pinned([before])]
    return pl.pallas_call(
        functools.partial(close_kernel, chunks),
        in_specs=[SMEM] + [VMEM] * (len(args) - 1),
        out_specs=VMEM,
        out_shape=jax.ShapeDtypeStruct((cells, sols), F32),
        scratch_shapes=[pltpu.VMEM((chunks, sols, rows), BF16), pltpu.VMEM((chunks, sols, rows), BF16)],
        compiler_params=PARAMS,
        cost_estimate=cost(chunks * rows, cells, sols, 0),
    )(*args)


def weigh_kernel(rank_ref, pieces_ref, observed_ref, copies_ref):
    misfit = jnp.sum(pieces_ref[...], axis=0) - observed_ref[...]
    weighted = misfit / jnp.maximum(jnp.abs(misfit), 1.0)
    copies_ref[...] = jnp.broadcast_to(weighted[None], copies_ref.shape)


def weigh(rank, pieces, observed):
    ranks, rows, sols = pieces.shape
    return pl.pallas_call(
        weigh_kernel,
        grid_spec=pltpu.PrefetchScalarGridSpec(
            num_scalar_prefetch=1,
            grid=(1,),
            in_specs=[
                pl.BlockSpec((ranks, rows, sols), lambda i, rank: (0, 0, 0)),
                pl.BlockSpec((rows, sols), lambda i, rank: (rank[0], 0)),
            ],
            out_specs=pl.BlockSpec((ranks, rows, sols), lambda i, rank: (0, 0, 0)),
        ),
        out_shape=jax.ShapeDtypeStruct(pieces.shape, F32),
        compiler_params=PARAMS,
    )(rank, pieces, observed)


def smooth_kernel(table_ref, own_ref, twin_ref, total_ref, parts_ref, turned_ref):
    cells, sols = own_ref.shape
    whole = own_ref[...]
    high = whole.astype(BF16)
    rest = whole - high.astype(F32)
    middle = rest.astype(BF16)
    low = (rest - middle.astype(F32)).astype(BF16)
    parts_ref[...] = jnp.concatenate([high, middle, low], axis=1)
    turned_ref[...] = table_ref[...].T
    lanes = lax.broadcasted_iota(jnp.int32, (ROWS, cells), 1).astype(F32)

    @pl.loop(0, cells // ROWS)
    def _(i):
        rows = block_of(i, ROWS)
        own = own_ref[rows, :]
        total = huber(twin_ref[rows, :] - own)
        for k in range(4):
            chosen = (lanes == turned_ref[rows, k : k + 1]).astype(F32).astype(BF16)
            taken = dot(chosen, parts_ref[...])
            other = taken[:, :sols] + taken[:, sols : 2 * sols] + taken[:, 2 * sols :]
            total = total + huber(other - own)
        total_ref[rows, :] = total


def smooth_of(table, own, twin):
    cells, sols = own.shape
    return pl.pallas_call(
        smooth_kernel,
        in_specs=[VMEM] * 3,
        out_specs=VMEM,
        out_shape=jax.ShapeDtypeStruct(own.shape, F32),
        scratch_shapes=[pltpu.VMEM((cells, 3 * sols), BF16), pltpu.VMEM((cells, table.shape[0]), F32)],
        compiler_params=PARAMS,
        cost_estimate=pl.CostEstimate(
            flops=24 * cells * cells * sols,
            bytes_accessed=16 * cells * sols,
            transcendentals=12 * cells * sols,
        ),
    )(table, own, twin)


def edge_kernel(table_ref, own_ref, beyond_ref, inner_ref, start_ref, new_ref):
    weight = table_ref[...].T[:, 4:5]
    total = inner_ref[...] + huber(beyond_ref[...] - own_ref[...])
    new_ref[...] = start_ref[...] + weight * total


def edge_of(table, own, beyond, inner, start):
    cells, sols = own.shape
    return pl.pallas_call(
        edge_kernel,
        in_specs=[VMEM] * 5,
        out_specs=VMEM,
        out_shape=jax.ShapeDtypeStruct(own.shape, F32),
        compiler_params=PARAMS,
        cost_estimate=pl.CostEstimate(
            flops=6 * cells * sols, bytes_accessed=16 * cells * sols, transcendentals=2 * cells * sols
        ),
    )(table, own, beyond, inner, start)


def place_kernel(plane_ref, value_ref, *refs):
    out_ref, sem = refs[-2:]
    rows = block_of(plane_ref[0], value_ref.shape[0])
    copy = pltpu.make_async_copy(value_ref, out_ref.at[rows], sem)
    copy.start()
    copy.wait()


def place(plane, value, before=()):
    cells, sols = value.shape
    return pl.pallas_call(
        place_kernel,
        in_specs=[SMEM, VMEM] + [ANY] * len(before),
        out_specs=ANY,
        out_shape=jax.ShapeDtypeStruct((2 * cells, sols), F32),
        scratch_shapes=[pltpu.SemaphoreType.DMA],
        input_output_aliases={2: 0} if before else {},
        compiler_params=PARAMS,
        cost_estimate=pl.CostEstimate(flops=0, bytes_accessed=8 * cells * sols, transcendentals=0),
    )(plane, value, *before)


def swap(value, axis):
    return lax.ppermute(value, axis, [(0, 1), (1, 0)])


def relay_of(own, ranks):
    half = ranks // 2
    pairs = [(ranks + half - 1, 2 * ranks - 1), (half, 0)]
    return lax.ppermute(own, ("core",) + CELLS, pairs)


def beyond_of(sent, ranks):
    half = ranks // 2
    up = [(ranks + i, i + 1) for i in range(ranks - 1) if i != half - 1]
    down = [(i + 1, ranks + i) for i in range(ranks - 1) if i != half - 1]
    cut = [(2 * ranks - 1, half), (0, ranks + half - 1)]
    return lax.ppermute(sent, ("core",) + CELLS, up + down + cut)


def ring_of(value, shift):
    yh, core, yl, x, z = (lax.axis_size(axis) for axis in ALL)
    pairs = []
    for h in range(yh):
        for l in range(yl):
            for i in range(x):
                for j in range(z):
                    at = lambda c, i, j: (((h * core + c) * yl + l) * x + i % x) * z + j % z
                    pairs.append((at(0, i, j), at(0, i, j + shift)))
                    pairs.append((at(1, i, j), at(1, i + shift, j)))
    return lax.ppermute(value, ALL, pairs)


def spread(value):
    yh, core, yl, x, z = (lax.axis_size(axis) for axis in ALL)
    at = lambda h, c, l, i, j: (((h * core + c) * yl + l) * x + i) * z + j
    groups = []
    for h in range(yh):
        groups += [[at(h, 0, l, i, j) for l in range(yl) for i in range(x)] for j in range(z)]
        groups += [[at(h, 1, l, i, j) for l in range(yl) for j in range(z)] for i in range(x)]
    return lax.all_to_all(value, ALL, 0, 0, axis_index_groups=groups, tiled=True)


def local(sensitivity, observed, models, neighbour_map, edge_mask):
    core = lax.axis_index("core").astype(jnp.int32)
    x, z = (lax.axis_index(axis).astype(jnp.int32) for axis in ("x", "z"))
    ring = jnp.where(core == 0, z, x)
    sub = lax.axis_index("yl").astype(jnp.int32) * lax.axis_size("x") + jnp.where(core == 0, x, z)
    rings = lax.axis_size("x")
    ranks = lax.axis_size(CELLS)
    subs = ranks // rings
    rank = (ring * subs + sub).reshape(1)
    block = [((ring + s) % rings).reshape(1) for s in range(rings)]
    sides = jnp.concatenate([block[1], block[3]])
    mine, theirs = core.reshape(1), (1 - core).reshape(1)
    both = jnp.concatenate([mine, theirs])
    cells = neighbour_map.shape[1]
    rows = observed.shape[0] // rings
    low_core = core == 0
    cells_rank = lax.axis_index(CELLS).astype(jnp.int32)
    carrier = cells_rank == core * (ranks - 1)
    rank, mine, theirs, both, block, sides, low_core, carrier = lax.optimization_barrier(
        (rank, mine, theirs, both, block, sides, low_core, carrier)
    )
    for step in range(ITERS):
        if step == 0:
            p2, h2, l2, *halves = first_forward(block[2], sensitivity, models, rows)
            s2 = [h2, l2]
            r2 = ring_of(p2, 2)
            p1, h1, l1, p3, h3, l3 = rest_forward(sides, sensitivity, halves, rows)
            s1, s3 = [h1, l1], [h3, l3]
            r1, r3 = ring_of(p1, 1), ring_of(p3, 3)
            p1, halves = lax.optimization_barrier((p1, halves))
            p0, *s0 = rest_forward(block[0], sensitivity, halves, rows)
            p0, start, numbers, mask = lax.optimization_barrier((p0, models, neighbour_map, edge_mask))
            own = jnp.where(low_core, start[:cells], start[cells:])
            twin = jnp.where(low_core, start[cells:], start[:cells])
            mask = jnp.where(low_core, mask[:cells], mask[cells:])
            weight = 0.05 * (1.0 - 0.75 * mask.astype(F32))
            table = jnp.concatenate(
                [numbers.astype(F32), weight[None], jnp.zeros((3, cells), F32)], axis=0
            )
        else:
            p2, p1, p3 = forward(mine, [own], s2 + s1 + s3)
            twin = swap(own, "core")
            (p2,) = forward(theirs, [twin], s2, [p2])
            r2 = ring_of(p2, 2)
            p1, p3 = forward(theirs, [twin], s1 + s3, [p1, p3])
            r1, r3 = ring_of(p1, 1), ring_of(p3, 3)
            (p0,) = forward(both, [own, twin], s0)
        p0, r1, r3 = lax.optimization_barrier((p0 + r2, r1, r3))
        p0, own, twin, table = lax.optimization_barrier((p0 + (r1 + r3), own, twin, table))
        pieces = spread(p0)
        copies = weigh(rank, pieces.reshape(subs, rows // subs, -1), observed)
        w0 = spread(copies.reshape(rows, -1))
        w0, sent = lax.optimization_barrier((w0, own))
        relay = relay_of(sent, ranks)
        w2, w3, w1 = ring_of(w0, 2), ring_of(w0, 1), ring_of(w0, 3)
        near = gather_up([w0], s0)
        near = gather_up([w3], s3, [near])
        near, relay = lax.optimization_barrier((near, relay))
        sent = jnp.where(carrier, relay, own)
        away = close(theirs, [w1, w2], s1 + s2, near, cells)
        home = close(mine, [w1, w2], s1 + s2, near, cells)
        half = home + swap(away, "core")
        half, own, twin, sent = lax.optimization_barrier((half, own, twin, sent))
        beyond = beyond_of(sent, ranks)
        gradient = half + swap(half, "yh")
        inner = smooth_of(table, own, twin)
        own = edge_of(table, own, beyond, inner, own - 1.0 * gradient)
    twin = swap(own, "core")
    return place(theirs, twin, [place(mine, own)])


def solution(mesh):
    fine = Mesh(mesh.devices.reshape(2, 2, 2, 4, 4), ALL)
    return jax.shard_map(
        local,
        mesh=fine,
        in_specs=(P(DATA, CELLS), P(DATA, None), P(CELLS, None), P(), P(CELLS)),
        out_specs=P(CELLS, None),
        check_vma=False,
    )
```

```python
import functools

import jax
import jax.numpy as jnp
from jax import lax
from jax.experimental import pallas as pl
from jax.experimental.pallas import tpu as pltpu
from jax.sharding import Mesh, PartitionSpec as P

ITERS = 2
DATA = ("yh", "core")
CELLS = ("yl", "x", "z")
ALL = DATA + CELLS
ROWS = 256
PARTS = 4
PARAMS = pltpu.CompilerParams(vmem_limit_bytes=24 * 1024 * 1024)
VMEM = pl.BlockSpec(memory_space=pltpu.VMEM)
SMEM = pl.BlockSpec(memory_space=pltpu.SMEM)
ANY = pl.BlockSpec(memory_space=pl.ANY)
F32 = jnp.float32
BF16 = jnp.bfloat16


def huber(diff):
    return diff / jnp.sqrt(1.0 + diff * diff)


def split(value):
    high = value.astype(BF16)
    low = (value - high.astype(F32)).astype(BF16)
    return high, low


def dot(a, b):
    return jnp.dot(a, b, preferred_element_type=F32)


def product(a, b):
    return dot(a[0], b[0]) + (dot(a[0], b[1]) + dot(a[1], b[0]))


def block_of(index, size):
    return pl.ds(pl.multiple_of(index * size, size), size)


def cost(data, cells, sols, wide):
    return pl.CostEstimate(
        flops=6 * data * cells * sols,
        bytes_accessed=4 * (wide * data * cells + cells * sols + data * sols),
        transcendentals=0,
    )


def first_kernel(blocks_ref, s_ref, x_ref, *refs):
    chunks = blocks_ref.shape[0]
    outs, refs = refs[: 3 * chunks], refs[3 * chunks :]
    xh_ref, xl_ref, in_ref, x_in_ref, in_sem, x_sem = refs
    steps = outs[0].shape[0] // ROWS

    def fetch(chunk, step):
        start = pl.multiple_of((blocks_ref[chunk] * steps + step) * ROWS, ROWS)
        slot = chunk * steps + step
        return pltpu.make_async_copy(s_ref.at[pl.ds(start, ROWS)], in_ref.at[slot], in_sem.at[slot])

    order = [(chunk, step) for chunk in range(chunks) for step in range(steps)]
    take = pltpu.make_async_copy(x_ref, x_in_ref, x_sem)
    take.start()
    for chunk, step in order:
        fetch(chunk, step).start()
    take.wait()
    xh_ref[...], xl_ref[...] = split(x_in_ref[...])
    for chunk, step in order:
        p_ref, high_ref, low_ref = outs[3 * chunk : 3 * chunk + 3]
        fetch(chunk, step).wait()
        high, low = split(in_ref[chunk * steps + step])
        rows = pl.ds(step * ROWS, ROWS)
        high_ref[rows, :] = high
        low_ref[rows, :] = low
        p_ref[rows, :] = product((high, low), (xh_ref[...], xl_ref[...]))


def first_forward(blocks, sensitivity, x, rows):
    cells, sols = x.shape
    chunks = blocks.shape[0]
    slots = chunks * rows // ROWS
    hbm = pl.BlockSpec(memory_space=pltpu.HBM)
    one = [
        pltpu.VMEM((rows, sols), F32),
        pltpu.VMEM((rows, cells), BF16),
        pltpu.VMEM((rows, cells), BF16),
    ]
    return pl.pallas_call(
        first_kernel,
        in_specs=[SMEM, hbm, hbm],
        out_specs=[VMEM] * (3 * chunks + 2),
        out_shape=one * chunks + [pltpu.VMEM((cells, sols), BF16)] * 2,
        scratch_shapes=[
            pltpu.VMEM((slots, ROWS, cells), F32),
            pltpu.VMEM((cells, sols), F32),
            pltpu.SemaphoreType.DMA((slots,)),
            pltpu.SemaphoreType.DMA,
        ],
        compiler_params=PARAMS,
        cost_estimate=cost(chunks * rows, cells, sols, 1),
    )(blocks, *[pltpu.with_memory_space_constraint(value, pltpu.HBM) for value in (sensitivity, x)])


def rest_kernel(blocks_ref, s_ref, xh_ref, xl_ref, *outs):
    tall = outs[0].shape[0]
    for chunk in range(blocks_ref.shape[0]):
        p_ref, high_ref, low_ref = outs[3 * chunk : 3 * chunk + 3]
        for step in range(tall // ROWS):
            start = pl.multiple_of(blocks_ref[chunk] * tall + step * ROWS, ROWS)
            high, low = split(s_ref[pl.ds(start, ROWS), :])
            rows = pl.ds(step * ROWS, ROWS)
            high_ref[rows, :] = high
            low_ref[rows, :] = low
            p_ref[rows, :] = product((high, low), (xh_ref[...], xl_ref[...]))


def rest_forward(blocks, sensitivity, halves, rows):
    cells, sols = halves[0].shape
    chunks = blocks.shape[0]
    one = [
        pltpu.VMEM((rows, sols), F32),
        pltpu.VMEM((rows, cells), BF16),
        pltpu.VMEM((rows, cells), BF16),
    ]
    return pl.pallas_call(
        rest_kernel,
        in_specs=[SMEM] + [VMEM] * 3,
        out_specs=[VMEM] * (3 * chunks),
        out_shape=one * chunks,
        compiler_params=PARAMS,
        cost_estimate=cost(chunks * rows, cells, sols, 0),
    )(blocks, *pinned([sensitivity]), *pinned(halves))


def forward_kernel(terms, chunks, before, planes_ref, *refs):
    x_refs, refs = refs[:terms], refs[terms:]
    sense, refs = refs[: 2 * chunks], refs[2 * chunks :]
    starts, outs = (refs[:chunks], refs[chunks:]) if before else ((), refs)
    cells = x_refs[0].shape[0]
    xs = [split(x_ref[...]) for x_ref in x_refs]
    columns = [block_of(planes_ref[t], cells) for t in range(terms)]
    for i in range(chunks):
        total = starts[i][...] if before else None
        for t in range(terms):
            part = product((sense[2 * i][:, columns[t]], sense[2 * i + 1][:, columns[t]]), xs[t])
            total = part if total is None else total + part
        outs[i][...] = total


def forward(planes, xs, sense, before=()):
    chunks = len(sense) // 2
    rows = sense[0].shape[0]
    cells, sols = xs[0].shape
    args = [planes, *xs, *pinned(sense), *pinned(before)]
    return pl.pallas_call(
        functools.partial(forward_kernel, len(xs), chunks, len(before) > 0),
        in_specs=[SMEM] + [VMEM] * (len(args) - 1),
        out_specs=[VMEM] * chunks,
        out_shape=[pltpu.VMEM((rows, sols), F32)] * chunks,
        compiler_params=PARAMS,
        cost_estimate=cost(chunks * rows, len(xs) * cells, sols, 0),
    )(*args)


def pinned(sense):
    return [pltpu.with_memory_space_constraint(half, pltpu.VMEM) for half in sense]


def gather_kernel(chunks, before, *refs):
    w_refs, refs = refs[:chunks], refs[chunks:]
    sense, refs = refs[: 2 * chunks], refs[2 * chunks :]
    start_ref, refs = (refs[0], refs[1:]) if before else (None, refs)
    sum_ref, wh_ref, wl_ref = refs
    for i in range(chunks):
        wh_ref[i], wl_ref[i] = split(w_refs[i][...].T)

    @pl.loop(0, sum_ref.shape[1] // ROWS)
    def _(j):
        columns = block_of(j, ROWS)
        total = start_ref[:, columns] if before else None
        for i in range(chunks):
            part = product((wh_ref[i], wl_ref[i]), (sense[2 * i][:, columns], sense[2 * i + 1][:, columns]))
            total = part if total is None else total + part
        sum_ref[:, columns] = total


def gather_up(ws, sense, before=()):
    chunks = len(ws)
    rows, sols = ws[0].shape
    cells = sense[0].shape[1]
    args = [*ws, *pinned(sense), *pinned(before)]
    return pl.pallas_call(
        functools.partial(gather_kernel, chunks, len(before) > 0),
        in_specs=[VMEM] * len(args),
        out_specs=VMEM,
        out_shape=pltpu.VMEM((sols, cells), F32),
        scratch_shapes=[pltpu.VMEM((chunks, sols, rows), BF16), pltpu.VMEM((chunks, sols, rows), BF16)],
        compiler_params=PARAMS,
        cost_estimate=cost(chunks * rows, cells, sols, 0),
    )(*args)


def home_kernel(chunks, plane_ref, wh_ref, wl_ref, *refs):
    sense, (start_ref, g_ref) = refs[: 2 * chunks], refs[2 * chunks :]
    blocks = g_ref.shape[0] // ROWS

    @pl.loop(0, blocks)
    def _(j):
        columns = block_of(plane_ref[0] * blocks + j, ROWS)
        total = start_ref[:, columns]
        for i in range(chunks):
            parts = (sense[2 * i][:, columns], sense[2 * i + 1][:, columns])
            total = total + product((wh_ref[i], wl_ref[i]), parts)
        g_ref[block_of(j, ROWS), :] = total.T


def away_kernel(chunks, plane_ref, *refs):
    w_refs, refs = refs[:chunks], refs[chunks:]
    inputs, (g_ref, wh_ref, wl_ref) = refs[:-3], refs[-3:]
    for i in range(chunks):
        wh_ref[i], wl_ref[i] = split(w_refs[i][...].T)
    home_kernel(chunks, plane_ref, wh_ref, wl_ref, *inputs, g_ref)


def close(theirs, mine, ws, sense, before, cells):
    chunks = len(ws)
    rows, sols = ws[0].shape
    held = [*pinned(sense), *pinned([before])]
    gradient = jax.ShapeDtypeStruct((cells, sols), F32)
    half = pltpu.VMEM((chunks, sols, rows), BF16)
    work = cost(chunks * rows, cells, sols, 0)
    away, high, low = pl.pallas_call(
        functools.partial(away_kernel, chunks),
        in_specs=[SMEM] + [VMEM] * (chunks + len(held)),
        out_specs=[VMEM] * 3,
        out_shape=[gradient, half, half],
        compiler_params=PARAMS,
        cost_estimate=work,
    )(theirs, *ws, *held)
    home = pl.pallas_call(
        functools.partial(home_kernel, chunks),
        in_specs=[SMEM] + [VMEM] * (2 + len(held)),
        out_specs=VMEM,
        out_shape=gradient,
        compiler_params=PARAMS,
        cost_estimate=work,
    )(mine, *pinned([high, low]), *held)
    return away, home


def weigh_kernel(rank_ref, pieces_ref, observed_ref, copies_ref):
    misfit = jnp.sum(pieces_ref[...], axis=0) - observed_ref[...]
    weighted = misfit / jnp.maximum(jnp.abs(misfit), 1.0)
    copies_ref[...] = jnp.broadcast_to(weighted[None], copies_ref.shape)


def weigh(rank, pieces, observed):
    ranks, rows, sols = pieces.shape
    return pl.pallas_call(
        weigh_kernel,
        grid_spec=pltpu.PrefetchScalarGridSpec(
            num_scalar_prefetch=1,
            grid=(1,),
            in_specs=[
                pl.BlockSpec((ranks, rows, sols), lambda i, rank: (0, 0, 0)),
                pl.BlockSpec((rows, sols), lambda i, rank: (rank[0], 0)),
            ],
            out_specs=pl.BlockSpec((ranks, rows, sols), lambda i, rank: (0, 0, 0)),
        ),
        out_shape=jax.ShapeDtypeStruct(pieces.shape, F32),
        compiler_params=PARAMS,
    )(rank, pieces, observed)


def smooth_kernel(table_ref, own_ref, twin_ref, total_ref, parts_ref, turned_ref):
    cells, sols = own_ref.shape
    whole = own_ref[...]
    high = whole.astype(BF16)
    rest = whole - high.astype(F32)
    middle = rest.astype(BF16)
    low = (rest - middle.astype(F32)).astype(BF16)
    parts_ref[...] = jnp.concatenate([high, middle, low], axis=1)
    turned_ref[...] = table_ref[...].T
    lanes = lax.broadcasted_iota(jnp.int32, (ROWS, cells), 1).astype(F32)

    @pl.loop(0, cells // ROWS)
    def _(i):
        rows = block_of(i, ROWS)
        own = own_ref[rows, :]
        total = huber(twin_ref[rows, :] - own)
        for k in range(4):
            chosen = (lanes == turned_ref[rows, k : k + 1]).astype(F32).astype(BF16)
            taken = dot(chosen, parts_ref[...])
            other = taken[:, :sols] + taken[:, sols : 2 * sols] + taken[:, 2 * sols :]
            total = total + huber(other - own)
        total_ref[rows, :] = total


def smooth_of(table, own, twin):
    cells, sols = own.shape
    return pl.pallas_call(
        smooth_kernel,
        in_specs=[VMEM] * 3,
        out_specs=VMEM,
        out_shape=jax.ShapeDtypeStruct(own.shape, F32),
        scratch_shapes=[pltpu.VMEM((cells, 3 * sols), BF16), pltpu.VMEM((cells, table.shape[0]), F32)],
        compiler_params=PARAMS,
        cost_estimate=pl.CostEstimate(
            flops=24 * cells * cells * sols,
            bytes_accessed=16 * cells * sols,
            transcendentals=12 * cells * sols,
        ),
    )(table, own, twin)


def edge_kernel(table_ref, own_ref, beyond_ref, inner_ref, start_ref, new_ref):
    weight = table_ref[...].T[:, 4:5]
    total = inner_ref[...] + huber(beyond_ref[...] - own_ref[...])
    new_ref[...] = start_ref[...] + weight * total


def edge_of(table, own, beyond, inner, start):
    cells, sols = own.shape
    return pl.pallas_call(
        edge_kernel,
        in_specs=[VMEM] * 5,
        out_specs=VMEM,
        out_shape=jax.ShapeDtypeStruct(own.shape, F32),
        compiler_params=PARAMS,
        cost_estimate=pl.CostEstimate(
            flops=6 * cells * sols, bytes_accessed=16 * cells * sols, transcendentals=2 * cells * sols
        ),
    )(table, own, beyond, inner, start)


def place_kernel(plane_ref, value_ref, *refs):
    out_ref, sem = refs[-2:]
    tall = value_ref.shape[0] // PARTS
    copies = []
    for i in range(PARTS):
        rows = block_of(plane_ref[0] * PARTS + i, tall)
        source = value_ref.at[pl.ds(i * tall, tall)]
        copies.append(pltpu.make_async_copy(source, out_ref.at[rows], sem.at[i]))
        copies[-1].start()
    for copy in copies:
        copy.wait()


def place(plane, value, before=()):
    cells, sols = value.shape
    return pl.pallas_call(
        place_kernel,
        in_specs=[SMEM, VMEM] + [ANY] * len(before),
        out_specs=ANY,
        out_shape=jax.ShapeDtypeStruct((2 * cells, sols), F32),
        scratch_shapes=[pltpu.SemaphoreType.DMA((PARTS,))],
        input_output_aliases={2: 0} if before else {},
        compiler_params=PARAMS,
        cost_estimate=pl.CostEstimate(flops=0, bytes_accessed=8 * cells * sols, transcendentals=0),
    )(plane, value, *before)


def swap(value, axis):
    return lax.ppermute(value, axis, [(0, 1), (1, 0)])


def relay_of(own, ranks):
    half = ranks // 2
    pairs = [(ranks + half - 1, 2 * ranks - 1), (half, 0)]
    return lax.ppermute(own, ("core",) + CELLS, pairs)


def beyond_of(sent, ranks):
    half = ranks // 2
    up = [(ranks + i, i + 1) for i in range(ranks - 1) if i != half - 1]
    down = [(i + 1, ranks + i) for i in range(ranks - 1) if i != half - 1]
    cut = [(2 * ranks - 1, half), (0, ranks + half - 1)]
    return lax.ppermute(sent, ("core",) + CELLS, up + down + cut)


def ring_of(value, shift):
    yh, core, yl, x, z = (lax.axis_size(axis) for axis in ALL)
    pairs = []
    for h in range(yh):
        for l in range(yl):
            for i in range(x):
                for j in range(z):
                    at = lambda c, i, j: (((h * core + c) * yl + l) * x + i % x) * z + j % z
                    pairs.append((at(0, i, j), at(0, i, j + shift)))
                    pairs.append((at(1, i, j), at(1, i + shift, j)))
    return lax.ppermute(value, ALL, pairs)


def spread(value):
    yh, core, yl, x, z = (lax.axis_size(axis) for axis in ALL)
    at = lambda h, c, l, i, j: (((h * core + c) * yl + l) * x + i) * z + j
    groups = []
    for h in range(yh):
        groups += [[at(h, 0, l, i, j) for l in range(yl) for i in range(x)] for j in range(z)]
        groups += [[at(h, 1, l, i, j) for l in range(yl) for j in range(z)] for i in range(x)]
    return lax.all_to_all(value, ALL, 0, 0, axis_index_groups=groups, tiled=True)


def local(sensitivity, observed, models, neighbour_map, edge_mask):
    core = lax.axis_index("core").astype(jnp.int32)
    x, z = (lax.axis_index(axis).astype(jnp.int32) for axis in ("x", "z"))
    ring = jnp.where(core == 0, z, x)
    sub = lax.axis_index("yl").astype(jnp.int32) * lax.axis_size("x") + jnp.where(core == 0, x, z)
    rings = lax.axis_size("x")
    ranks = lax.axis_size(CELLS)
    subs = ranks // rings
    rank = (ring * subs + sub).reshape(1)
    block = [((ring + s) % rings).reshape(1) for s in range(rings)]
    sides = jnp.concatenate([block[1], block[3]])
    mine, theirs = core.reshape(1), (1 - core).reshape(1)
    both = jnp.concatenate([mine, theirs])
    cells = neighbour_map.shape[1]
    rows = observed.shape[0] // rings
    low_core = core == 0
    cells_rank = lax.axis_index(CELLS).astype(jnp.int32)
    carrier = cells_rank == core * (ranks - 1)
    rank, mine, theirs, both, block, sides, low_core, carrier = lax.optimization_barrier(
        (rank, mine, theirs, both, block, sides, low_core, carrier)
    )
    for step in range(ITERS):
        if step == 0:
            p2, h2, l2, *halves = first_forward(block[2], sensitivity, models, rows)
            s2 = [h2, l2]
            r2 = ring_of(p2, 2)
            p1, h1, l1, p3, h3, l3 = rest_forward(sides, sensitivity, halves, rows)
            s1, s3 = [h1, l1], [h3, l3]
            r1, r3 = ring_of(p1, 1), ring_of(p3, 3)
            p1, halves = lax.optimization_barrier((p1, halves))
            p0, *s0 = rest_forward(block[0], sensitivity, halves, rows)
            p0, start, numbers, mask = lax.optimization_barrier((p0, models, neighbour_map, edge_mask))
            own = jnp.where(low_core, start[:cells], start[cells:])
            twin = jnp.where(low_core, start[cells:], start[:cells])
            mask = jnp.where(low_core, mask[:cells], mask[cells:])
            weight = 0.05 * (1.0 - 0.75 * mask.astype(F32))
            table = jnp.concatenate(
                [numbers.astype(F32), weight[None], jnp.zeros((3, cells), F32)], axis=0
            )
        else:
            p2, p1, p3 = forward(mine, [own], s2 + s1 + s3)
            twin = swap(own, "core")
            (p2,) = forward(theirs, [twin], s2, [p2])
            r2 = ring_of(p2, 2)
            p1, p3 = forward(theirs, [twin], s1 + s3, [p1, p3])
            r1, r3 = ring_of(p1, 1), ring_of(p3, 3)
            (p0,) = forward(both, [own, twin], s0)
        p0, r1, r3 = lax.optimization_barrier((p0 + r2, r1, r3))
        p0, own, twin, table = lax.optimization_barrier((p0 + (r1 + r3), own, twin, table))
        pieces = spread(p0)
        copies = weigh(rank, pieces.reshape(subs, rows // subs, -1), observed)
        w0 = spread(copies.reshape(rows, -1))
        w0, sent = lax.optimization_barrier((w0, own))
        relay = relay_of(sent, ranks)
        w2, w3, w1 = ring_of(w0, 2), ring_of(w0, 1), ring_of(w0, 3)
        near = gather_up([w0], s0)
        near = gather_up([w3], s3, [near])
        near, relay = lax.optimization_barrier((near, relay))
        sent = jnp.where(carrier, relay, own)
        away, home = close(theirs, mine, [w1, w2], s1 + s2, near, cells)
        half = home + swap(away, "core")
        half, own, twin, sent = lax.optimization_barrier((half, own, twin, sent))
        beyond = beyond_of(sent, ranks)
        gradient = half + swap(half, "yh")
        inner = smooth_of(table, own, twin)
        own = edge_of(table, own, beyond, inner, own - 1.0 * gradient)
    twin = swap(own, "core")
    return place(theirs, twin, [place(mine, own)])


def solution(mesh):
    fine = Mesh(mesh.devices.reshape(2, 2, 2, 4, 4), ALL)
    return jax.shard_map(
        local,
        mesh=fine,
        in_specs=(P(DATA, CELLS), P(DATA, None), P(CELLS, None), P(), P(CELLS)),
        out_specs=P(CELLS, None),
        check_vma=False,
    )
```

```python
import functools

import jax
import jax.numpy as jnp
from jax import lax
from jax.experimental import pallas as pl
from jax.experimental.pallas import tpu as pltpu
from jax.sharding import Mesh, PartitionSpec as P

ITERS = 2
DATA = ("yh", "core")
CELLS = ("yl", "x", "z")
ALL = DATA + CELLS
ROWS = 256
PARTS = 4
PARAMS = pltpu.CompilerParams(vmem_limit_bytes=24 * 1024 * 1024)
VMEM = pl.BlockSpec(memory_space=pltpu.VMEM)
SMEM = pl.BlockSpec(memory_space=pltpu.SMEM)
ANY = pl.BlockSpec(memory_space=pl.ANY)
F32 = jnp.float32
BF16 = jnp.bfloat16


def huber(diff):
    return diff / jnp.sqrt(1.0 + diff * diff)


def split(value):
    high = value.astype(BF16)
    low = (value - high.astype(F32)).astype(BF16)
    return high, low


def dot(a, b):
    return jnp.dot(a, b, preferred_element_type=F32)


def product(a, b):
    return dot(a[0], b[0]) + (dot(a[0], b[1]) + dot(a[1], b[0]))


def block_of(index, size):
    return pl.ds(pl.multiple_of(index * size, size), size)


def cost(data, cells, sols, wide):
    return pl.CostEstimate(
        flops=6 * data * cells * sols,
        bytes_accessed=4 * (wide * data * cells + cells * sols + data * sols),
        transcendentals=0,
    )


def first_kernel(blocks_ref, s_ref, x_ref, *refs):
    chunks = blocks_ref.shape[0]
    outs, refs = refs[: 3 * chunks], refs[3 * chunks :]
    xh_ref, xl_ref, in_ref, x_in_ref, in_sem, x_sem = refs
    steps = outs[0].shape[0] // ROWS

    def fetch(chunk, step):
        start = pl.multiple_of((blocks_ref[chunk] * steps + step) * ROWS, ROWS)
        slot = chunk * steps + step
        return pltpu.make_async_copy(s_ref.at[pl.ds(start, ROWS)], in_ref.at[slot], in_sem.at[slot])

    order = [(chunk, step) for chunk in range(chunks) for step in range(steps)]
    take = pltpu.make_async_copy(x_ref, x_in_ref, x_sem)
    take.start()
    for chunk, step in order:
        fetch(chunk, step).start()
    take.wait()
    xh_ref[...], xl_ref[...] = split(x_in_ref[...])
    for chunk, step in order:
        p_ref, high_ref, low_ref = outs[3 * chunk : 3 * chunk + 3]
        fetch(chunk, step).wait()
        high, low = split(in_ref[chunk * steps + step])
        rows = pl.ds(step * ROWS, ROWS)
        high_ref[rows, :] = high
        low_ref[rows, :] = low
        p_ref[rows, :] = product((high, low), (xh_ref[...], xl_ref[...]))


def first_forward(blocks, sensitivity, x, rows):
    cells, sols = x.shape
    chunks = blocks.shape[0]
    slots = chunks * rows // ROWS
    hbm = pl.BlockSpec(memory_space=pltpu.HBM)
    one = [
        pltpu.VMEM((rows, sols), F32),
        pltpu.VMEM((rows, cells), BF16),
        pltpu.VMEM((rows, cells), BF16),
    ]
    return pl.pallas_call(
        first_kernel,
        in_specs=[SMEM, hbm, hbm],
        out_specs=[VMEM] * (3 * chunks + 2),
        out_shape=one * chunks + [pltpu.VMEM((cells, sols), BF16)] * 2,
        scratch_shapes=[
            pltpu.VMEM((slots, ROWS, cells), F32),
            pltpu.VMEM((cells, sols), F32),
            pltpu.SemaphoreType.DMA((slots,)),
            pltpu.SemaphoreType.DMA,
        ],
        compiler_params=PARAMS,
        cost_estimate=cost(chunks * rows, cells, sols, 1),
    )(blocks, *[pltpu.with_memory_space_constraint(value, pltpu.HBM) for value in (sensitivity, x)])


def rest_kernel(blocks_ref, s_ref, xh_ref, xl_ref, *outs):
    tall = outs[0].shape[0]
    for chunk in range(blocks_ref.shape[0]):
        p_ref, high_ref, low_ref = outs[3 * chunk : 3 * chunk + 3]
        for step in range(tall // ROWS):
            start = pl.multiple_of(blocks_ref[chunk] * tall + step * ROWS, ROWS)
            high, low = split(s_ref[pl.ds(start, ROWS), :])
            rows = pl.ds(step * ROWS, ROWS)
            high_ref[rows, :] = high
            low_ref[rows, :] = low
            p_ref[rows, :] = product((high, low), (xh_ref[...], xl_ref[...]))


def rest_forward(blocks, sensitivity, halves, rows):
    cells, sols = halves[0].shape
    chunks = blocks.shape[0]
    one = [
        pltpu.VMEM((rows, sols), F32),
        pltpu.VMEM((rows, cells), BF16),
        pltpu.VMEM((rows, cells), BF16),
    ]
    return pl.pallas_call(
        rest_kernel,
        in_specs=[SMEM] + [VMEM] * 3,
        out_specs=[VMEM] * (3 * chunks),
        out_shape=one * chunks,
        compiler_params=PARAMS,
        cost_estimate=cost(chunks * rows, cells, sols, 0),
    )(blocks, *pinned([sensitivity]), *pinned(halves))


def forward_kernel(terms, chunks, before, planes_ref, *refs):
    x_refs, refs = refs[:terms], refs[terms:]
    sense, refs = refs[: 2 * chunks], refs[2 * chunks :]
    starts, outs = (refs[:chunks], refs[chunks:]) if before else ((), refs)
    cells = x_refs[0].shape[0]
    xs = [split(x_ref[...]) for x_ref in x_refs]
    columns = [block_of(planes_ref[t], cells) for t in range(terms)]
    for i in range(chunks):
        total = starts[i][...] if before else None
        for t in range(terms):
            part = product((sense[2 * i][:, columns[t]], sense[2 * i + 1][:, columns[t]]), xs[t])
            total = part if total is None else total + part
        outs[i][...] = total


def forward(planes, xs, sense, before=()):
    chunks = len(sense) // 2
    rows = sense[0].shape[0]
    cells, sols = xs[0].shape
    args = [planes, *xs, *pinned(sense), *pinned(before)]
    return pl.pallas_call(
        functools.partial(forward_kernel, len(xs), chunks, len(before) > 0),
        in_specs=[SMEM] + [VMEM] * (len(args) - 1),
        out_specs=[VMEM] * chunks,
        out_shape=[pltpu.VMEM((rows, sols), F32)] * chunks,
        compiler_params=PARAMS,
        cost_estimate=cost(chunks * rows, len(xs) * cells, sols, 0),
    )(*args)


def pinned(sense):
    return [pltpu.with_memory_space_constraint(half, pltpu.VMEM) for half in sense]


def gather_kernel(chunks, before, *refs):
    w_refs, refs = refs[:chunks], refs[chunks:]
    sense, refs = refs[: 2 * chunks], refs[2 * chunks :]
    start_ref, refs = (refs[0], refs[1:]) if before else (None, refs)
    sum_ref, wh_ref, wl_ref = refs
    for i in range(chunks):
        wh_ref[i], wl_ref[i] = split(w_refs[i][...].T)

    @pl.loop(0, sum_ref.shape[1] // ROWS)
    def _(j):
        columns = block_of(j, ROWS)
        total = start_ref[:, columns] if before else None
        for i in range(chunks):
            part = product((wh_ref[i], wl_ref[i]), (sense[2 * i][:, columns], sense[2 * i + 1][:, columns]))
            total = part if total is None else total + part
        sum_ref[:, columns] = total


def gather_up(ws, sense, before=()):
    chunks = len(ws)
    rows, sols = ws[0].shape
    cells = sense[0].shape[1]
    args = [*ws, *pinned(sense), *pinned(before)]
    return pl.pallas_call(
        functools.partial(gather_kernel, chunks, len(before) > 0),
        in_specs=[VMEM] * len(args),
        out_specs=VMEM,
        out_shape=pltpu.VMEM((sols, cells), F32),
        scratch_shapes=[pltpu.VMEM((chunks, sols, rows), BF16), pltpu.VMEM((chunks, sols, rows), BF16)],
        compiler_params=PARAMS,
        cost_estimate=cost(chunks * rows, cells, sols, 0),
    )(*args)


def home_kernel(chunks, plane_ref, wh_ref, wl_ref, *refs):
    sense, (start_ref, g_ref) = refs[: 2 * chunks], refs[2 * chunks :]
    blocks = g_ref.shape[0] // ROWS

    @pl.loop(0, blocks)
    def _(j):
        columns = block_of(plane_ref[0] * blocks + j, ROWS)
        total = start_ref[:, columns]
        for i in range(chunks):
            parts = (sense[2 * i][:, columns], sense[2 * i + 1][:, columns])
            total = total + product((wh_ref[i], wl_ref[i]), parts)
        g_ref[block_of(j, ROWS), :] = total.T


def away_kernel(chunks, plane_ref, *refs):
    w_refs, refs = refs[:chunks], refs[chunks:]
    inputs, (g_ref, wh_ref, wl_ref) = refs[:-3], refs[-3:]
    for i in range(chunks):
        wh_ref[i], wl_ref[i] = split(w_refs[i][...].T)
    home_kernel(chunks, plane_ref, wh_ref, wl_ref, *inputs, g_ref)


def close(theirs, mine, ws, sense, before, cells):
    chunks = len(ws)
    rows, sols = ws[0].shape
    held = [*pinned(sense), *pinned([before])]
    gradient = jax.ShapeDtypeStruct((cells, sols), F32)
    half = pltpu.VMEM((chunks, sols, rows), BF16)
    work = cost(chunks * rows, cells, sols, 0)
    away, high, low = pl.pallas_call(
        functools.partial(away_kernel, chunks),
        in_specs=[SMEM] + [VMEM] * (chunks + len(held)),
        out_specs=[VMEM] * 3,
        out_shape=[gradient, half, half],
        compiler_params=PARAMS,
        cost_estimate=work,
    )(theirs, *ws, *held)
    home = pl.pallas_call(
        functools.partial(home_kernel, chunks),
        in_specs=[SMEM] + [VMEM] * (2 + len(held)),
        out_specs=VMEM,
        out_shape=gradient,
        compiler_params=PARAMS,
        cost_estimate=work,
    )(mine, *pinned([high, low]), *held)
    return away, home


def weigh_kernel(rank_ref, pieces_ref, observed_ref, copies_ref):
    misfit = jnp.sum(pieces_ref[...], axis=0) - observed_ref[...]
    weighted = misfit / jnp.maximum(jnp.abs(misfit), 1.0)
    copies_ref[...] = jnp.broadcast_to(weighted[None], copies_ref.shape)


def weigh(rank, pieces, observed):
    ranks, rows, sols = pieces.shape
    return pl.pallas_call(
        weigh_kernel,
        grid_spec=pltpu.PrefetchScalarGridSpec(
            num_scalar_prefetch=1,
            grid=(1,),
            in_specs=[
                pl.BlockSpec((ranks, rows, sols), lambda i, rank: (0, 0, 0)),
                pl.BlockSpec((rows, sols), lambda i, rank: (rank[0], 0)),
            ],
            out_specs=pl.BlockSpec((ranks, rows, sols), lambda i, rank: (0, 0, 0)),
        ),
        out_shape=jax.ShapeDtypeStruct(pieces.shape, F32),
        compiler_params=PARAMS,
    )(rank, pieces, observed)


def smooth_kernel(table_ref, own_ref, twin_ref, total_ref, parts_ref, turned_ref):
    cells, sols = own_ref.shape
    whole = own_ref[...]
    high = whole.astype(BF16)
    rest = whole - high.astype(F32)
    middle = rest.astype(BF16)
    low = (rest - middle.astype(F32)).astype(BF16)
    parts_ref[...] = jnp.concatenate([high, middle, low], axis=1)
    turned_ref[...] = table_ref[...].T
    lanes = lax.broadcasted_iota(jnp.int32, (ROWS, cells), 1).astype(F32)

    @pl.loop(0, cells // ROWS)
    def _(i):
        rows = block_of(i, ROWS)
        own = own_ref[rows, :]
        total = huber(twin_ref[rows, :] - own)
        for k in range(4):
            chosen = (lanes == turned_ref[rows, k : k + 1]).astype(F32).astype(BF16)
            taken = dot(chosen, parts_ref[...])
            other = taken[:, :sols] + taken[:, sols : 2 * sols] + taken[:, 2 * sols :]
            total = total + huber(other - own)
        total_ref[rows, :] = total


def smooth_of(table, own, twin):
    cells, sols = own.shape
    return pl.pallas_call(
        smooth_kernel,
        in_specs=[VMEM] * 3,
        out_specs=VMEM,
        out_shape=jax.ShapeDtypeStruct(own.shape, F32),
        scratch_shapes=[pltpu.VMEM((cells, 3 * sols), BF16), pltpu.VMEM((cells, table.shape[0]), F32)],
        compiler_params=PARAMS,
        cost_estimate=pl.CostEstimate(
            flops=24 * cells * cells * sols,
            bytes_accessed=16 * cells * sols,
            transcendentals=12 * cells * sols,
        ),
    )(table, own, twin)


def edge_kernel(table_ref, own_ref, beyond_ref, inner_ref, start_ref, new_ref):
    weight = table_ref[...].T[:, 4:5]
    total = inner_ref[...] + huber(beyond_ref[...] - own_ref[...])
    new_ref[...] = start_ref[...] + weight * total


def edge_of(table, own, beyond, inner, start):
    cells, sols = own.shape
    return pl.pallas_call(
        edge_kernel,
        in_specs=[VMEM] * 5,
        out_specs=VMEM,
        out_shape=jax.ShapeDtypeStruct(own.shape, F32),
        compiler_params=PARAMS,
        cost_estimate=pl.CostEstimate(
            flops=6 * cells * sols, bytes_accessed=16 * cells * sols, transcendentals=2 * cells * sols
        ),
    )(table, own, beyond, inner, start)


def place_kernel(plane_ref, value_ref, *refs):
    out_ref, sem = refs[-2:]
    tall = value_ref.shape[0] // PARTS
    copies = []
    for i in range(PARTS):
        rows = block_of(plane_ref[0] * PARTS + i, tall)
        source = value_ref.at[pl.ds(i * tall, tall)]
        copies.append(pltpu.make_async_copy(source, out_ref.at[rows], sem.at[i]))
        copies[-1].start()
    for copy in copies:
        copy.wait()


def place(plane, value, before=()):
    cells, sols = value.shape
    return pl.pallas_call(
        place_kernel,
        in_specs=[SMEM, VMEM] + [ANY] * len(before),
        out_specs=ANY,
        out_shape=jax.ShapeDtypeStruct((2 * cells, sols), F32),
        scratch_shapes=[pltpu.SemaphoreType.DMA((PARTS,))],
        input_output_aliases={2: 0} if before else {},
        compiler_params=PARAMS,
        cost_estimate=pl.CostEstimate(flops=0, bytes_accessed=8 * cells * sols, transcendentals=0),
    )(plane, value, *before)


def swap(value, axis):
    return lax.ppermute(value, axis, [(0, 1), (1, 0)])


def relay_of(own, ranks):
    half = ranks // 2
    pairs = [(ranks + half - 1, 2 * ranks - 1), (half, 0)]
    return lax.ppermute(own, ("core",) + CELLS, pairs)


def beyond_of(sent, ranks):
    half = ranks // 2
    up = [(ranks + i, i + 1) for i in range(ranks - 1) if i != half - 1]
    down = [(i + 1, ranks + i) for i in range(ranks - 1) if i != half - 1]
    cut = [(2 * ranks - 1, half), (0, ranks + half - 1)]
    return lax.ppermute(sent, ("core",) + CELLS, up + down + cut)


def ring_of(value, shift):
    yh, core, yl, x, z = (lax.axis_size(axis) for axis in ALL)
    pairs = []
    for h in range(yh):
        for l in range(yl):
            for i in range(x):
                for j in range(z):
                    at = lambda c, i, j: (((h * core + c) * yl + l) * x + i % x) * z + j % z
                    pairs.append((at(0, i, j), at(0, i, j + shift)))
                    pairs.append((at(1, i, j), at(1, i + shift, j)))
    return lax.ppermute(value, ALL, pairs)


def spread(value):
    yh, core, yl, x, z = (lax.axis_size(axis) for axis in ALL)
    at = lambda h, c, l, i, j: (((h * core + c) * yl + l) * x + i) * z + j
    groups = []
    for h in range(yh):
        groups += [[at(h, 0, l, i, j) for l in range(yl) for i in range(x)] for j in range(z)]
        groups += [[at(h, 1, l, i, j) for l in range(yl) for j in range(z)] for i in range(x)]
    return lax.all_to_all(value, ALL, 0, 0, axis_index_groups=groups, tiled=True)


def local(sensitivity, observed, models, neighbour_map, edge_mask):
    core = lax.axis_index("core").astype(jnp.int32)
    x, z = (lax.axis_index(axis).astype(jnp.int32) for axis in ("x", "z"))
    ring = jnp.where(core == 0, z, x)
    sub = lax.axis_index("yl").astype(jnp.int32) * lax.axis_size("x") + jnp.where(core == 0, x, z)
    rings = lax.axis_size("x")
    ranks = lax.axis_size(CELLS)
    subs = ranks // rings
    rank = (ring * subs + sub).reshape(1)
    block = [((ring + s) % rings).reshape(1) for s in range(rings)]
    sides = jnp.concatenate([block[1], block[3]])
    mine, theirs = core.reshape(1), (1 - core).reshape(1)
    both = jnp.concatenate([mine, theirs])
    cells = neighbour_map.shape[1]
    rows = observed.shape[0] // rings
    low_core = core == 0
    cells_rank = lax.axis_index(CELLS).astype(jnp.int32)
    carrier = cells_rank == core * (ranks - 1)
    rank, mine, theirs, both, block, sides, low_core, carrier = lax.optimization_barrier(
        (rank, mine, theirs, both, block, sides, low_core, carrier)
    )
    for step in range(ITERS):
        if step == 0:
            p2, h2, l2, *halves = first_forward(block[2], sensitivity, models, rows)
            s2 = [h2, l2]
            r2 = ring_of(p2, 2)
            p1, *s1 = rest_forward(block[1], sensitivity, halves, rows)
            r1 = ring_of(p1, 1)
            p1, halves = lax.optimization_barrier((p1, halves))
            p3, *s3 = rest_forward(block[3], sensitivity, halves, rows)
            r3 = ring_of(p3, 3)
            p3, halves = lax.optimization_barrier((p3, halves))
            p0, *s0 = rest_forward(block[0], sensitivity, halves, rows)
            p0, start, numbers, mask = lax.optimization_barrier((p0, models, neighbour_map, edge_mask))
            own = jnp.where(low_core, start[:cells], start[cells:])
            twin = jnp.where(low_core, start[cells:], start[:cells])
            mask = jnp.where(low_core, mask[:cells], mask[cells:])
            weight = 0.05 * (1.0 - 0.75 * mask.astype(F32))
            table = jnp.concatenate(
                [numbers.astype(F32), weight[None], jnp.zeros((3, cells), F32)], axis=0
            )
        else:
            p2, p1, p3 = forward(mine, [own], s2 + s1 + s3)
            twin = swap(own, "core")
            (p2,) = forward(theirs, [twin], s2, [p2])
            r2 = ring_of(p2, 2)
            p1, p3 = forward(theirs, [twin], s1 + s3, [p1, p3])
            r1, r3 = ring_of(p1, 1), ring_of(p3, 3)
            (p0,) = forward(both, [own, twin], s0)
        p0, r1, r3 = lax.optimization_barrier((p0 + r2, r1, r3))
        p0, r3 = lax.optimization_barrier((p0 + r1, r3))
        p0, own, twin, table = lax.optimization_barrier((p0 + r3, own, twin, table))
        pieces = spread(p0)
        copies = weigh(rank, pieces.reshape(subs, rows // subs, -1), observed)
        w0 = spread(copies.reshape(rows, -1))
        w0, sent = lax.optimization_barrier((w0, own))
        relay = relay_of(sent, ranks)
        w2, w3, w1 = ring_of(w0, 2), ring_of(w0, 1), ring_of(w0, 3)
        near = gather_up([w0], s0)
        near = gather_up([w3], s3, [near])
        near, relay = lax.optimization_barrier((near, relay))
        sent = jnp.where(carrier, relay, own)
        away, home = close(theirs, mine, [w1, w2], s1 + s2, near, cells)
        half = home + swap(away, "core")
        half, own, twin, sent = lax.optimization_barrier((half, own, twin, sent))
        beyond = beyond_of(sent, ranks)
        gradient = half + swap(half, "yh")
        inner = smooth_of(table, own, twin)
        own = edge_of(table, own, beyond, inner, own - 1.0 * gradient)
    twin = swap(own, "core")
    return place(theirs, twin, [place(mine, own)])


def solution(mesh):
    fine = Mesh(mesh.devices.reshape(2, 2, 2, 4, 4), ALL)
    return jax.shard_map(
        local,
        mesh=fine,
        in_specs=(P(DATA, CELLS), P(DATA, None), P(CELLS, None), P(), P(CELLS)),
        out_specs=P(CELLS, None),
        check_vma=False,
    )
```
